32 devices in a mesh: groups: 2 (over x), row: 8 (over z, y), col: 2 (over core).
Axes of the slice: x: 2, y: 2, z: 4, core: 2. Of those that a mesh axis runs over, the one named last changes fastest.
Arguments:
- canvas: bfloat16 [512, 64, 512], P(('groups', 'row'), 'col'), parts along dimension 0, may hold values from -50 to 50
- keep_mask: int32 [512, 64], P(('groups', 'row'), 'col'), parts along dimension 0, may hold values from 0 to 1, as said below
- w_qkv: bfloat16 [512, 1536], replicated, may hold values from -0.25 to 0.25
- w_spread: bfloat16 [5, 5, 1536], replicated, may hold values from -1.25 to 1.25
- w_group: bfloat16 [48, 32, 32], replicated, may hold values from -1 to 1
- w_proj: bfloat16 [1024, 512], replicated, may hold values from -0.1875 to 0.1875
- gain_attn: float32 [512], replicated, may hold values from 0.1 to 1.9
- w_expand: bfloat16 [512, 4096], replicated, may hold values from -0.25 to 0.25
- w_spatial: bfloat16 [3, 3, 4096], replicated, may hold values from -2 to 2
- w_reduce: bfloat16 [2048, 512], replicated, may hold values from -0.125 to 0.125
- gain_ff: float32 [512], replicated, may hold values from 0.1 to 1.9
Outputs:
- decoded: bfloat16 [512, 64, 512], P(('groups', 'row'), 'col'), parts along dimension 0
The draws below stay inside these ranges and needn't reach their ends.
There are 2 independent parts, one for each index of `groups`. The reference program is written for one: setup_inputs(seed, part) draws one part's arguments, and reference() takes and returns one part's arrays. A program takes and returns all parts, laid end to end along the dimension named above; an argument that names none is the same for every part. Nothing has to cross between parts.
Inputs may be any that keep to these rules, and one draw needn't show every extreme that they name: `keep_mask`: one bit per cell.
All inputs are finite; a program needn't handle non-finite values.
Results may differ from the reference program's by a relative error of at most 0.008.
Values may be sent and summed in bfloat16 or wider, within the bound.
No kernel may reach another device: no remote copies, remote signals or barrier semaphores. Data moves between devices by JAX's collectives and lax.ppermute only.
A program may use at most 128 MiB of HBM per device.

```python
import math
import jax
import jax.numpy as jnp
from jax import lax

C = 512
HEADS = 16
HD = 32
FF = 2048
H = 256
W = 64


def draw_canvas(key, part):
    key_base, key_rowscale, key_chan = jax.random.split(key, 3)
    row_scale = jnp.exp(jax.random.uniform(key_rowscale, (H, 1, 1), jnp.float32, math.log(0.3), math.log(3.0)))
    chan_scale = jnp.exp(jax.random.uniform(key_chan, (1, 1, C), jnp.float32, math.log(0.5), math.log(2.0)))
    base = jnp.clip(jax.random.normal(key_base, (H, W, C), jnp.float32), -4.0, 4.0)
    values = base * row_scale * chan_scale
    return values.astype(jnp.bfloat16)


def draw_keep_mask(key, part):
    row_index = jnp.arange(H, dtype=jnp.int32)
    threshold = 25 + 70 * row_index // max(H - 1, 1)
    ticket = jax.random.randint(key, (H, W), 0, 100, dtype=jnp.int32)
    return (ticket < threshold[:, None]).astype(jnp.int32)


def bell_draw(stream_key, dims, deviation, most, kind=jnp.bfloat16):
    return jnp.clip(deviation * jax.random.normal(stream_key, dims, jnp.float32), -most, most).astype(kind)


def setup_inputs(seed: int = 0, part: int = 0) -> dict:
    keys = jax.random.split(jax.random.key(seed), 12)
    part_keys = jax.random.split(jax.random.fold_in(keys[11], part), 12)
    return {
        "canvas": draw_canvas(jax.random.fold_in(jax.random.fold_in(keys[11], part), 71), part),
        "keep_mask": draw_keep_mask(jax.random.fold_in(jax.random.fold_in(keys[11], part), 71), part),
        "w_qkv": bell_draw(keys[2], (C, 3 * C), C ** -0.5, 0.25),
        "w_spread": bell_draw(keys[3], (5, 5, 3 * C), 25 ** -0.5, 1.25),
        "w_group": bell_draw(keys[4], (3 * HEADS, HD, HD), HD ** -0.5, 1.0),
        "w_proj": bell_draw(keys[5], (2 * C, C), (2 * C) ** -0.5, 0.1875),
        "gain_attn": jnp.clip(1.0 + 0.18 * jax.random.normal(keys[6], (C,), jnp.float32), 0.1, 1.9),
        "w_expand": bell_draw(keys[7], (C, 2 * FF), C ** -0.5, 0.25),
        "w_spatial": bell_draw(keys[8], (3, 3, 2 * FF), 9 ** -0.5, 2.0),
        "w_reduce": bell_draw(keys[9], (FF, C), FF ** -0.5, 0.125),
        "gain_ff": jnp.clip(1.0 + 0.18 * jax.random.normal(keys[10], (C,), jnp.float32), 0.1, 1.9),
    }


def depthwise(padded, weight, tile_rows, tile_cols, kernel_span):
    summed = jnp.zeros((tile_rows, tile_cols, padded.shape[2]), jnp.float32)
    for shift_row in range(kernel_span):
        for shift_col in range(kernel_span):
            window = padded[shift_row:shift_row + tile_rows, shift_col:shift_col + tile_cols]
            summed = summed + window.astype(jnp.float32) * weight[shift_row, shift_col].astype(jnp.float32)
    return summed

def rms_scale(branch, gain):
    return branch * lax.rsqrt(lax.optimization_barrier(jnp.mean(branch * branch, axis=-1, keepdims=True)) + 1e-05) * gain

def reference(canvas, keep_mask, w_qkv, w_spread, w_group, w_proj, gain_attn, w_expand, w_spatial, w_reduce, gain_ff):
    canvas_rows, canvas_cols = (canvas.shape[0], canvas.shape[1])
    cell_count = canvas_rows * canvas_cols
    flat = canvas.reshape(cell_count, C)
    projected = jnp.dot(flat, w_qkv, preferred_element_type=jnp.float32).astype(jnp.bfloat16)
    padded = jnp.pad(projected.reshape(canvas_rows, canvas_cols, 3 * C), ((2, 2), (2, 2), (0, 0)))
    spread = depthwise(padded, w_spread, canvas_rows, canvas_cols, 5).astype(jnp.bfloat16)
    grouped = spread.reshape(cell_count, 3 * HEADS, HD).astype(jnp.float32)
    aggregated = jnp.einsum('cgi,gio->cgo', grouped, w_group.astype(jnp.float32)).astype(jnp.bfloat16)
    both = jnp.concatenate([projected.reshape(cell_count, 3, HEADS, HD), aggregated.reshape(cell_count, 3, HEADS, HD)], axis=2)
    queries, keys_raw, value_rows = (both[:, 0], both[:, 1], both[:, 2])
    keep = keep_mask.reshape(cell_count).astype(jnp.bfloat16)
    key_feats = jax.nn.relu(keys_raw) * keep[:, None, None]
    kv_stats = jnp.einsum('chi,chj->hij', key_feats.astype(jnp.float32), value_rows.astype(jnp.float32))
    key_sums = lax.optimization_barrier(jnp.sum(key_feats.astype(jnp.float32), axis=0))
    query_feats = jax.nn.relu(queries).astype(jnp.float32)
    numerator = jnp.einsum('chi,hij->chj', query_feats, kv_stats, precision=lax.Precision.HIGHEST)
    denominator = jnp.einsum('chi,hi->ch', query_feats, key_sums, precision=lax.Precision.HIGHEST) + 1.0
    attended = (numerator / denominator[:, :, None]).astype(jnp.bfloat16).reshape(cell_count, 2 * C)
    branch = jnp.dot(attended, w_proj, preferred_element_type=jnp.float32)
    midway = (flat.astype(jnp.float32) + rms_scale(branch, gain_attn)).astype(jnp.bfloat16)
    block_width = math.gcd(FF, 512)
    block_count = FF // block_width

    def feed_block(carry, index):
        start = index * block_width
        w_sel = jnp.concatenate([lax.dynamic_slice_in_dim(w_expand, start, block_width, 1), lax.dynamic_slice_in_dim(w_expand, start + FF, block_width, 1)], axis=1)
        s_sel = jnp.concatenate([lax.dynamic_slice_in_dim(w_spatial, start, block_width, 2), lax.dynamic_slice_in_dim(w_spatial, start + FF, block_width, 2)], axis=2)
        expanded = jax.nn.silu(jnp.dot(midway, w_sel, preferred_element_type=jnp.float32)).astype(jnp.bfloat16)
        padded_hidden = jnp.pad(expanded.reshape(canvas_rows, canvas_cols, 2 * block_width), ((1, 1), (1, 1), (0, 0)))
        conv = depthwise(padded_hidden, s_sel, canvas_rows, canvas_cols, 3)
        gated = (conv[..., :block_width] * jax.nn.silu(conv[..., block_width:])).astype(jnp.bfloat16)
        rows_sel = lax.dynamic_slice_in_dim(w_reduce, start, block_width, 0)
        return (carry + jnp.dot(gated.reshape(cell_count, block_width), rows_sel, preferred_element_type=jnp.float32), None)
    reduced, _ = lax.scan(feed_block, jnp.zeros((cell_count, C), jnp.float32), jnp.arange(block_count, dtype=jnp.int32))
    decoded = (midway.astype(jnp.float32) + rms_scale(reduced, gain_ff)).astype(jnp.bfloat16)
    return decoded.reshape(canvas_rows, canvas_cols, C)
```

```python
import functools

import jax
import jax.numpy as jnp
from jax import lax
from jax.experimental import pallas as pl
from jax.experimental.pallas import tpu as pltpu
from jax.sharding import PartitionSpec as P

LANES = 128
BLOCK = 256
PAD = 8
VMEM_BYTES = 60 * 1024 * 1024
BF16 = jnp.bfloat16
F32 = jnp.float32


def depthwise_rows(load, taps, span, out_rows, emit):
    sums = {}
    for row_in in range(out_rows + span - 1):
        views = [load(row_in, b) for b in range(span)]
        for a in range(span):
            row_out = row_in - a
            if not 0 <= row_out < out_rows:
                continue
            part = views[0] * taps[a * span]
            for b in range(1, span):
                part = part + views[b] * taps[a * span + b]
            sums[row_out] = part if a == 0 else sums[row_out] + part
            if a == span - 1:
                emit(row_out, sums.pop(row_out))


def tap_list(weight_ref, lanes, rows):
    count = weight_ref.shape[0]
    return [
        jnp.broadcast_to(weight_ref[t : t + 1, lanes], (rows, LANES)).astype(BF16)
        for t in range(count)
    ]


def head_mask(size, head):
    return (
        lax.broadcasted_iota(jnp.int32, (size, size), 0) // head
        == lax.broadcasted_iota(jnp.int32, (size, size), 1) // head
    )


def spread_blocks(rows, head):
    size = rows.shape[0]
    pick = (
        lax.broadcasted_iota(jnp.int32, (head, size), 1) % head
        == lax.broadcasted_iota(jnp.int32, (head, size), 0)
    ).astype(BF16)
    wide = jnp.dot(rows, pick, preferred_element_type=F32)
    return jnp.where(head_mask(size, head), wide, 0.0).astype(BF16)


def project(dims, main_ref, rows_ref, cols_ref, w_ref, place, on_main):
    tile_rows, tile_cols, reach, tall = dims
    stride = tile_cols + PAD
    w = w_ref[...]
    group = 4
    for first in range(0, tile_rows, group):
        p = jnp.dot(
            main_ref[first * tile_cols : (first + group) * tile_cols],
            w,
            preferred_element_type=F32,
        )
        for k in range(group):
            place(first + k, p[k * tile_cols : (k + 1) * tile_cols])
        on_main(first * tile_cols, p)
    p = jnp.dot(rows_ref[...], w, preferred_element_type=F32)
    for k in range(reach):
        place(k - reach, p[k * tile_cols : (k + 1) * tile_cols])
        low = (reach + k) * tile_cols
        place(tile_rows + k, p[low : low + tile_cols])
    p = jnp.dot(cols_ref[...], w, preferred_element_type=F32)
    for side in range(2):
        for k in range(reach):
            col = k - reach if side == 0 else tile_cols + k
            low = (side * reach + k) * tall
            place((PAD + col, tall, stride), p[low : low + tall])


def placer(buf, reach, stride):
    def place(where, values):
        for ch in range(values.shape[1] // LANES):
            part = values[:, ch * LANES : (ch + 1) * LANES]
            if isinstance(where, tuple):
                start, count, step = where
                buf[ch, pl.ds(start, count, stride=step), :] = part
            else:
                start = PAD + (where + reach) * stride
                buf[ch, pl.ds(start, part.shape[0]), :] = part

    return place


def key_value_kernel(
    dims,
    head,
    main_ref,
    rows_ref,
    cols_ref,
    keep_ref,
    wk_ref,
    wv_ref,
    sk_ref,
    sv_ref,
    gk_ref,
    gv_ref,
    stats_ref,
    buf_k,
    buf_v,
    mat_k,
    mat_v,
    agg_k,
    agg_v,
):
    tile_rows, tile_cols, reach, tall = dims
    stride = tile_cols + PAD

    def keep_keys(start, p):
        rows = p.shape[0]
        keep = keep_ref[start : start + rows]
        for ch in range(BLOCK // LANES):
            lanes = slice(ch * LANES, (ch + 1) * LANES)
            mat_k[start : start + rows, lanes] = (
                jnp.maximum(p[:, lanes].astype(BF16), 0) * keep
            )

    def keep_values(start, p):
        mat_v[start : start + p.shape[0]] = p.astype(BF16)

    project(dims, main_ref, rows_ref, cols_ref, wk_ref, placer(buf_k, reach, stride), keep_keys)
    project(dims, main_ref, rows_ref, cols_ref, wv_ref, placer(buf_v, reach, stride), keep_values)

    def summarise(scale, keys, values):
        kv = lax.dot_general(
            keys[...], values[...], (((0,), (0,)), ((), ())), preferred_element_type=F32
        )
        lane_head = lax.broadcasted_iota(jnp.int32, (head, BLOCK), 1) // head
        packed = jnp.zeros((head, BLOCK), F32)
        for h in range(BLOCK // head):
            packed = packed + jnp.where(lane_head == h, kv[h * head : (h + 1) * head], 0.0)
        stats_ref[scale, 0:head, :] = packed
        total = jnp.sum(keys[...].astype(F32), axis=0, keepdims=True)
        stats_ref[scale, head : head + 8, :] = jnp.broadcast_to(total, (8, BLOCK))

    summarise(0, mat_k, mat_v)

    for buf, sp_ref, out in ((buf_k, sk_ref, mat_k), (buf_v, sv_ref, mat_v)):
        for ch in range(BLOCK // LANES):
            lanes = slice(ch * LANES, (ch + 1) * LANES)
            taps = tap_list(sp_ref, lanes, tile_cols)

            def load(row_in, b, buf=buf, ch=ch):
                start = PAD + (row_in + 1) * stride + b - 2
                return buf[ch, pl.ds(start, tile_cols), :].astype(BF16)

            def emit(row, value, out=out, lanes=lanes):
                out[row * tile_cols : (row + 1) * tile_cols, lanes] = value

            depthwise_rows(load, taps, 5, tile_rows, emit)

    for spread, g_ref, out, is_key in (
        (mat_k, gk_ref, agg_k, True),
        (mat_v, gv_ref, agg_v, False),
    ):
        blocks = spread_blocks(g_ref[...], head)
        cells = spread.shape[0]
        step = 256
        for start in range(0, cells, step):
            agg = jnp.dot(
                spread[start : start + step], blocks, preferred_element_type=F32
            ).astype(BF16)
            if is_key:
                keep = keep_ref[start : start + step]
                agg = jnp.maximum(agg, 0)
                for ch in range(BLOCK // LANES):
                    lanes = slice(ch * LANES, (ch + 1) * LANES)
                    out[start : start + step, lanes] = agg[:, lanes] * keep
            else:
                out[start : start + step] = agg
    summarise(1, agg_k, agg_v)


def query_kernel(
    dims, head, main_ref, rows_ref, cols_ref, wq_ref, sq_ref, gq_ref, q_ref, buf, spread
):
    tile_rows, tile_cols, reach, tall = dims
    stride = tile_cols + PAD
    cells = tile_rows * tile_cols
    project(
        dims,
        main_ref,
        rows_ref,
        cols_ref,
        wq_ref,
        placer(buf, reach, stride),
        lambda start, p: None,
    )

    def slot(row):
        if row < 0:
            return cells
        if row >= tile_rows:
            return cells + tile_cols
        return row * tile_cols

    side0 = cells + 2 * tile_cols
    for ch in range(BLOCK // LANES):
        lanes = slice(ch * LANES, (ch + 1) * LANES)
        for row in range(-1, tile_rows + 1):
            start = PAD + (row + reach) * stride
            value = buf[ch, pl.ds(start, tile_cols), :].astype(BF16)
            q_ref[0, 0, slot(row) : slot(row) + tile_cols, lanes] = jnp.maximum(value, 0)
        for side, col in enumerate((-1, tile_cols)):
            value = buf[ch, pl.ds(PAD + 2 * stride + col, tall, stride=stride), :].astype(BF16)
            low = side0 + side * tall
            q_ref[0, 0, low : low + tall, lanes] = jnp.maximum(value, 0)

        taps = tap_list(sq_ref, lanes, tile_cols)

        def load(row_in, b, ch=ch):
            start = PAD + row_in * stride + b - 2
            return buf[ch, pl.ds(start, tile_cols), :].astype(BF16)

        def emit(row, value, lanes=lanes):
            low = slot(row - 1)
            spread[low : low + tile_cols, lanes] = value

        depthwise_rows(load, taps, 5, tile_rows + 2, emit)
        taps = tap_list(sq_ref, lanes, tall)
        for side, col in enumerate((-1, tile_cols)):
            total = None
            for a in range(5):
                part = None
                for b in range(5):
                    start = PAD + a * stride + col + b - 2
                    view = buf[ch, pl.ds(start, tall, stride=stride), :].astype(BF16)
                    term = view * taps[a * 5 + b]
                    part = term if part is None else part + term
                total = part if total is None else total + part
            low = side0 + side * tall
            spread[low : low + tall, lanes] = total

    blocks = spread_blocks(gq_ref[...], head)
    count = spread.shape[0]
    for start in range(0, count, 256):
        stop = min(count, start + 256)
        agg = jnp.dot(spread[start:stop], blocks, preferred_element_type=F32)
        q_ref[1, 0, start:stop] = jnp.maximum(agg.astype(BF16), 0)


def rms_add(residual, branch, gain):
    scale = lax.rsqrt(jnp.mean(branch * branch, axis=-1, keepdims=True) + 1e-05)
    return residual.astype(F32) + branch * scale * gain


def feed_kernel(
    dims,
    head,
    flags_ref,
    main_ref,
    edge_ref,
    q_ref,
    stats_ref,
    wp_ref,
    gain_a_ref,
    wev_ref,
    weg_ref,
    spv_ref,
    spg_ref,
    wr_ref,
    gain_f_ref,
    out_ref,
    mid,
    att,
    buf_v,
    buf_g,
    gated,
):
    tile_rows, tile_cols, reach, tall = dims
    stride = tile_cols + PAD
    cells = tile_rows * tile_cols
    step_index = pl.program_id(0)
    scales, heads_blocks = q_ref.shape[0], q_ref.shape[1]

    @pl.when(step_index == 0)
    def _():
        same = head_mask(BLOCK, head)
        eye = lax.broadcasted_iota(jnp.int32, (BLOCK, BLOCK), 0) == lax.broadcasted_iota(
            jnp.int32, (BLOCK, BLOCK), 1
        )
        count = mid.shape[0]
        bounds = [(s, s + 256) for s in range(0, cells, 256)] + [(cells, count)]
        for scale in range(scales):
            for blk in range(heads_blocks):
                lanes = slice(blk * BLOCK, (blk + 1) * BLOCK)
                packed = stats_ref[scale, 0:head, lanes]
                kv = jnp.where(same, jnp.concatenate([packed] * (BLOCK // head), axis=0), 0.0)
                sums = stats_ref[scale, head : head + 1, lanes]
                diag = jnp.where(eye, jnp.broadcast_to(sums, (BLOCK, BLOCK)), 0.0)
                ks = jnp.dot(
                    diag.astype(BF16), same.astype(BF16), preferred_element_type=F32
                ).astype(BF16)
                kv = kv.astype(BF16)
                low = (scale * heads_blocks + blk) * BLOCK
                for start, stop in bounds:
                    q = q_ref[scale, blk, start:stop]
                    num = jnp.dot(q, kv, preferred_element_type=F32)
                    den = jnp.dot(q, ks, preferred_element_type=F32)
                    att[start:stop, low : low + BLOCK] = (num / (den + 1.0)).astype(BF16)
        gain = gain_a_ref[...]
        for start, stop in bounds:
            branch = jnp.dot(att[start:stop], wp_ref[...], preferred_element_type=F32)
            if start < cells:
                mid[start:stop] = rms_add(main_ref[start:stop], branch, gain).astype(BF16)
            else:
                value = rms_add(edge_ref[...], branch, gain)
                index = lax.broadcasted_iota(jnp.int32, (stop - start, 1), 0)
                side = index - 2 * tile_cols
                place = lax.rem(side + tall, tall)
                in_rows = index < 2 * tile_cols
                is_top = (index < tile_cols) | (~in_rows & (place == 0))
                is_bottom = (in_rows & (index >= tile_cols)) | (
                    ~in_rows & (place == tile_rows + 1)
                )
                is_left = ~in_rows & (side < tall)
                is_right = ~in_rows & (side >= tall)
                dead = (
                    (is_top & (flags_ref[0] == 0))
                    | (is_bottom & (flags_ref[1] == 0))
                    | (is_left & (flags_ref[2] == 0))
                    | (is_right & (flags_ref[3] == 0))
                )
                mid[start:stop] = jnp.where(dead, 0.0, value).astype(BF16)

    def silu(x):
        half = 0.5 * x
        return half * jnp.tanh(half) + half

    for w_ref, buf in ((wev_ref, buf_v), (weg_ref, buf_g)):
        w = w_ref[...]
        place = placer(buf, 1, stride)
        group = 4
        for first in range(0, tile_rows, group):
            p = silu(
                jnp.dot(
                    mid[first * tile_cols : (first + group) * tile_cols],
                    w,
                    preferred_element_type=F32,
                )
            )
            for k in range(group):
                place(first + k, p[k * tile_cols : (k + 1) * tile_cols])
        p = silu(jnp.dot(mid[cells:], w, preferred_element_type=F32))
        place(-1, p[:tile_cols])
        place(tile_rows, p[tile_cols : 2 * tile_cols])
        for side, col in enumerate((-1, tile_cols)):
            low = 2 * tile_cols + side * tall
            place((PAD + col, tall, stride), p[low : low + tall])

    base = step_index * BLOCK
    for ch in range(BLOCK // LANES):
        lanes = slice(ch * LANES, (ch + 1) * LANES)
        halves = []
        for buf, sp_ref in ((buf_v, spv_ref), (buf_g, spg_ref)):
            rows = []

            def load(row_in, b, buf=buf):
                start = PAD + row_in * stride + b - 1
                return buf[ch, pl.ds(start, tile_cols), :].astype(BF16)

            halves.append((load, tap_list(sp_ref, lanes, tile_cols)))

        pending = {}

        def finish(row, gate):
            value = pending.pop(row).astype(F32)
            result = value * silu(gate.astype(F32))
            col0 = pl.multiple_of(base + ch * LANES, LANES)
            gated[row * tile_cols : (row + 1) * tile_cols, pl.ds(col0, LANES)] = result.astype(
                BF16
            )

        depthwise_pair(halves, 3, tile_rows, pending, finish)

    @pl.when(step_index == pl.num_programs(0) - 1)
    def _():
        gain = gain_f_ref[...]
        for start in range(0, cells, 256):
            reduced = jnp.dot(
                gated[start : start + 256], wr_ref[...], preferred_element_type=F32
            )
            out_ref[start : start + 256] = rms_add(
                mid[start : start + 256], reduced, gain
            ).astype(BF16)


def depthwise_pair(halves, span, out_rows, pending, finish):
    sums = ({}, {})
    for row_in in range(out_rows + span - 1):
        for side, (load, taps) in enumerate(halves):
            views = [load(row_in, b) for b in range(span)]
            for a in range(span):
                row_out = row_in - a
                if not 0 <= row_out < out_rows:
                    continue
                part = views[0] * taps[a * span]
                for b in range(1, span):
                    part = part + views[b] * taps[a * span + b]
                sums[side][row_out] = part if a == 0 else sums[side][row_out] + part
                if a == span - 1:
                    if side == 0:
                        pending[row_out] = sums[0].pop(row_out)
                    else:
                        finish(row_out, sums[1].pop(row_out))


def neighbours(axis):
    count = lax.axis_size(axis)
    forward = [(i, i + 1) for i in range(count - 1)]
    return forward, [(b, a) for a, b in forward]


def total_over(x, axes):
    for axis in axes:
        count = lax.axis_size(axis)
        if count & (count - 1):
            x = lax.psum(x, axis)
            continue
        step = 1
        while step < count:
            x = x + lax.ppermute(x, axis, [(i, i ^ step) for i in range(count)])
            step *= 2
    return x


def body(
    canvas,
    keep_mask,
    w_qkv,
    w_spread,
    w_group,
    w_proj,
    gain_attn,
    w_expand,
    w_spatial,
    w_reduce,
    gain_ff,
):
    tile_rows, tile_cols, channels = canvas.shape
    cells = tile_rows * tile_cols
    head = w_group.shape[1]
    hidden = w_reduce.shape[0]
    blocks = channels // BLOCK
    reach = 3
    tall = tile_rows + PAD
    stride = tile_cols + PAD
    dims = (tile_rows, tile_cols, reach, tall)
    flat_rows = -(-(PAD + (tall + 4) * stride) // 8) * 8
    flat_rows_ff = PAD + tall * stride

    down, up = neighbours("row")
    above = lax.ppermute(canvas[tile_rows - reach :], "row", down)
    below = lax.ppermute(canvas[:reach], "row", up)

    def strip(low):
        return jnp.concatenate(
            [
                above[:, low : low + reach],
                canvas[:, low : low + reach],
                below[:, low : low + reach],
                jnp.zeros((tall - tile_rows - 2 * reach, reach, channels), canvas.dtype),
            ],
            axis=0,
        ).transpose(1, 0, 2)

    col_index = lax.axis_index("col")
    col_count = lax.axis_size("col")
    row_index = lax.axis_index("row")
    row_count = lax.axis_size("row")
    first, last = strip(0), strip(tile_cols - reach)
    if col_count == 2:
        got = lax.ppermute(jnp.where(col_index == 0, last, first), "col", [(0, 1), (1, 0)])
        left = jnp.where(col_index == 1, got, 0)
        right = jnp.where(col_index == 0, got, 0)
    else:
        right_way, left_way = neighbours("col")
        left = lax.ppermute(last, "col", right_way)
        right = lax.ppermute(first, "col", left_way)

    main = canvas.reshape(cells, channels)
    rows_in = jnp.concatenate([above, below], axis=0).reshape(2 * reach * tile_cols, channels)
    cols_in = jnp.concatenate([left, right], axis=0).reshape(2 * reach * tall, channels)
    filler = jnp.zeros((reach - 1, channels), canvas.dtype)
    edge = jnp.concatenate(
        [
            above[reach - 1],
            below[0],
            left[reach - 1, reach - 1 :],
            filler,
            right[0, reach - 1 :],
            filler,
        ],
        axis=0,
    )
    keep = jnp.broadcast_to(keep_mask.reshape(cells, 1).astype(BF16), (cells, LANES))
    flags = jnp.stack(
        [
            (row_index > 0),
            (row_index < row_count - 1),
            (col_index > 0),
            (col_index < col_count - 1),
        ]
    ).astype(jnp.int32)
    spread_w = w_spread.reshape(25, 3 * channels).astype(F32)
    group_w = w_group.reshape(3 * channels, head)
    spatial_w = w_spatial.reshape(9, 2 * hidden).astype(F32)

    def whole(shape):
        return pl.BlockSpec(shape, lambda *_: (0,) * len(shape))

    params = pltpu.CompilerParams(
        dimension_semantics=("arbitrary",), vmem_limit_bytes=VMEM_BYTES
    )

    stats = pl.pallas_call(
        functools.partial(key_value_kernel, dims, head),
        grid=(blocks,),
        in_specs=[
            whole(main.shape),
            whole(rows_in.shape),
            whole(cols_in.shape),
            whole(keep.shape),
            pl.BlockSpec((channels, BLOCK), lambda j: (0, blocks + j)),
            pl.BlockSpec((channels, BLOCK), lambda j: (0, 2 * blocks + j)),
            pl.BlockSpec((25, BLOCK), lambda j: (0, blocks + j)),
            pl.BlockSpec((25, BLOCK), lambda j: (0, 2 * blocks + j)),
            pl.BlockSpec((BLOCK, head), lambda j: (blocks + j, 0)),
            pl.BlockSpec((BLOCK, head), lambda j: (2 * blocks + j, 0)),
        ],
        out_specs=pl.BlockSpec((2, head + 8, BLOCK), lambda j: (0, 0, j)),
        out_shape=jax.ShapeDtypeStruct((2, head + 8, channels), F32),
        scratch_shapes=[
            pltpu.VMEM((BLOCK // LANES, flat_rows, LANES), F32),
            pltpu.VMEM((BLOCK // LANES, flat_rows, LANES), F32),
            pltpu.VMEM((cells, BLOCK), BF16),
            pltpu.VMEM((cells, BLOCK), BF16),
            pltpu.VMEM((cells, BLOCK), BF16),
            pltpu.VMEM((cells, BLOCK), BF16),
        ],
        compiler_params=params,
        cost_estimate=pl.CostEstimate(
            flops=2 * cells * channels * 2 * channels,
            bytes_accessed=4 * cells * channels,
            transcendentals=0,
        ),
        name="key_value",
    )(main, rows_in, cols_in, keep, w_qkv, w_qkv, spread_w, spread_w, group_w, group_w)
    stats = total_over(stats, ("col", "row"))

    count = cells + 2 * tile_cols + 2 * tall
    queries = pl.pallas_call(
        functools.partial(query_kernel, dims, head),
        grid=(blocks,),
        in_specs=[
            whole(main.shape),
            whole(rows_in.shape),
            whole(cols_in.shape),
            pl.BlockSpec((channels, BLOCK), lambda j: (0, j)),
            pl.BlockSpec((25, BLOCK), lambda j: (0, j)),
            pl.BlockSpec((BLOCK, head), lambda j: (j, 0)),
        ],
        out_specs=pl.BlockSpec((2, 1, count, BLOCK), lambda j: (0, j, 0, 0)),
        out_shape=jax.ShapeDtypeStruct((2, blocks, count, BLOCK), BF16),
        scratch_shapes=[
            pltpu.VMEM((BLOCK // LANES, flat_rows, LANES), F32),
            pltpu.VMEM((count, BLOCK), BF16),
        ],
        compiler_params=params,
        cost_estimate=pl.CostEstimate(
            flops=2 * cells * channels * channels,
            bytes_accessed=6 * cells * channels,
            transcendentals=0,
        ),
        name="query",
    )(main, rows_in, cols_in, w_qkv, spread_w, group_w)

    steps = hidden // BLOCK
    decoded = pl.pallas_call(
        functools.partial(feed_kernel, dims, head),
        grid=(steps,),
        in_specs=[
            pl.BlockSpec(memory_space=pltpu.SMEM),
            whole(main.shape),
            whole(edge.shape),
            whole(queries.shape),
            whole(stats.shape),
            whole(w_proj.shape),
            whole((1, channels)),
            pl.BlockSpec((channels, BLOCK), lambda j: (0, j)),
            pl.BlockSpec((channels, BLOCK), lambda j: (0, steps + j)),
            pl.BlockSpec((9, BLOCK), lambda j: (0, j)),
            pl.BlockSpec((9, BLOCK), lambda j: (0, steps + j)),
            whole(w_reduce.shape),
            whole((1, channels)),
        ],
        out_specs=whole(main.shape),
        out_shape=jax.ShapeDtypeStruct(main.shape, BF16),
        scratch_shapes=[
            pltpu.VMEM((count, channels), BF16),
            pltpu.VMEM((count, 2 * channels), BF16),
            pltpu.VMEM((BLOCK // LANES, flat_rows_ff, LANES), F32),
            pltpu.VMEM((BLOCK // LANES, flat_rows_ff, LANES), F32),
            pltpu.VMEM((cells, hidden), BF16),
        ],
        compiler_params=params,
        name="feed",
    )(
        flags,
        main,
        edge,
        queries,
        stats,
        w_proj,
        gain_attn.reshape(1, channels),
        w_expand,
        w_expand,
        spatial_w,
        spatial_w,
        w_reduce,
        gain_ff.reshape(1, channels),
    )
    return decoded.reshape(tile_rows, tile_cols, channels)


def solution(mesh):
    tile = P(("groups", "row"), "col", None)
    return jax.shard_map(
        body,
        mesh=mesh,
        in_specs=(tile, P(("groups", "row"), "col")) + (P(),) * 9,
        out_specs=tile,
        check_vma=False,
    )
```

```python
import functools

import jax
import jax.numpy as jnp
from jax import lax
from jax.experimental import pallas as pl
from jax.experimental.pallas import tpu as pltpu
from jax.sharding import PartitionSpec as P

LANES = 128
BLOCK = 256
PAD = 8
REACH = 3
VMEM_BYTES = 60 * 1024 * 1024
BF16 = jnp.bfloat16
F32 = jnp.float32


def lane_chunks(width=BLOCK):
    return [slice(low, low + LANES) for low in range(0, width, LANES)]


def depthwise_rows(streams, span, out_rows, emit):
    sums = [{} for _ in streams]
    for row_in in range(out_rows + span - 1):
        for side, (load, taps) in enumerate(streams):
            views = [load(row_in, b) for b in range(span)]
            for a in range(span):
                row_out = row_in - a
                if not 0 <= row_out < out_rows:
                    continue
                part = views[0] * taps[a * span]
                for b in range(1, span):
                    part = part + views[b] * taps[a * span + b]
                sums[side][row_out] = part if a == 0 else sums[side][row_out] + part
        done = row_in - span + 1
        if done >= 0:
            emit(done, *[s.pop(done) for s in sums])


def tap_list(weight_ref, lanes, rows):
    span = weight_ref.shape[0]
    return [
        jnp.broadcast_to(weight_ref[a, b : b + 1, lanes].astype(F32), (rows, LANES)).astype(BF16)
        for a in range(span)
        for b in range(span)
    ]


def head_mask(size, head):
    return (
        lax.broadcasted_iota(jnp.int32, (size, size), 0) // head
        == lax.broadcasted_iota(jnp.int32, (size, size), 1) // head
    )


def spread_blocks(group_ref):
    count, head, _ = group_ref.shape
    size = count * head
    rows = group_ref[...].reshape(size, head)
    pick = (
        lax.broadcasted_iota(jnp.int32, (head, size), 1) % head
        == lax.broadcasted_iota(jnp.int32, (head, size), 0)
    ).astype(BF16)
    wide = jnp.dot(rows, pick, preferred_element_type=F32)
    return jnp.where(head_mask(size, head), wide, 0.0).astype(BF16)


def fill_keep(keep_ref, out):
    rows, cols = keep_ref.shape
    cell = lax.broadcasted_iota(jnp.int32, (rows * cols, rows), 0)
    own_row = cell // cols == lax.broadcasted_iota(jnp.int32, (rows * cols, rows), 1)
    lines = jnp.dot(
        own_row.astype(BF16), keep_ref[...].astype(F32).astype(BF16), preferred_element_type=F32
    )
    cell = lax.broadcasted_iota(jnp.int32, (rows * cols, cols), 0)
    own_col = cell % cols == lax.broadcasted_iota(jnp.int32, (rows * cols, cols), 1)
    picked = jnp.where(own_col, lines, 0.0).astype(BF16)
    out[...] = jnp.dot(picked, jnp.ones((cols, LANES), BF16), preferred_element_type=F32).astype(
        BF16
    )


def summarise(keys, values, head):
    kv = lax.dot_general(
        keys[...], values[...], (((0,), (0,)), ((), ())), preferred_element_type=F32
    )
    lane_head = lax.broadcasted_iota(jnp.int32, (head, BLOCK), 1) // head
    packed = jnp.zeros((head, BLOCK), F32)
    for h in range(BLOCK // head):
        packed = packed + jnp.where(lane_head == h, kv[h * head : (h + 1) * head], 0.0)
    total = jnp.sum(keys[...].astype(F32), axis=0, keepdims=True)
    return packed, jnp.broadcast_to(total, (8, BLOCK))


def early_kernel(head, main_ref, keep_ref, wk_ref, wv_ref, proj_ref, stats_ref, keep, mat_k):
    @pl.when(pl.program_id(0) == 0)
    def _():
        fill_keep(keep_ref, keep)

    cells = main_ref.shape[0]
    step = 256
    for index, w_ref in enumerate((wk_ref, wv_ref)):
        w = w_ref[...]
        for start in range(0, cells, step):
            p = jnp.dot(main_ref[start : start + step], w, preferred_element_type=F32).astype(BF16)
            proj_ref[0, index, start : start + step] = p
            if index == 0:
                for lanes in lane_chunks():
                    mat_k[start : start + step, lanes] = (
                        jnp.maximum(p[:, lanes], 0) * keep[start : start + step]
                    )
    packed, total = summarise(mat_k, proj_ref.at[0, 1], head)
    stats_ref[0, 0:head] = packed
    stats_ref[0, head : head + 8] = total


def query_project_kernel(main_ref, w_ref, proj_ref):
    cells = main_ref.shape[0]
    step = 256
    w = w_ref[...]
    for start in range(0, cells, step):
        proj_ref[0, start : start + step] = jnp.dot(
            main_ref[start : start + step], w, preferred_element_type=F32
        ).astype(BF16)


def fill_projected(tile, flags, main, halos, w_ref, buf):
    rows, cols = tile
    stride = cols + PAD
    above_ref, below_ref, left_ref, right_ref = halos
    w = w_ref[...]

    def put(row, col, values):
        for ch, lanes in enumerate(lane_chunks()):
            start = PAD + (row + REACH) * stride + col
            buf[ch, pl.ds(start, values.shape[0]), :] = values[:, lanes]

    for row in range(rows):
        put(row, 0, main(slice(row * cols, (row + 1) * cols)).astype(F32))
    for halo_ref, row0 in ((above_ref, -REACH), (below_ref, rows)):
        p = jnp.dot(halo_ref[...], w, preferred_element_type=F32)
        for k in range(REACH):
            low = k * stride
            put(row0 + k, 0, p[low : low + cols])
            tail = p[low + cols : low + stride]
            put(row0 + k, -REACH, jnp.where(flags[0], tail, 0.0)[0:REACH])
            put(row0 + k, cols, jnp.where(flags[1], tail, 0.0)[REACH : 2 * REACH])
    for halo_ref, col0, flag in ((left_ref, -REACH, flags[0]), (right_ref, cols, flags[1])):
        p = jnp.where(flag, jnp.dot(halo_ref[...], w, preferred_element_type=F32), 0.0)
        for k in range(REACH):
            for ch, lanes in enumerate(lane_chunks()):
                start = PAD + REACH * stride + col0 + k
                buf[ch, pl.ds(start, rows, stride=stride), :] = p[k * rows : (k + 1) * rows, lanes]


def key_value_kernel(
    tile,
    head,
    flags_ref,
    proj_ref,
    above_ref,
    below_ref,
    left_ref,
    right_ref,
    keep_ref,
    early_ref,
    wk_ref,
    wv_ref,
    sk_ref,
    sv_ref,
    gk_ref,
    gv_ref,
    stats_ref,
    buf_k,
    buf_v,
    keep,
    mat_k,
    mat_v,
    agg_k,
    agg_v,
):
    rows, cols = tile
    stride = cols + PAD

    @pl.when(pl.program_id(0) == 0)
    def _():
        fill_keep(keep_ref, keep)

    flags = (flags_ref[2] != 0, flags_ref[3] != 0)
    halos = (above_ref, below_ref, left_ref, right_ref)
    parts = (
        (0, wk_ref, sk_ref, gk_ref, buf_k, mat_k, agg_k),
        (1, wv_ref, sv_ref, gv_ref, buf_v, mat_v, agg_v),
    )
    for index, w_ref, s_ref, g_ref, buf, mat, agg_out in parts:
        fill_projected(tile, flags, lambda at, i=index: proj_ref[0, i, at], halos, w_ref, buf)
    for index, w_ref, s_ref, g_ref, buf, mat, agg_out in parts:
        for ch, lanes in enumerate(lane_chunks()):
            taps = tap_list(s_ref, lanes, cols)

            def load(row_in, b, buf=buf, ch=ch):
                start = PAD + (row_in + 1) * stride + b - 2
                return buf[ch, pl.ds(start, cols), :].astype(BF16)

            def emit(row, value, out=mat, lanes=lanes):
                out[row * cols : (row + 1) * cols, lanes] = value

            depthwise_rows([(load, taps)], 5, rows, emit)
        blocks = spread_blocks(g_ref)
        step = 256
        for start in range(0, mat.shape[0], step):
            agg = jnp.dot(mat[start : start + step], blocks, preferred_element_type=F32)
            agg = agg.astype(BF16)
            if index == 0:
                for lanes in lane_chunks():
                    agg_out[start : start + step, lanes] = (
                        jnp.maximum(agg[:, lanes], 0) * keep[start : start + step]
                    )
            else:
                agg_out[start : start + step] = agg
    packed, total = summarise(agg_k, agg_v, head)
    stats_ref[0, 0:head] = early_ref[0, 0:head].astype(BF16)
    stats_ref[0, head : 2 * head] = packed.astype(BF16)
    stats_ref[0, 2 * head :] = jnp.concatenate(
        [early_ref[0, head : head + 8], total], axis=0
    ).astype(BF16)


def query_kernel(
    tile,
    flags_ref,
    proj_ref,
    above_ref,
    below_ref,
    left_ref,
    right_ref,
    w_ref,
    s_ref,
    g_ref,
    edge_ref,
    q_ref,
    buf,
    spread,
):
    rows, cols = tile
    stride = cols + PAD
    cells = rows * cols
    tall = rows + PAD
    flags = (flags_ref[2] != 0, flags_ref[3] != 0)
    halos = (above_ref, below_ref, left_ref, right_ref)
    fill_projected(tile, flags, lambda at: proj_ref[0, at], halos, w_ref, buf)
    side0 = cells + 2 * cols

    def slot(row):
        if row < 0:
            return cells
        if row >= rows:
            return cells + cols
        return row * cols

    for ch, lanes in enumerate(lane_chunks()):
        for row in (-1, rows):
            start = PAD + (row + REACH) * stride
            value = buf[ch, pl.ds(start, cols), :].astype(BF16)
            low = slot(row) - cells
            edge_ref[0, low : low + cols, lanes] = jnp.maximum(value, 0)
        for side, col in enumerate((-1, cols)):
            start = PAD + (REACH - 1) * stride + col
            value = buf[ch, pl.ds(start, tall, stride=stride), :].astype(BF16)
            low = 2 * cols + side * tall
            edge_ref[0, low : low + tall, lanes] = jnp.maximum(value, 0)

        taps = tap_list(s_ref, lanes, cols)

        def load(row_in, b, ch=ch):
            start = PAD + row_in * stride + b - 2
            return buf[ch, pl.ds(start, cols), :].astype(BF16)

        def emit(row, value, lanes=lanes):
            low = slot(row - 1)
            spread[low : low + cols, lanes] = value

        depthwise_rows([(load, taps)], 5, rows + 2, emit)
        taps = tap_list(s_ref, lanes, tall)
        for side, col in enumerate((-1, cols)):
            total = None
            for a in range(5):
                part = None
                for b in range(5):
                    start = PAD + a * stride + col + b - 2
                    view = buf[ch, pl.ds(start, tall, stride=stride), :].astype(BF16)
                    term = view * taps[a * 5 + b]
                    part = term if part is None else part + term
                total = part if total is None else total + part
            low = side0 + side * tall
            spread[low : low + tall, lanes] = total

    blocks = spread_blocks(g_ref)
    count = spread.shape[0]
    for start in range(0, count, 256):
        stop = min(count, start + 256)
        agg = jnp.dot(spread[start:stop], blocks, preferred_element_type=F32)
        q_ref[0, start:stop] = jnp.maximum(agg.astype(BF16), 0)


def rms_add(residual, branch, gain):
    scale = lax.rsqrt(jnp.mean(branch * branch, axis=-1, keepdims=True) + 1e-05)
    return residual.astype(F32) + branch * scale * gain


def silu(x):
    half = 0.5 * x
    return half * jnp.tanh(half) + half


def feed_kernel(
    tile,
    head,
    flags_ref,
    main_ref,
    above_ref,
    below_ref,
    left_ref,
    right_ref,
    proj_ref,
    q_edge_ref,
    q_far_ref,
    mine_ref,
    other_ref,
    wp_ref,
    gain_a_ref,
    wev_ref,
    weg_ref,
    spv_ref,
    spg_ref,
    wr_ref,
    gain_f_ref,
    out_ref,
    mid,
    att,
    edge,
    buf_v,
    buf_g,
    gated,
):
    rows, cols = tile
    stride = cols + PAD
    cells = rows * cols
    tall = rows + PAD
    step_index = pl.program_id(0)
    blocks = proj_ref.shape[0]
    channels = main_ref.shape[1]

    @pl.when(step_index == 0)
    def _():
        same = head_mask(BLOCK, head)
        eye = lax.broadcasted_iota(jnp.int32, (BLOCK, BLOCK), 0) == lax.broadcasted_iota(
            jnp.int32, (BLOCK, BLOCK), 1
        )
        count = mid.shape[0]
        bounds = [(s, s + 256) for s in range(0, cells, 256)] + [(cells, count)]
        for blk in range(blocks):
            mine = flags_ref[4] == blk
            for scale in range(2):
                low = scale * head
                packed = jnp.where(
                    mine,
                    mine_ref[low : low + head].astype(F32),
                    other_ref[low : low + head].astype(F32),
                )
                kv = jnp.where(same, jnp.concatenate([packed] * (BLOCK // head), axis=0), 0.0)
                both = jnp.where(
                    mine,
                    mine_ref[2 * head : 2 * head + 16].astype(F32),
                    other_ref[2 * head : 2 * head + 16].astype(F32),
                )
                sums = both[8 * scale : 8 * scale + 1]
                diag = jnp.where(eye, jnp.broadcast_to(sums, (BLOCK, BLOCK)), 0.0)
                ks = jnp.dot(
                    diag.astype(BF16), same.astype(BF16), preferred_element_type=F32
                ).astype(BF16)
                kv = kv.astype(BF16)
                low = scale * channels + blk * BLOCK
                for start, stop in bounds:
                    if scale:
                        q = q_far_ref[blk, start:stop]
                    elif start < cells:
                        q = jnp.maximum(proj_ref[blk, start:stop], 0)
                    else:
                        q = q_edge_ref[blk]
                    num = jnp.dot(q, kv, preferred_element_type=F32)
                    den = jnp.dot(q, ks, preferred_element_type=F32)
                    att[start:stop, low : low + BLOCK] = (num / (den + 1.0)).astype(BF16)

        edge[0:cols] = above_ref[(REACH - 1) * stride : (REACH - 1) * stride + cols].astype(F32)
        edge[cols : 2 * cols] = below_ref[0:cols].astype(F32)
        top_tail = above_ref[(REACH - 1) * stride + cols : REACH * stride].astype(F32)
        low_tail = below_ref[cols:stride].astype(F32)
        for side, (ref, near) in enumerate(((left_ref, REACH - 1), (right_ref, 0))):
            base = 2 * cols + side * tall
            pick = side * REACH + near
            edge[base : base + 1] = top_tail[pick : pick + 1]
            edge[base + 1 : base + 1 + rows] = ref[near * rows : (near + 1) * rows].astype(F32)
            edge[base + 1 + rows : base + 2 + rows] = low_tail[pick : pick + 1]
            edge[base + 2 + rows : base + tall] = jnp.zeros((tall - rows - 2, channels), F32)

        gain = gain_a_ref[...]
        for start, stop in bounds:
            branch = jnp.dot(att[start:stop], wp_ref[...], preferred_element_type=F32)
            if start < cells:
                mid[start:stop] = rms_add(main_ref[start:stop], branch, gain).astype(BF16)
            else:
                value = rms_add(edge[...], branch, gain)
                index = lax.broadcasted_iota(jnp.int32, (stop - start, 1), 0)
                side = index - 2 * cols
                place = lax.rem(side + tall, tall)
                in_rows = index < 2 * cols
                is_top = (index < cols) | (~in_rows & (place == 0))
                is_bottom = (in_rows & (index >= cols)) | (~in_rows & (place == rows + 1))
                is_left = ~in_rows & (side < tall)
                is_right = ~in_rows & (side >= tall)
                dead = (
                    (is_top & (flags_ref[0] == 0))
                    | (is_bottom & (flags_ref[1] == 0))
                    | (is_left & (flags_ref[2] == 0))
                    | (is_right & (flags_ref[3] == 0))
                )
                mid[start:stop] = jnp.where(dead, 0.0, value).astype(BF16)

    for w_ref, buf in ((wev_ref, buf_v), (weg_ref, buf_g)):
        w = w_ref[...]

        def put(row, values, buf=buf):
            start = PAD + (row + 1) * stride
            for ch, lanes in enumerate(lane_chunks()):
                buf[ch, pl.ds(start, cols), :] = values[:, lanes]

        group = 4
        for first in range(0, rows, group):
            p = silu(
                jnp.dot(
                    mid[first * cols : (first + group) * cols], w, preferred_element_type=F32
                )
            )
            for k in range(group):
                put(first + k, p[k * cols : (k + 1) * cols])
        p = silu(jnp.dot(mid[cells:], w, preferred_element_type=F32))
        put(-1, p[:cols])
        put(rows, p[cols : 2 * cols])
        for side, col in enumerate((-1, cols)):
            low = 2 * cols + side * tall
            for ch, lanes in enumerate(lane_chunks()):
                buf[ch, pl.ds(PAD + col, tall, stride=stride), :] = p[low : low + tall, lanes]

    base = step_index * BLOCK
    for ch, lanes in enumerate(lane_chunks()):
        streams = []
        for buf, sp_ref in ((buf_v, spv_ref), (buf_g, spg_ref)):

            def load(row_in, b, buf=buf, ch=ch):
                start = PAD + row_in * stride + b - 1
                return buf[ch, pl.ds(start, cols), :].astype(BF16)

            streams.append((load, tap_list(sp_ref, lanes, cols)))
        col0 = pl.multiple_of(base + ch * LANES, LANES)

        def emit(row, value, gate, col0=col0):
            gated[row * cols : (row + 1) * cols, pl.ds(col0, LANES)] = (
                value.astype(F32) * silu(gate.astype(F32))
            ).astype(BF16)

        depthwise_rows(streams, 3, rows, emit)

    @pl.when(step_index == pl.num_programs(0) - 1)
    def _():
        gain = gain_f_ref[...]
        for start in range(0, cells, 256):
            reduced = jnp.dot(
                gated[start : start + 256], wr_ref[...], preferred_element_type=F32
            )
            out_ref[start : start + 256] = rms_add(
                mid[start : start + 256], reduced, gain
            ).astype(BF16)


def neighbours(axis):
    count = lax.axis_size(axis)
    forward = [(i, i + 1) for i in range(count - 1)]
    return forward, [(b, a) for a, b in forward]


def total_over(x, axis):
    count = lax.axis_size(axis)
    if count & (count - 1):
        return lax.psum(x.astype(F32), axis).astype(BF16)
    step = 1
    while step < count:
        rest = count // step
        radix = 4 if rest % 4 == 0 and rest != 8 else 2
        total = x.astype(F32)
        for k in range(1, radix):
            pairs = [(i, i ^ (k * step)) for i in range(count)]
            total = total + lax.ppermute(x, axis, pairs).astype(F32)
        x = total.astype(BF16)
        step *= radix
    return x


def body(
    canvas,
    keep_mask,
    w_qkv,
    w_spread,
    w_group,
    w_proj,
    gain_attn,
    w_expand,
    w_spatial,
    w_reduce,
    gain_ff,
):
    rows, cols, channels = canvas.shape
    cells = rows * cols
    head = w_group.shape[1]
    hidden = w_reduce.shape[0]
    blocks = channels // BLOCK
    per = BLOCK // head
    tall = rows + PAD
    stride = cols + PAD
    tile = (rows, cols)
    flat_rows = PAD + (tall + 4) * stride
    flat_rows_ff = PAD + tall * stride

    col_index = lax.axis_index("col")
    col_count = lax.axis_size("col")
    row_index = lax.axis_index("row")
    row_count = lax.axis_size("row")
    swap = [(0, 1), (1, 0)]
    paired = col_count == 2 and blocks == 2

    def strip(low):
        return canvas[:, low : low + REACH].transpose(1, 0, 2)

    if col_count == 2:
        low = jnp.where(col_index == 0, cols - REACH, 0)
        mine = lax.dynamic_slice_in_dim(canvas, low, REACH, axis=1).transpose(1, 0, 2)
        left = right = lax.ppermute(mine, "col", swap)
    else:
        right_way, left_way = neighbours("col")
        left = lax.ppermute(strip(cols - REACH), "col", right_way)
        right = lax.ppermute(strip(0), "col", left_way)

    def wide(low):
        return jnp.concatenate(
            [
                canvas[low : low + REACH],
                left[:, low : low + REACH].transpose(1, 0, 2),
                right[:, low : low + REACH].transpose(1, 0, 2),
                jnp.zeros((REACH, PAD - 2 * REACH, channels), canvas.dtype),
            ],
            axis=1,
        )

    down, up = neighbours("row")
    above = lax.ppermute(wide(rows - REACH), "row", down).reshape(REACH * stride, channels)
    below = lax.ppermute(wide(0), "row", up).reshape(REACH * stride, channels)
    left = left.reshape(REACH * rows, channels)
    right = right.reshape(REACH * rows, channels)
    main = canvas.reshape(cells, channels)
    flags = jnp.stack(
        [
            (row_index > 0).astype(jnp.int32),
            (row_index < row_count - 1).astype(jnp.int32),
            (col_index > 0).astype(jnp.int32),
            (col_index < col_count - 1).astype(jnp.int32),
            col_index.astype(jnp.int32) if paired else jnp.int32(0),
        ]
    )

    def whole(shape):
        return pl.BlockSpec(shape, lambda *_: (0,) * len(shape))

    smem = pl.BlockSpec(memory_space=pltpu.SMEM)
    params = pltpu.CompilerParams(
        dimension_semantics=("arbitrary",), vmem_limit_bytes=VMEM_BYTES
    )

    def cost(macs, moved):
        return pl.CostEstimate(flops=2 * macs, bytes_accessed=moved, transcendentals=0)

    proj_kv, early = pl.pallas_call(
        functools.partial(early_kernel, head),
        grid=(blocks,),
        in_specs=[
            whole(main.shape),
            whole(keep_mask.shape),
            pl.BlockSpec((channels, BLOCK), lambda j: (0, blocks + j)),
            pl.BlockSpec((channels, BLOCK), lambda j: (0, 2 * blocks + j)),
        ],
        out_specs=[
            pl.BlockSpec((1, 2, cells, BLOCK), lambda j: (j, 0, 0, 0)),
            pl.BlockSpec((1, head + 8, BLOCK), lambda j: (j, 0, 0)),
        ],
        out_shape=[
            jax.ShapeDtypeStruct((blocks, 2, cells, BLOCK), BF16),
            jax.ShapeDtypeStruct((blocks, head + 8, BLOCK), F32),
        ],
        scratch_shapes=[pltpu.VMEM((cells, LANES), BF16), pltpu.VMEM((cells, BLOCK), BF16)],
        compiler_params=params,
        cost_estimate=cost(2 * cells * channels * channels, 6 * cells * channels),
        name="early",
    )(main, keep_mask, w_qkv, w_qkv)

    proj_q = pl.pallas_call(
        query_project_kernel,
        grid=(blocks,),
        in_specs=[
            whole(main.shape),
            pl.BlockSpec((channels, BLOCK), lambda j: (0, j)),
        ],
        out_specs=pl.BlockSpec((1, cells, BLOCK), lambda j: (j, 0, 0)),
        out_shape=jax.ShapeDtypeStruct((blocks, cells, BLOCK), BF16),
        compiler_params=params,
        cost_estimate=cost(cells * channels * channels, 4 * cells * channels),
        name="query_project",
    )(main, w_qkv)

    halos = (above, below, left, right)
    halo_specs = [whole(h.shape) for h in halos]
    stats = pl.pallas_call(
        functools.partial(key_value_kernel, tile, head),
        grid=(blocks,),
        in_specs=[
            smem,
            pl.BlockSpec((1, 2, cells, BLOCK), lambda j: (j, 0, 0, 0)),
            *halo_specs,
            whole(keep_mask.shape),
            pl.BlockSpec((1, head + 8, BLOCK), lambda j: (j, 0, 0)),
            pl.BlockSpec((channels, BLOCK), lambda j: (0, blocks + j)),
            pl.BlockSpec((channels, BLOCK), lambda j: (0, 2 * blocks + j)),
            pl.BlockSpec((5, 5, BLOCK), lambda j: (0, 0, blocks + j)),
            pl.BlockSpec((5, 5, BLOCK), lambda j: (0, 0, 2 * blocks + j)),
            pl.BlockSpec((per, head, head), lambda j: (blocks + j, 0, 0)),
            pl.BlockSpec((per, head, head), lambda j: (2 * blocks + j, 0, 0)),
        ],
        out_specs=pl.BlockSpec((1, 2 * head + 16, BLOCK), lambda j: (j, 0, 0)),
        out_shape=jax.ShapeDtypeStruct((blocks, 2 * head + 16, BLOCK), BF16),
        scratch_shapes=[
            pltpu.VMEM((BLOCK // LANES, flat_rows, LANES), F32),
            pltpu.VMEM((BLOCK // LANES, flat_rows, LANES), F32),
            pltpu.VMEM((cells, LANES), BF16),
            pltpu.VMEM((cells, BLOCK), BF16),
            pltpu.VMEM((cells, BLOCK), BF16),
            pltpu.VMEM((cells, BLOCK), BF16),
            pltpu.VMEM((cells, BLOCK), BF16),
        ],
        compiler_params=params,
        cost_estimate=cost(8 * cells * channels * channels, 8 * cells * channels),
        name="key_value",
    )(
        flags,
        proj_kv,
        *halos,
        keep_mask,
        early,
        w_qkv,
        w_qkv,
        w_spread,
        w_spread,
        w_group,
        w_group,
    )
    if paired:
        sent = lax.dynamic_index_in_dim(stats, 1 - col_index, keepdims=False)
        kept = lax.dynamic_index_in_dim(stats, col_index, keepdims=False)
        got = lax.ppermute(sent, "col", swap)
        mine = total_over((kept.astype(F32) + got.astype(F32)).astype(BF16), "row")
        other = lax.ppermute(mine, "col", swap)
    else:
        stats = total_over(total_over(stats, "col"), "row")
        mine, other = stats[0], stats[blocks - 1]

    count = cells + 2 * cols + 2 * tall
    q_edge, q_far = pl.pallas_call(
        functools.partial(query_kernel, tile),
        grid=(blocks,),
        in_specs=[
            smem,
            pl.BlockSpec((1, cells, BLOCK), lambda j: (j, 0, 0)),
            *halo_specs,
            pl.BlockSpec((channels, BLOCK), lambda j: (0, j)),
            pl.BlockSpec((5, 5, BLOCK), lambda j: (0, 0, j)),
            pl.BlockSpec((per, head, head), lambda j: (j, 0, 0)),
        ],
        out_specs=[
            pl.BlockSpec((1, count - cells, BLOCK), lambda j: (j, 0, 0)),
            pl.BlockSpec((1, count, BLOCK), lambda j: (j, 0, 0)),
        ],
        out_shape=[
            jax.ShapeDtypeStruct((blocks, count - cells, BLOCK), BF16),
            jax.ShapeDtypeStruct((blocks, count, BLOCK), BF16),
        ],
        scratch_shapes=[
            pltpu.VMEM((BLOCK // LANES, flat_rows, LANES), F32),
            pltpu.VMEM((count, BLOCK), BF16),
        ],
        compiler_params=params,
        cost_estimate=cost(5 * cells * channels * channels, 6 * cells * channels),
        name="query",
    )(flags, proj_q, *halos, w_qkv, w_spread, w_group)

    steps = hidden // BLOCK
    decoded = pl.pallas_call(
        functools.partial(feed_kernel, tile, head),
        grid=(steps,),
        in_specs=[
            smem,
            whole(main.shape),
            *halo_specs,
            whole(proj_q.shape),
            whole(q_edge.shape),
            whole(q_far.shape),
            whole(mine.shape),
            whole(other.shape),
            whole(w_proj.shape),
            whole((1, channels)),
            pl.BlockSpec((channels, BLOCK), lambda j: (0, j)),
            pl.BlockSpec((channels, BLOCK), lambda j: (0, steps + j)),
            pl.BlockSpec((3, 3, BLOCK), lambda j: (0, 0, j)),
            pl.BlockSpec((3, 3, BLOCK), lambda j: (0, 0, steps + j)),
            whole(w_reduce.shape),
            whole((1, channels)),
        ],
        out_specs=whole(main.shape),
        out_shape=jax.ShapeDtypeStruct(main.shape, BF16),
        scratch_shapes=[
            pltpu.VMEM((count, channels), BF16),
            pltpu.VMEM((count, 2 * channels), BF16),
            pltpu.VMEM((count - cells, channels), F32),
            pltpu.VMEM((BLOCK // LANES, flat_rows_ff, LANES), F32),
            pltpu.VMEM((BLOCK // LANES, flat_rows_ff, LANES), F32),
            pltpu.VMEM((cells, hidden), BF16),
        ],
        compiler_params=params,
        name="feed",
    )(
        flags,
        main,
        *halos,
        proj_q,
        q_edge,
        q_far,
        mine,
        other,
        w_proj,
        gain_attn.reshape(1, channels),
        w_expand,
        w_expand,
        w_spatial,
        w_spatial,
        w_reduce,
        gain_ff.reshape(1, channels),
    )
    return decoded.reshape(rows, cols, channels)


def solution(mesh):
    tile = P(("groups", "row"), "col", None)
    return jax.shard_map(
        body,
        mesh=mesh,
        in_specs=(tile, P(("groups", "row"), "col")) + (P(),) * 9,
        out_specs=tile,
        check_vma=False,
    )
```

```python
import functools

import jax
import jax.numpy as jnp
from jax import lax
from jax.experimental import pallas as pl
from jax.experimental.pallas import tpu as pltpu
from jax.sharding import PartitionSpec as P

LANES = 128
BLOCK = 256
PAD = 8
REACH = 3
VMEM_BYTES = 60 * 1024 * 1024
BF16 = jnp.bfloat16
F32 = jnp.float32


def lane_chunks(width=BLOCK):
    return [slice(low, low + LANES) for low in range(0, width, LANES)]


def depthwise_rows(streams, span, out_rows, emit):
    sums = [{} for _ in streams]
    for row_in in range(out_rows + span - 1):
        for side, (load, taps) in enumerate(streams):
            views = [load(row_in, b) for b in range(span)]
            for a in range(span):
                row_out = row_in - a
                if not 0 <= row_out < out_rows:
                    continue
                part = views[0] * taps[a * span]
                for b in range(1, span):
                    part = part + views[b] * taps[a * span + b]
                sums[side][row_out] = part if a == 0 else sums[side][row_out] + part
        done = row_in - span + 1
        if done >= 0:
            emit(done, *[s.pop(done) for s in sums])


def tap_list(weight_ref, lanes, rows):
    span = weight_ref.shape[0]
    return [
        jnp.broadcast_to(weight_ref[a, b : b + 1, lanes].astype(F32), (rows, LANES)).astype(BF16)
        for a in range(span)
        for b in range(span)
    ]


def head_mask(size, head):
    return (
        lax.broadcasted_iota(jnp.int32, (size, size), 0) // head
        == lax.broadcasted_iota(jnp.int32, (size, size), 1) // head
    )


def spread_blocks(group_ref):
    count, head, _ = group_ref.shape
    size = count * head
    rows = group_ref[...].reshape(size, head)
    pick = (
        lax.broadcasted_iota(jnp.int32, (head, size), 1) % head
        == lax.broadcasted_iota(jnp.int32, (head, size), 0)
    ).astype(BF16)
    wide = jnp.dot(rows, pick, preferred_element_type=F32)
    return jnp.where(head_mask(size, head), wide, 0.0).astype(BF16)


def fill_keep(keep_ref, out):
    rows, cols = keep_ref.shape
    cell = lax.broadcasted_iota(jnp.int32, (rows * cols, rows), 0)
    own_row = cell // cols == lax.broadcasted_iota(jnp.int32, (rows * cols, rows), 1)
    lines = jnp.dot(
        own_row.astype(BF16), keep_ref[...].astype(F32).astype(BF16), preferred_element_type=F32
    )
    cell = lax.broadcasted_iota(jnp.int32, (rows * cols, cols), 0)
    own_col = cell % cols == lax.broadcasted_iota(jnp.int32, (rows * cols, cols), 1)
    picked = jnp.where(own_col, lines, 0.0).astype(BF16)
    out[...] = jnp.dot(picked, jnp.ones((cols, LANES), BF16), preferred_element_type=F32).astype(
        BF16
    )


def summarise(keys, values, head):
    kv = lax.dot_general(
        keys[...], values[...], (((0,), (0,)), ((), ())), preferred_element_type=F32
    )
    lane_head = lax.broadcasted_iota(jnp.int32, (head, BLOCK), 1) // head
    packed = jnp.zeros((head, BLOCK), F32)
    for h in range(BLOCK // head):
        packed = packed + jnp.where(lane_head == h, kv[h * head : (h + 1) * head], 0.0)
    total = jnp.sum(keys[...].astype(F32), axis=0, keepdims=True)
    return packed, jnp.broadcast_to(total, (8, BLOCK))


def early_kernel(head, main_ref, keep_ref, wk_ref, wv_ref, proj_ref, stats_ref, keep, mat_k):
    @pl.when(pl.program_id(0) == 0)
    def _():
        fill_keep(keep_ref, keep)

    cells = main_ref.shape[0]
    step = 256
    for index, w_ref in enumerate((wk_ref, wv_ref)):
        w = w_ref[...]
        for start in range(0, cells, step):
            p = jnp.dot(main_ref[start : start + step], w, preferred_element_type=F32).astype(BF16)
            proj_ref[0, index, start : start + step] = p
            if index == 0:
                for lanes in lane_chunks():
                    mat_k[start : start + step, lanes] = (
                        jnp.maximum(p[:, lanes], 0) * keep[start : start + step]
                    )
    packed, total = summarise(mat_k, proj_ref.at[0, 1], head)
    stats_ref[0, 0:head] = packed
    stats_ref[0, head : head + 8] = total


def query_project_kernel(main_ref, w_ref, proj_ref):
    cells = main_ref.shape[0]
    step = 256
    w = w_ref[...]
    for start in range(0, cells, step):
        proj_ref[0, start : start + step] = jnp.dot(
            main_ref[start : start + step], w, preferred_element_type=F32
        ).astype(BF16)


def fill_projected(tile, flags, main, halos, w_ref, buf):
    rows, cols = tile
    stride = cols + PAD
    above_ref, below_ref, left_ref, right_ref = halos
    w = w_ref[...]

    def put(row, col, values):
        for ch, lanes in enumerate(lane_chunks()):
            start = PAD + (row + REACH) * stride + col
            buf[ch, pl.ds(start, values.shape[0]), :] = values[:, lanes]

    for row in range(rows):
        put(row, 0, main(slice(row * cols, (row + 1) * cols)).astype(F32))
    for halo_ref, row0 in ((above_ref, -REACH), (below_ref, rows)):
        p = jnp.dot(halo_ref[...], w, preferred_element_type=F32)
        for k in range(REACH):
            low = k * stride
            put(row0 + k, 0, p[low : low + cols])
            tail = p[low + cols : low + stride]
            put(row0 + k, -REACH, jnp.where(flags[0], tail, 0.0)[0:REACH])
            put(row0 + k, cols, jnp.where(flags[1], tail, 0.0)[REACH : 2 * REACH])
    for halo_ref, col0, flag in ((left_ref, -REACH, flags[0]), (right_ref, cols, flags[1])):
        p = jnp.where(flag, jnp.dot(halo_ref[...], w, preferred_element_type=F32), 0.0)
        for k in range(REACH):
            for ch, lanes in enumerate(lane_chunks()):
                start = PAD + REACH * stride + col0 + k
                buf[ch, pl.ds(start, rows, stride=stride), :] = p[k * rows : (k + 1) * rows, lanes]


def key_value_kernel(
    tile,
    head,
    flags_ref,
    proj_ref,
    above_ref,
    below_ref,
    left_ref,
    right_ref,
    keep_ref,
    early_ref,
    wk_ref,
    wv_ref,
    sk_ref,
    sv_ref,
    gk_ref,
    gv_ref,
    mine_ref,
    sent_ref,
    buf_k,
    buf_v,
    keep,
    mat_k,
    mat_v,
    agg_k,
    agg_v,
):
    rows, cols = tile
    stride = cols + PAD

    @pl.when(pl.program_id(0) == 0)
    def _():
        fill_keep(keep_ref, keep)

    flags = (flags_ref[2] != 0, flags_ref[3] != 0)
    halos = (above_ref, below_ref, left_ref, right_ref)
    parts = (
        (0, wk_ref, sk_ref, gk_ref, buf_k, mat_k, agg_k),
        (1, wv_ref, sv_ref, gv_ref, buf_v, mat_v, agg_v),
    )
    for index, w_ref, s_ref, g_ref, buf, mat, agg_out in parts:
        fill_projected(tile, flags, lambda at, i=index: proj_ref[0, i, at], halos, w_ref, buf)
    for index, w_ref, s_ref, g_ref, buf, mat, agg_out in parts:
        for ch, lanes in enumerate(lane_chunks()):
            taps = tap_list(s_ref, lanes, cols)

            def load(row_in, b, buf=buf, ch=ch):
                start = PAD + (row_in + 1) * stride + b - 2
                return buf[ch, pl.ds(start, cols), :].astype(BF16)

            def emit(row, value, out=mat, lanes=lanes):
                out[row * cols : (row + 1) * cols, lanes] = value

            depthwise_rows([(load, taps)], 5, rows, emit)
        blocks = spread_blocks(g_ref)
        step = 256
        for start in range(0, mat.shape[0], step):
            agg = jnp.dot(mat[start : start + step], blocks, preferred_element_type=F32)
            agg = agg.astype(BF16)
            if index == 0:
                for lanes in lane_chunks():
                    agg_out[start : start + step, lanes] = (
                        jnp.maximum(agg[:, lanes], 0) * keep[start : start + step]
                    )
            else:
                agg_out[start : start + step] = agg
    packed, total = summarise(agg_k, agg_v, head)
    own = pl.program_id(0) == flags_ref[4]

    def store(out_ref):
        out_ref[0:head] = early_ref[0, 0:head].astype(BF16)
        out_ref[head : 2 * head] = packed.astype(BF16)
        out_ref[2 * head :] = jnp.concatenate(
            [early_ref[0, head : head + 8], total], axis=0
        ).astype(BF16)

    @pl.when(own)
    def _():
        store(mine_ref)

    @pl.when(jnp.logical_not(own))
    def _():
        store(sent_ref)


def query_kernel(
    tile,
    flags_ref,
    proj_ref,
    above_ref,
    below_ref,
    left_ref,
    right_ref,
    w_ref,
    s_ref,
    g_ref,
    edge_ref,
    q_ref,
    buf,
    spread,
):
    rows, cols = tile
    stride = cols + PAD
    cells = rows * cols
    tall = rows + PAD
    flags = (flags_ref[2] != 0, flags_ref[3] != 0)
    halos = (above_ref, below_ref, left_ref, right_ref)
    fill_projected(tile, flags, lambda at: proj_ref[0, at], halos, w_ref, buf)
    side0 = cells + 2 * cols

    def slot(row):
        if row < 0:
            return cells
        if row >= rows:
            return cells + cols
        return row * cols

    for ch, lanes in enumerate(lane_chunks()):
        for row in (-1, rows):
            start = PAD + (row + REACH) * stride
            value = buf[ch, pl.ds(start, cols), :].astype(BF16)
            low = slot(row) - cells
            edge_ref[low : low + cols, lanes] = jnp.maximum(value, 0)
        for side, col in enumerate((-1, cols)):
            start = PAD + (REACH - 1) * stride + col
            value = buf[ch, pl.ds(start, tall, stride=stride), :].astype(BF16)
            low = 2 * cols + side * tall
            edge_ref[low : low + tall, lanes] = jnp.maximum(value, 0)

        taps = tap_list(s_ref, lanes, cols)

        def load(row_in, b, ch=ch):
            start = PAD + row_in * stride + b - 2
            return buf[ch, pl.ds(start, cols), :].astype(BF16)

        def emit(row, value, lanes=lanes):
            low = slot(row - 1)
            spread[low : low + cols, lanes] = value

        depthwise_rows([(load, taps)], 5, rows + 2, emit)
        taps = tap_list(s_ref, lanes, tall)
        for side, col in enumerate((-1, cols)):
            total = None
            for a in range(5):
                part = None
                for b in range(5):
                    start = PAD + a * stride + col + b - 2
                    view = buf[ch, pl.ds(start, tall, stride=stride), :].astype(BF16)
                    term = view * taps[a * 5 + b]
                    part = term if part is None else part + term
                total = part if total is None else total + part
            low = side0 + side * tall
            spread[low : low + tall, lanes] = total

    blocks = spread_blocks(g_ref)
    count = spread.shape[0]
    for start in range(0, count, 256):
        stop = min(count, start + 256)
        agg = jnp.dot(spread[start:stop], blocks, preferred_element_type=F32)
        q_ref[start:stop] = jnp.maximum(agg.astype(BF16), 0)


def rms_add(residual, branch, gain):
    scale = lax.rsqrt(jnp.mean(branch * branch, axis=-1, keepdims=True) + 1e-05)
    return residual.astype(F32) + branch * scale * gain


def silu(x):
    half = 0.5 * x
    return half * jnp.tanh(half) + half


def feed_kernel(
    tile,
    head,
    flags_ref,
    main_any,
    above_ref,
    below_ref,
    left_ref,
    right_ref,
    proj_any,
    q_edge_a_ref,
    q_edge_b_ref,
    q_far_a_any,
    q_far_b_any,
    mine_ref,
    other_ref,
    wp_any,
    gain_a_ref,
    we_any,
    sp_ref,
    wr_any,
    gain_f_ref,
    out_any,
    main_ref,
    proj_ref,
    q_far_ref,
    wp_ref,
    we_ref,
    wr_ref,
    mid,
    half,
    att,
    edge,
    buf_av,
    buf_ag,
    buf_bv,
    buf_bg,
    gated,
    result,
    sems,
):
    rows, cols = tile
    stride = cols + PAD
    cells = rows * cols
    tall = rows + PAD
    blocks = proj_ref.shape[0]
    channels = main_ref.shape[1]
    hidden = wr_ref.shape[0]
    steps = hidden // BLOCK
    count = mid.shape[0]
    big = cells // 2
    bounds = [(0, big), (big, cells), (cells, count)]

    loads = [
        pltpu.make_async_copy(src, dst, sems.at[i])
        for i, (src, dst) in enumerate(
            (
                (proj_any, proj_ref),
                (q_far_a_any, q_far_ref.at[0]),
                (q_far_b_any, q_far_ref.at[1]),
                (wp_any, wp_ref),
                (main_any, main_ref),
                (we_any, we_ref),
                (wr_any, wr_ref),
            )
        )
    ]
    for load in loads:
        load.start()
    q_edges = (q_edge_a_ref, q_edge_b_ref)

    edge[0:cols] = above_ref[(REACH - 1) * stride : (REACH - 1) * stride + cols].astype(F32)
    edge[cols : 2 * cols] = below_ref[0:cols].astype(F32)
    top_tail = above_ref[(REACH - 1) * stride + cols : REACH * stride].astype(F32)
    low_tail = below_ref[cols:stride].astype(F32)
    for side, (ref, near) in enumerate(((left_ref, REACH - 1), (right_ref, 0))):
        base = 2 * cols + side * tall
        pick = side * REACH + near
        edge[base : base + 1] = top_tail[pick : pick + 1]
        edge[base + 1 : base + 1 + rows] = ref[near * rows : (near + 1) * rows].astype(F32)
        edge[base + 1 + rows : base + 2 + rows] = low_tail[pick : pick + 1]
        edge[base + 2 + rows : base + tall] = jnp.zeros((tall - rows - 2, channels), F32)

    same = head_mask(BLOCK, head)
    eye = lax.broadcasted_iota(jnp.int32, (BLOCK, BLOCK), 0) == lax.broadcasted_iota(
        jnp.int32, (BLOCK, BLOCK), 1
    )
    loads[0].wait()
    for scale in range(2):
        if scale:
            loads[1].wait()
            loads[2].wait()
        for blk in range(blocks):
            mine = flags_ref[4] == blk
            low = scale * head
            packed = jnp.where(
                mine,
                mine_ref[low : low + head].astype(F32),
                other_ref[low : low + head].astype(F32),
            )
            kv = jnp.where(same, jnp.concatenate([packed] * (BLOCK // head), axis=0), 0.0)
            both = jnp.where(
                mine,
                mine_ref[2 * head : 2 * head + 16].astype(F32),
                other_ref[2 * head : 2 * head + 16].astype(F32),
            )
            sums = both[8 * scale : 8 * scale + 1]
            diag = jnp.where(eye, jnp.broadcast_to(sums, (BLOCK, BLOCK)), 0.0)
            ks = jnp.dot(
                diag.astype(BF16), same.astype(BF16), preferred_element_type=F32
            ).astype(BF16)
            kv = kv.astype(BF16)
            low = scale * channels + blk * BLOCK
            for start, stop in bounds:
                if scale:
                    q = q_far_ref[blk, start:stop]
                elif start < cells:
                    q = jnp.maximum(proj_ref[blk, start:stop], 0)
                else:
                    q = q_edges[blk][...]
                num = jnp.dot(q, kv, preferred_element_type=F32)
                den = jnp.dot(q, ks, preferred_element_type=F32)
                att[start:stop, low : low + BLOCK] = (num / (den + 1.0)).astype(BF16)

    gain = gain_a_ref[...]
    loads[3].wait()
    loads[4].wait()
    for start, stop in bounds:
        branch = jnp.dot(att[start:stop], wp_ref[...], preferred_element_type=F32)
        if start < cells:
            value = rms_add(main_ref[start:stop], branch, gain)
        else:
            value = rms_add(edge[...], branch, gain)
            index = lax.broadcasted_iota(jnp.int32, (stop - start, 1), 0)
            side = index - 2 * cols
            place = lax.rem(side + tall, tall)
            in_rows = index < 2 * cols
            is_top = (index < cols) | (~in_rows & (place == 0))
            is_bottom = (in_rows & (index >= cols)) | (~in_rows & (place == rows + 1))
            is_left = ~in_rows & (side < tall)
            is_right = ~in_rows & (side >= tall)
            dead = (
                (is_top & (flags_ref[0] == 0))
                | (is_bottom & (flags_ref[1] == 0))
                | (is_left & (flags_ref[2] == 0))
                | (is_right & (flags_ref[3] == 0))
            )
            value = jnp.where(dead, 0.0, value)
        value = value.astype(BF16)
        mid[start:stop] = value
        half[start:stop] = value * jnp.asarray(0.5, BF16)

    def expand(j, bufs):
        for part, buf in enumerate(bufs):
            w = we_ref[:, pl.ds(pl.multiple_of(part * hidden + j * BLOCK, BLOCK), BLOCK)]
            for start, stop in bounds:
                p = jnp.dot(half[start:stop], w, preferred_element_type=F32)
                p = p * jnp.tanh(p) + p
                for ch, lanes in enumerate(lane_chunks()):

                    def put(row, low):
                        at = PAD + (row + 1) * stride
                        buf[ch, pl.ds(at, cols), :] = p[low : low + cols, lanes]

                    if start < cells:
                        for low in range(0, stop - start, cols):
                            put((start + low) // cols, low)
                    else:
                        put(-1, 0)
                        put(rows, cols)
                        for side, col in enumerate((-1, cols)):
                            low = 2 * cols + side * tall
                            buf[ch, pl.ds(PAD + col, tall, stride=stride), :] = p[
                                low : low + tall, lanes
                            ]

    def mix(j, bufs):
        for ch in range(BLOCK // LANES):
            col0 = pl.multiple_of(j * BLOCK + ch * LANES, LANES)
            streams = []
            for part, buf in enumerate(bufs):

                def load(row_in, b, buf=buf, ch=ch):
                    start = PAD + row_in * stride + b - 1
                    return buf[ch, pl.ds(start, cols), :].astype(BF16)

                at = pl.multiple_of(part * hidden + j * BLOCK + ch * LANES, LANES)
                taps = tap_list(sp_ref, pl.ds(at, LANES), cols)
                if part:
                    taps = [t * jnp.asarray(0.5, BF16) for t in taps]
                streams.append((load, taps))

            def emit(row, value, gate, col0=col0):
                gated[row * cols : (row + 1) * cols, pl.ds(col0, LANES)] = value * (
                    gate * jnp.tanh(gate) + gate
                )

            depthwise_rows(streams, 3, rows, emit)

    loads[5].wait()
    bufs_a, bufs_b = (buf_av, buf_ag), (buf_bv, buf_bg)
    expand(0, bufs_a)

    def pair(i, carry):
        j = 2 * i
        expand(j + 1, bufs_b)
        mix(j, bufs_a)
        expand(jnp.minimum(j + 2, steps - 1), bufs_a)
        mix(j + 1, bufs_b)
        return carry

    lax.fori_loop(0, steps // 2, pair, 0)

    loads[6].wait()
    gain = gain_f_ref[...]
    stores = []
    for n, (start, stop) in enumerate(bounds[:2]):
        reduced = jnp.dot(gated[start:stop], wr_ref[...], preferred_element_type=F32)
        result[start:stop] = rms_add(mid[start:stop], reduced, gain).astype(BF16)
        store = pltpu.make_async_copy(
            result.at[start:stop], out_any.at[start:stop], sems.at[len(loads) + n]
        )
        store.start()
        stores.append(store)
    for store in stores:
        store.wait()


def neighbours(axis):
    count = lax.axis_size(axis)
    forward = [(i, i + 1) for i in range(count - 1)]
    return forward, [(b, a) for a, b in forward]


def total_over(x, axis):
    count = lax.axis_size(axis)
    if count & (count - 1):
        return lax.psum(x.astype(F32), axis).astype(BF16)
    step = 1
    while step < count:
        rest = count // step
        radix = 4 if rest % 4 == 0 and rest != 8 else 2
        total = x.astype(F32)
        for k in range(1, radix):
            pairs = [(i, i ^ (k * step)) for i in range(count)]
            total = total + lax.ppermute(x, axis, pairs).astype(F32)
        x = total.astype(BF16)
        step *= radix
    return x


def body(
    canvas,
    keep_mask,
    w_qkv,
    w_spread,
    w_group,
    w_proj,
    gain_attn,
    w_expand,
    w_spatial,
    w_reduce,
    gain_ff,
):
    rows, cols, channels = canvas.shape
    cells = rows * cols
    head = w_group.shape[1]
    hidden = w_reduce.shape[0]
    blocks = channels // BLOCK
    per = BLOCK // head
    tall = rows + PAD
    stride = cols + PAD
    tile = (rows, cols)
    flat_rows = PAD + (tall + 4) * stride
    flat_rows_ff = PAD + tall * stride

    main = canvas.reshape(cells, channels)

    def whole(shape):
        return pl.BlockSpec(shape, lambda *_: (0,) * len(shape))

    smem = pl.BlockSpec(memory_space=pltpu.SMEM)
    params = pltpu.CompilerParams(
        dimension_semantics=("arbitrary",), vmem_limit_bytes=VMEM_BYTES
    )

    def cost(macs, moved):
        return pl.CostEstimate(flops=2 * macs, bytes_accessed=moved, transcendentals=0)

    col_index = lax.axis_index("col")
    col_count = lax.axis_size("col")
    row_index = lax.axis_index("row")
    row_count = lax.axis_size("row")
    swap = [(0, 1), (1, 0)]
    paired = col_count == 2 and blocks == 2

    def strip(low):
        return canvas[:, low : low + REACH].transpose(1, 0, 2)

    if col_count == 2:
        low = jnp.where(col_index == 0, cols - REACH, 0)
        mine = lax.dynamic_slice_in_dim(canvas, low, REACH, axis=1).transpose(1, 0, 2)
        left = right = lax.ppermute(mine, "col", swap)
    else:
        right_way, left_way = neighbours("col")
        left = lax.ppermute(strip(cols - REACH), "col", right_way)
        right = lax.ppermute(strip(0), "col", left_way)

    proj_kv, early = pl.pallas_call(
        functools.partial(early_kernel, head),
        grid=(blocks,),
        in_specs=[
            whole(main.shape),
            whole(keep_mask.shape),
            pl.BlockSpec((channels, BLOCK), lambda j: (0, blocks + j)),
            pl.BlockSpec((channels, BLOCK), lambda j: (0, 2 * blocks + j)),
        ],
        out_specs=[
            pl.BlockSpec((1, 2, cells, BLOCK), lambda j: (j, 0, 0, 0)),
            pl.BlockSpec((1, head + 8, BLOCK), lambda j: (j, 0, 0)),
        ],
        out_shape=[
            jax.ShapeDtypeStruct((blocks, 2, cells, BLOCK), BF16),
            jax.ShapeDtypeStruct((blocks, head + 8, BLOCK), F32),
        ],
        scratch_shapes=[pltpu.VMEM((cells, LANES), BF16), pltpu.VMEM((cells, BLOCK), BF16)],
        compiler_params=params,
        cost_estimate=cost(2 * cells * channels * channels, 6 * cells * channels),
        name="early",
    )(main, keep_mask, w_qkv, w_qkv)

    left, right, early = lax.optimization_barrier((left, right, early))

    def wide(low):
        return jnp.concatenate(
            [
                canvas[low : low + REACH],
                left[:, low : low + REACH].transpose(1, 0, 2),
                right[:, low : low + REACH].transpose(1, 0, 2),
                jnp.zeros((REACH, PAD - 2 * REACH, channels), canvas.dtype),
            ],
            axis=1,
        )

    down, up = neighbours("row")
    above = lax.ppermute(wide(rows - REACH), "row", down).reshape(REACH * stride, channels)
    below = lax.ppermute(wide(0), "row", up).reshape(REACH * stride, channels)
    left = left.reshape(REACH * rows, channels)
    right = right.reshape(REACH * rows, channels)
    flags = jnp.stack(
        [
            (row_index > 0).astype(jnp.int32),
            (row_index < row_count - 1).astype(jnp.int32),
            (col_index > 0).astype(jnp.int32),
            (col_index < col_count - 1).astype(jnp.int32),
            col_index.astype(jnp.int32) if paired else jnp.int32(0),
        ]
    )

    proj_q = pl.pallas_call(
        query_project_kernel,
        grid=(blocks,),
        in_specs=[
            whole(main.shape),
            pl.BlockSpec((channels, BLOCK), lambda j: (0, j)),
        ],
        out_specs=pl.BlockSpec((1, cells, BLOCK), lambda j: (j, 0, 0)),
        out_shape=jax.ShapeDtypeStruct((blocks, cells, BLOCK), BF16),
        compiler_params=params,
        cost_estimate=cost(cells * channels * channels, 4 * cells * channels),
        name="query_project",
    )(main, w_qkv)

    halos = (above, below, left, right)
    halo_specs = [whole(h.shape) for h in halos]
    mine, sent = pl.pallas_call(
        functools.partial(key_value_kernel, tile, head),
        grid=(blocks,),
        in_specs=[
            smem,
            pl.BlockSpec((1, 2, cells, BLOCK), lambda j: (j, 0, 0, 0)),
            *halo_specs,
            whole(keep_mask.shape),
            pl.BlockSpec((1, head + 8, BLOCK), lambda j: (j, 0, 0)),
            pl.BlockSpec((channels, BLOCK), lambda j: (0, blocks + j)),
            pl.BlockSpec((channels, BLOCK), lambda j: (0, 2 * blocks + j)),
            pl.BlockSpec((5, 5, BLOCK), lambda j: (0, 0, blocks + j)),
            pl.BlockSpec((5, 5, BLOCK), lambda j: (0, 0, 2 * blocks + j)),
            pl.BlockSpec((per, head, head), lambda j: (blocks + j, 0, 0)),
            pl.BlockSpec((per, head, head), lambda j: (2 * blocks + j, 0, 0)),
        ],
        out_specs=[whole((2 * head + 16, BLOCK))] * 2,
        out_shape=[jax.ShapeDtypeStruct((2 * head + 16, BLOCK), BF16)] * 2,
        scratch_shapes=[
            pltpu.VMEM((BLOCK // LANES, flat_rows, LANES), F32),
            pltpu.VMEM((BLOCK // LANES, flat_rows, LANES), F32),
            pltpu.VMEM((cells, LANES), BF16),
            pltpu.VMEM((cells, BLOCK), BF16),
            pltpu.VMEM((cells, BLOCK), BF16),
            pltpu.VMEM((cells, BLOCK), BF16),
            pltpu.VMEM((cells, BLOCK), BF16),
        ],
        compiler_params=params,
        cost_estimate=cost(8 * cells * channels * channels, 8 * cells * channels),
        name="key_value",
    )(
        flags,
        proj_kv,
        *halos,
        keep_mask,
        early,
        w_qkv,
        w_qkv,
        w_spread,
        w_spread,
        w_group,
        w_group,
    )
    if paired:
        got = lax.ppermute(sent, "col", swap)
        mine = total_over((mine.astype(F32) + got.astype(F32)).astype(BF16), "row")
        other = lax.ppermute(mine, "col", swap)
    else:
        mine = total_over(total_over(mine, "col"), "row")
        other = total_over(total_over(sent, "col"), "row")

    count = cells + 2 * cols + 2 * tall
    far = []
    for blk in range(blocks):
        far.append(
            pl.pallas_call(
                functools.partial(query_kernel, tile),
                grid=(1,),
                in_specs=[
                    smem,
                    pl.BlockSpec((1, cells, BLOCK), lambda j, blk=blk: (blk, 0, 0)),
                    *halo_specs,
                    pl.BlockSpec((channels, BLOCK), lambda j, blk=blk: (0, blk)),
                    pl.BlockSpec((5, 5, BLOCK), lambda j, blk=blk: (0, 0, blk)),
                    pl.BlockSpec((per, head, head), lambda j, blk=blk: (blk, 0, 0)),
                ],
                out_specs=[whole((count - cells, BLOCK)), whole((count, BLOCK))],
                out_shape=[
                    jax.ShapeDtypeStruct((count - cells, BLOCK), BF16),
                    jax.ShapeDtypeStruct((count, BLOCK), BF16),
                ],
                scratch_shapes=[
                    pltpu.VMEM((BLOCK // LANES, flat_rows, LANES), F32),
                    pltpu.VMEM((count, BLOCK), BF16),
                ],
                compiler_params=params,
                cost_estimate=cost(3 * cells * channels * channels, 3 * cells * channels),
                name=f"query_{blk}",
            )(flags, proj_q, *halos, w_qkv, w_spread, w_group)
        )

    hbm = pl.BlockSpec(memory_space=pl.ANY)
    vmem = pl.BlockSpec(memory_space=pltpu.VMEM)
    buf = pltpu.VMEM((BLOCK // LANES, flat_rows_ff, LANES), F32)
    decoded = pl.pallas_call(
        functools.partial(feed_kernel, tile, head),
        in_specs=[
            smem,
            hbm,
            *[vmem] * 4,
            hbm,
            vmem,
            vmem,
            hbm,
            hbm,
            vmem,
            vmem,
            hbm,
            vmem,
            hbm,
            vmem,
            hbm,
            vmem,
        ],
        out_specs=hbm,
        out_shape=jax.ShapeDtypeStruct(main.shape, BF16),
        scratch_shapes=[
            pltpu.VMEM(main.shape, BF16),
            pltpu.VMEM(proj_q.shape, BF16),
            pltpu.VMEM((blocks, count, BLOCK), BF16),
            pltpu.VMEM(w_proj.shape, BF16),
            pltpu.VMEM(w_expand.shape, BF16),
            pltpu.VMEM(w_reduce.shape, BF16),
            pltpu.VMEM((count, channels), BF16),
            pltpu.VMEM((count, channels), BF16),
            pltpu.VMEM((count, 2 * channels), BF16),
            pltpu.VMEM((count - cells, channels), F32),
            buf,
            buf,
            buf,
            buf,
            pltpu.VMEM((cells, hidden), BF16),
            pltpu.VMEM(main.shape, BF16),
            pltpu.SemaphoreType.DMA((9,)),
        ],
        compiler_params=pltpu.CompilerParams(vmem_limit_bytes=VMEM_BYTES),
        name="feed",
    )(
        flags,
        main,
        *halos,
        proj_q,
        far[0][0],
        far[1][0],
        far[0][1],
        far[1][1],
        mine,
        other,
        w_proj,
        gain_attn.reshape(1, channels),
        w_expand,
        w_spatial,
        w_reduce,
        gain_ff.reshape(1, channels),
    )
    return decoded.reshape(rows, cols, channels)


def solution(mesh):
    tile = P(("groups", "row"), "col", None)
    return jax.shard_map(
        body,
        mesh=mesh,
        in_specs=(tile, P(("groups", "row"), "col")) + (P(),) * 9,
        out_specs=tile,
        check_vma=False,
    )
```

```python
import functools

import jax
import jax.numpy as jnp
from jax import lax
from jax.experimental import pallas as pl
from jax.experimental.pallas import tpu as pltpu
from jax.sharding import PartitionSpec as P

LANES = 128
BLOCK = 256
PAD = 8
REACH = 3
SMALL_VMEM = 24 * 1024 * 1024
FEED_VMEM = 40 * 1024 * 1024
BF16 = jnp.bfloat16
F32 = jnp.float32


def lane_chunks(width=BLOCK):
    return [slice(low, low + LANES) for low in range(0, width, LANES)]


def depthwise_rows(streams, span, out_rows, emit):
    sums = [{} for _ in streams]
    for row_in in range(out_rows + span - 1):
        for side, (load, taps) in enumerate(streams):
            views = [load(row_in, b) for b in range(span)]
            for a in range(span):
                row_out = row_in - a
                if not 0 <= row_out < out_rows:
                    continue
                part = views[0] * taps[a * span]
                for b in range(1, span):
                    part = part + views[b] * taps[a * span + b]
                sums[side][row_out] = part if a == 0 else sums[side][row_out] + part
        done = row_in - span + 1
        if done >= 0:
            emit(done, *[s.pop(done) for s in sums])


def tap_list(weight_ref, lanes, rows):
    span = weight_ref.shape[0]
    return [
        jnp.broadcast_to(weight_ref[a, b : b + 1, lanes].astype(F32), (rows, LANES)).astype(BF16)
        for a in range(span)
        for b in range(span)
    ]


def head_mask(size, head):
    return (
        lax.broadcasted_iota(jnp.int32, (size, size), 0) // head
        == lax.broadcasted_iota(jnp.int32, (size, size), 1) // head
    )


def spread_blocks(group_ref):
    count, head, _ = group_ref.shape
    size = count * head
    rows = group_ref[...].reshape(size, head)
    pick = (
        lax.broadcasted_iota(jnp.int32, (head, size), 1) % head
        == lax.broadcasted_iota(jnp.int32, (head, size), 0)
    ).astype(BF16)
    wide = jnp.dot(rows, pick, preferred_element_type=F32)
    return jnp.where(head_mask(size, head), wide, 0.0).astype(BF16)


def fill_keep(keep_ref, out):
    rows, cols = keep_ref.shape
    cell = lax.broadcasted_iota(jnp.int32, (rows * cols, rows), 0)
    own_row = cell // cols == lax.broadcasted_iota(jnp.int32, (rows * cols, rows), 1)
    lines = jnp.dot(
        own_row.astype(BF16), keep_ref[...].astype(F32).astype(BF16), preferred_element_type=F32
    )
    cell = lax.broadcasted_iota(jnp.int32, (rows * cols, cols), 0)
    own_col = cell % cols == lax.broadcasted_iota(jnp.int32, (rows * cols, cols), 1)
    picked = jnp.where(own_col, lines, 0.0).astype(BF16)
    out[...] = jnp.dot(picked, jnp.ones((cols, LANES), BF16), preferred_element_type=F32).astype(
        BF16
    )


def summarise(keys, values, head):
    kv = lax.dot_general(
        keys[...], values[...], (((0,), (0,)), ((), ())), preferred_element_type=F32
    )
    lane_head = lax.broadcasted_iota(jnp.int32, (head, BLOCK), 1) // head
    packed = jnp.zeros((head, BLOCK), F32)
    for h in range(BLOCK // head):
        packed = packed + jnp.where(lane_head == h, kv[h * head : (h + 1) * head], 0.0)
    total = jnp.sum(keys[...].astype(F32), axis=0, keepdims=True)
    return packed, jnp.broadcast_to(total, (8, BLOCK))


def put_row(buf, stride, row, col, values):
    for ch, lanes in enumerate(lane_chunks()):
        start = PAD + (row + REACH) * stride + col
        buf[ch, pl.ds(start, values.shape[0]), :] = values[:, lanes]


def fill_sides(tile, flags, sides, w, buf):
    rows, cols = tile
    stride = cols + PAD
    left_ref, right_ref = sides
    for halo_ref, col0, flag in ((left_ref, -REACH, flags[0]), (right_ref, cols, flags[1])):
        p = jnp.where(flag, jnp.dot(halo_ref[...], w, preferred_element_type=F32), 0.0)
        for k in range(REACH):
            for ch, lanes in enumerate(lane_chunks()):
                start = PAD + REACH * stride + col0 + k
                buf[ch, pl.ds(start, rows, stride=stride), :] = p[k * rows : (k + 1) * rows, lanes]


def fill_ends(tile, flags, ends, w, buf):
    rows, cols = tile
    stride = cols + PAD
    for halo_ref, row0 in zip(ends, (-REACH, rows)):
        p = jnp.dot(halo_ref[...], w, preferred_element_type=F32)
        for k in range(REACH):
            low = k * stride
            put_row(buf, stride, row0 + k, 0, p[low : low + cols])
            tail = p[low + cols : low + stride]
            put_row(buf, stride, row0 + k, -REACH, jnp.where(flags[0], tail, 0.0)[0:REACH])
            put_row(
                buf, stride, row0 + k, cols, jnp.where(flags[1], tail, 0.0)[REACH : 2 * REACH]
            )


def conv_rows(buf, s_ref, cols, row_first, row_count, out, out_row):
    stride = cols + PAD
    for ch, lanes in enumerate(lane_chunks()):
        taps = tap_list(s_ref, lanes, cols)

        def load(row_in, b, ch=ch):
            start = PAD + (row_first + row_in - 2 + REACH) * stride + b - 2
            return buf[ch, pl.ds(start, cols), :].astype(BF16)

        def emit(row, value, lanes=lanes):
            low = (out_row + row) * cols
            out[low : low + cols, lanes] = value

        depthwise_rows([(load, taps)], 5, row_count, emit)


def keep_keys(values, keep):
    values = jnp.maximum(values, 0)
    return jnp.concatenate([values[:, lanes] * keep for lanes in lane_chunks()], axis=1)


def interior_kernel(tile, head, first, *refs):
    if first:
        (flags_ref, main_ref, keep_in_ref, left_ref, right_ref, *weights, part_ref, keep_ref) = (
            refs[:13]
        )
        fill_keep(keep_in_ref, keep_ref)
        scratch = refs[13:]
    else:
        (flags_ref, main_ref, keep_ref, left_ref, right_ref, *weights, part_ref) = refs[:12]
        scratch = refs[12:]
    wk_ref, wv_ref, sk_ref, sv_ref, gk_ref, gv_ref = weights
    buf_k, buf_v, mat_k, mat_v, sp_k, sp_v, agg_k, agg_v = scratch
    rows, cols = tile
    stride = cols + PAD
    flags = (flags_ref[2] != 0, flags_ref[3] != 0)
    step = main_ref.shape[0] // 2
    for w_ref, buf, mat, is_key in ((wk_ref, buf_k, mat_k, True), (wv_ref, buf_v, mat_v, False)):
        w = w_ref[...]
        for start in range(0, 2 * step, step):
            p = jnp.dot(main_ref[start : start + step], w, preferred_element_type=F32)
            for low in range(0, step, cols):
                put_row(buf, stride, (start + low) // cols, 0, p[low : low + cols])
            p = p.astype(BF16)
            if is_key:
                p = keep_keys(p, keep_ref[start : start + step])
            mat[start : start + step] = p
        fill_sides(tile, flags, (left_ref, right_ref), w, buf)
    packed, total = summarise(mat_k, mat_v, head)
    part_ref[0:head] = packed
    part_ref[2 * head : 2 * head + 8] = total
    for s_ref, g_ref, buf, spread, out, is_key in (
        (sk_ref, gk_ref, buf_k, sp_k, agg_k, True),
        (sv_ref, gv_ref, buf_v, sp_v, agg_v, False),
    ):
        conv_rows(buf, s_ref, cols, 2, rows - 4, spread, 0)
        blocks = spread_blocks(g_ref)
        count = spread.shape[0]
        for start in range(0, count, count // 2):
            stop = start + count // 2
            agg = jnp.dot(spread[start:stop], blocks, preferred_element_type=F32).astype(BF16)
            if is_key:
                agg = keep_keys(agg, keep_ref[2 * cols + start : 2 * cols + stop])
            out[start:stop] = agg
    packed, total = summarise(agg_k, agg_v, head)
    part_ref[head : 2 * head] = packed
    part_ref[2 * head + 8 : 2 * head + 16] = total


def border_kernel(
    tile,
    head,
    flags_ref,
    main_ref,
    above_ref,
    below_ref,
    left_ref,
    right_ref,
    keep_ref,
    part_a_ref,
    part_b_ref,
    wk_ref,
    wv_ref,
    sk_ref,
    sv_ref,
    gk_ref,
    gv_ref,
    mine_ref,
    sent_ref,
    buf_k,
    buf_v,
    sp_k,
    sp_v,
    agg_k,
    agg_v,
):
    rows, cols = tile
    stride = cols + PAD
    flags = (flags_ref[2] != 0, flags_ref[3] != 0)
    for w_ref, buf in ((wk_ref, buf_k), (wv_ref, buf_v)):
        w = w_ref[...]
        for row0 in (0, rows - 4):
            p = jnp.dot(
                main_ref[row0 * cols : (row0 + 4) * cols], w, preferred_element_type=F32
            )
            for k in range(4):
                put_row(buf, stride, row0 + k, 0, p[k * cols : (k + 1) * cols])
        fill_sides(tile, flags, (left_ref, right_ref), w, buf)
        fill_ends(tile, flags, (above_ref, below_ref), w, buf)
    for s_ref, g_ref, buf, spread, out, is_key in (
        (sk_ref, gk_ref, buf_k, sp_k, agg_k, True),
        (sv_ref, gv_ref, buf_v, sp_v, agg_v, False),
    ):
        conv_rows(buf, s_ref, cols, 0, 2, spread, 0)
        conv_rows(buf, s_ref, cols, rows - 2, 2, spread, 2)
        agg = jnp.dot(spread[...], spread_blocks(g_ref), preferred_element_type=F32).astype(BF16)
        if is_key:
            keep = jnp.concatenate(
                [keep_ref[0 : 2 * cols], keep_ref[(rows - 2) * cols : rows * cols]], axis=0
            )
            agg = keep_keys(agg, keep)
        out[...] = agg
    packed, total = summarise(agg_k, agg_v, head)
    step = pl.program_id(0)
    part = jnp.where(step == 0, part_a_ref[...], part_b_ref[...])
    own = step == flags_ref[4]

    def store(out_ref):
        out_ref[0:head] = part[0:head].astype(BF16)
        out_ref[head : 2 * head] = (part[head : 2 * head] + packed).astype(BF16)
        low = 2 * head
        out_ref[low : low + 16] = jnp.concatenate(
            [part[low : low + 8], part[low + 8 : low + 16] + total], axis=0
        ).astype(BF16)

    @pl.when(own)
    def _():
        store(mine_ref)

    @pl.when(jnp.logical_not(own))
    def _():
        store(sent_ref)


def query_project_kernel(main_ref, w_ref, proj_ref):
    cells = main_ref.shape[0]
    step = 256
    w = w_ref[...]
    for start in range(0, cells, step):
        proj_ref[0, start : start + step] = jnp.dot(
            main_ref[start : start + step], w, preferred_element_type=F32
        ).astype(BF16)


def fill_projected(tile, flags, main, halos, w_ref, buf):
    rows, cols = tile
    w = w_ref[...]
    for row in range(rows):
        values = main(slice(row * cols, (row + 1) * cols)).astype(F32)
        put_row(buf, cols + PAD, row, 0, values)
    fill_ends(tile, flags, halos[:2], w, buf)
    fill_sides(tile, flags, halos[2:], w, buf)


def query_kernel(
    tile,
    flags_ref,
    proj_ref,
    above_ref,
    below_ref,
    left_ref,
    right_ref,
    w_ref,
    s_ref,
    g_ref,
    edge_ref,
    q_ref,
    buf,
    spread,
):
    rows, cols = tile
    stride = cols + PAD
    cells = rows * cols
    tall = rows + PAD
    flags = (flags_ref[2] != 0, flags_ref[3] != 0)
    halos = (above_ref, below_ref, left_ref, right_ref)
    fill_projected(tile, flags, lambda at: proj_ref[0, at], halos, w_ref, buf)
    side0 = cells + 2 * cols

    def slot(row):
        if row < 0:
            return cells
        if row >= rows:
            return cells + cols
        return row * cols

    for ch, lanes in enumerate(lane_chunks()):
        for row in (-1, rows):
            start = PAD + (row + REACH) * stride
            value = buf[ch, pl.ds(start, cols), :].astype(BF16)
            low = slot(row) - cells
            edge_ref[low : low + cols, lanes] = jnp.maximum(value, 0)
        for side, col in enumerate((-1, cols)):
            start = PAD + (REACH - 1) * stride + col
            value = buf[ch, pl.ds(start, tall, stride=stride), :].astype(BF16)
            low = 2 * cols + side * tall
            edge_ref[low : low + tall, lanes] = jnp.maximum(value, 0)

        taps = tap_list(s_ref, lanes, cols)

        def load(row_in, b, ch=ch):
            start = PAD + row_in * stride + b - 2
            return buf[ch, pl.ds(start, cols), :].astype(BF16)

        def emit(row, value, lanes=lanes):
            low = slot(row - 1)
            spread[low : low + cols, lanes] = value

        depthwise_rows([(load, taps)], 5, rows + 2, emit)
        taps = tap_list(s_ref, lanes, tall)
        for side, col in enumerate((-1, cols)):
            total = None
            for a in range(5):
                part = None
                for b in range(5):
                    start = PAD + a * stride + col + b - 2
                    view = buf[ch, pl.ds(start, tall, stride=stride), :].astype(BF16)
                    term = view * taps[a * 5 + b]
                    part = term if part is None else part + term
                total = part if total is None else total + part
            low = side0 + side * tall
            spread[low : low + tall, lanes] = total

    blocks = spread_blocks(g_ref)
    count = spread.shape[0]
    for start in range(0, count, 256):
        stop = min(count, start + 256)
        agg = jnp.dot(spread[start:stop], blocks, preferred_element_type=F32)
        q_ref[start:stop] = jnp.maximum(agg.astype(BF16), 0)


def rms_add(residual, branch, gain):
    scale = lax.rsqrt(jnp.mean(branch * branch, axis=-1, keepdims=True) + 1e-05)
    return residual.astype(F32) + branch * scale * gain


def silu(x):
    half = 0.5 * x
    return half * jnp.tanh(half) + half


def feed_kernel(
    tile,
    head,
    flags_ref,
    main_any,
    above_ref,
    below_ref,
    left_ref,
    right_ref,
    proj_any,
    q_edge_a_ref,
    q_edge_b_ref,
    q_far_a_any,
    q_far_b_any,
    mine_ref,
    other_ref,
    wp_any,
    gain_a_ref,
    we_any,
    sp_ref,
    wr_any,
    gain_f_ref,
    out_any,
    main_ref,
    proj_ref,
    q_far_ref,
    wp_ref,
    we_ref,
    wr_ref,
    mid,
    half,
    att,
    edge,
    buf_av,
    buf_ag,
    buf_bv,
    buf_bg,
    gated,
    result,
    sems,
):
    rows, cols = tile
    stride = cols + PAD
    cells = rows * cols
    tall = rows + PAD
    blocks = proj_ref.shape[0]
    channels = main_ref.shape[1]
    hidden = wr_ref.shape[0]
    steps = hidden // BLOCK
    count = mid.shape[0]
    big = cells // 2
    bounds = [(0, big), (big, cells), (cells, count)]

    loads = [
        pltpu.make_async_copy(src, dst, sems.at[i])
        for i, (src, dst) in enumerate(
            (
                (proj_any, proj_ref),
                (q_far_a_any, q_far_ref.at[0]),
                (q_far_b_any, q_far_ref.at[1]),
                (wp_any, wp_ref),
                (main_any, main_ref),
                (we_any, we_ref),
                (wr_any, wr_ref),
            )
        )
    ]
    for load in loads:
        load.start()
    q_edges = (q_edge_a_ref, q_edge_b_ref)

    edge[0:cols] = above_ref[(REACH - 1) * stride : (REACH - 1) * stride + cols].astype(F32)
    edge[cols : 2 * cols] = below_ref[0:cols].astype(F32)
    top_tail = above_ref[(REACH - 1) * stride + cols : REACH * stride].astype(F32)
    low_tail = below_ref[cols:stride].astype(F32)
    for side, (ref, near) in enumerate(((left_ref, REACH - 1), (right_ref, 0))):
        base = 2 * cols + side * tall
        pick = side * REACH + near
        edge[base : base + 1] = top_tail[pick : pick + 1]
        edge[base + 1 : base + 1 + rows] = ref[near * rows : (near + 1) * rows].astype(F32)
        edge[base + 1 + rows : base + 2 + rows] = low_tail[pick : pick + 1]
        edge[base + 2 + rows : base + tall] = jnp.zeros((tall - rows - 2, channels), F32)

    same = head_mask(BLOCK, head)
    eye = lax.broadcasted_iota(jnp.int32, (BLOCK, BLOCK), 0) == lax.broadcasted_iota(
        jnp.int32, (BLOCK, BLOCK), 1
    )
    loads[0].wait()
    for scale in range(2):
        if scale:
            loads[1].wait()
            loads[2].wait()
        for blk in range(blocks):
            mine = flags_ref[4] == blk
            low = scale * head
            packed = jnp.where(
                mine,
                mine_ref[low : low + head].astype(F32),
                other_ref[low : low + head].astype(F32),
            )
            kv = jnp.where(same, jnp.concatenate([packed] * (BLOCK // head), axis=0), 0.0)
            both = jnp.where(
                mine,
                mine_ref[2 * head : 2 * head + 16].astype(F32),
                other_ref[2 * head : 2 * head + 16].astype(F32),
            )
            sums = both[8 * scale : 8 * scale + 1]
            diag = jnp.where(eye, jnp.broadcast_to(sums, (BLOCK, BLOCK)), 0.0)
            ks = jnp.dot(
                diag.astype(BF16), same.astype(BF16), preferred_element_type=F32
            ).astype(BF16)
            kv = kv.astype(BF16)
            low = scale * channels + blk * BLOCK
            for start, stop in bounds:
                if scale:
                    q = q_far_ref[blk, start:stop]
                elif start < cells:
                    q = jnp.maximum(proj_ref[blk, start:stop], 0)
                else:
                    q = q_edges[blk][...]
                num = jnp.dot(q, kv, preferred_element_type=F32)
                den = jnp.dot(q, ks, preferred_element_type=F32)
                att[start:stop, low : low + BLOCK] = (num / (den + 1.0)).astype(BF16)

    gain = gain_a_ref[...]
    loads[3].wait()
    loads[4].wait()
    for start, stop in bounds:
        branch = jnp.dot(att[start:stop], wp_ref[...], preferred_element_type=F32)
        if start < cells:
            value = rms_add(main_ref[start:stop], branch, gain)
        else:
            value = rms_add(edge[...], branch, gain)
            index = lax.broadcasted_iota(jnp.int32, (stop - start, 1), 0)
            side = index - 2 * cols
            place = lax.rem(side + tall, tall)
            in_rows = index < 2 * cols
            is_top = (index < cols) | (~in_rows & (place == 0))
            is_bottom = (in_rows & (index >= cols)) | (~in_rows & (place == rows + 1))
            is_left = ~in_rows & (side < tall)
            is_right = ~in_rows & (side >= tall)
            dead = (
                (is_top & (flags_ref[0] == 0))
                | (is_bottom & (flags_ref[1] == 0))
                | (is_left & (flags_ref[2] == 0))
                | (is_right & (flags_ref[3] == 0))
            )
            value = jnp.where(dead, 0.0, value)
        value = value.astype(BF16)
        mid[start:stop] = value
        half[start:stop] = value * jnp.asarray(0.5, BF16)

    def expand(j, bufs):
        for part, buf in enumerate(bufs):
            w = we_ref[:, pl.ds(pl.multiple_of(part * hidden + j * BLOCK, BLOCK), BLOCK)]
            for start, stop in bounds:
                p = jnp.dot(half[start:stop], w, preferred_element_type=F32)
                p = p * jnp.tanh(p) + p
                for ch, lanes in enumerate(lane_chunks()):

                    def put(row, low):
                        at = PAD + (row + 1) * stride
                        buf[ch, pl.ds(at, cols), :] = p[low : low + cols, lanes]

                    if start < cells:
                        for low in range(0, stop - start, cols):
                            put((start + low) // cols, low)
                    else:
                        put(-1, 0)
                        put(rows, cols)
                        for side, col in enumerate((-1, cols)):
                            low = 2 * cols + side * tall
                            buf[ch, pl.ds(PAD + col, tall, stride=stride), :] = p[
                                low : low + tall, lanes
                            ]

    def mix(j, bufs):
        for ch in range(BLOCK // LANES):
            col0 = pl.multiple_of(j * BLOCK + ch * LANES, LANES)
            streams = []
            for part, buf in enumerate(bufs):

                def load(row_in, b, buf=buf, ch=ch):
                    start = PAD + row_in * stride + b - 1
                    return buf[ch, pl.ds(start, cols), :].astype(BF16)

                at = pl.multiple_of(part * hidden + j * BLOCK + ch * LANES, LANES)
                taps = tap_list(sp_ref, pl.ds(at, LANES), cols)
                if part:
                    taps = [t * jnp.asarray(0.5, BF16) for t in taps]
                streams.append((load, taps))

            def emit(row, value, gate, col0=col0):
                gated[row * cols : (row + 1) * cols, pl.ds(col0, LANES)] = value * (
                    gate * jnp.tanh(gate) + gate
                )

            depthwise_rows(streams, 3, rows, emit)

    loads[5].wait()
    bufs_a, bufs_b = (buf_av, buf_ag), (buf_bv, buf_bg)
    expand(0, bufs_a)

    def pair(i, carry):
        j = 2 * i
        expand(j + 1, bufs_b)
        mix(j, bufs_a)
        expand(jnp.minimum(j + 2, steps - 1), bufs_a)
        mix(j + 1, bufs_b)
        return carry

    lax.fori_loop(0, steps // 2, pair, 0)

    loads[6].wait()
    gain = gain_f_ref[...]
    stores = []
    for n, (start, stop) in enumerate(bounds[:2]):
        reduced = jnp.dot(gated[start:stop], wr_ref[...], preferred_element_type=F32)
        result[start:stop] = rms_add(mid[start:stop], reduced, gain).astype(BF16)
        store = pltpu.make_async_copy(
            result.at[start:stop], out_any.at[start:stop], sems.at[len(loads) + n]
        )
        store.start()
        stores.append(store)
    for store in stores:
        store.wait()


def wide(canvas, left, right, low):
    channels = canvas.shape[2]
    return jnp.concatenate(
        [
            canvas[low : low + REACH],
            left[:, low : low + REACH].transpose(1, 0, 2),
            right[:, low : low + REACH].transpose(1, 0, 2),
            jnp.zeros((REACH, PAD - 2 * REACH, channels), canvas.dtype),
        ],
        axis=1,
    )


def neighbours(axis):
    count = lax.axis_size(axis)
    forward = [(i, i + 1) for i in range(count - 1)]
    return forward, [(b, a) for a, b in forward]


def total_over(x, axis):
    count = lax.axis_size(axis)
    if count & (count - 1):
        return lax.psum(x.astype(F32), axis).astype(BF16)
    step = 1
    while step < count:
        radix = 2
        total = x.astype(F32)
        for k in range(1, radix):
            pairs = [(i, i ^ (k * step)) for i in range(count)]
            total = total + lax.ppermute(x, axis, pairs).astype(F32)
        x = total.astype(BF16)
        step *= radix
    return x


def body(
    canvas,
    keep_mask,
    w_qkv,
    w_spread,
    w_group,
    w_proj,
    gain_attn,
    w_expand,
    w_spatial,
    w_reduce,
    gain_ff,
):
    rows, cols, channels = canvas.shape
    cells = rows * cols
    head = w_group.shape[1]
    hidden = w_reduce.shape[0]
    blocks = channels // BLOCK
    per = BLOCK // head
    tall = rows + PAD
    stride = cols + PAD
    tile = (rows, cols)
    flat_rows = PAD + (tall + 4) * stride
    flat_rows_ff = PAD + tall * stride

    main = canvas.reshape(cells, channels)

    def whole(shape):
        return pl.BlockSpec(shape, lambda *_: (0,) * len(shape))

    smem = pl.BlockSpec(memory_space=pltpu.SMEM)
    params = pltpu.CompilerParams(
        dimension_semantics=("arbitrary",), vmem_limit_bytes=SMALL_VMEM
    )

    def cost(macs, moved):
        return pl.CostEstimate(flops=2 * macs, bytes_accessed=moved, transcendentals=0)

    col_index = lax.axis_index("col")
    col_count = lax.axis_size("col")
    row_index = lax.axis_index("row")
    row_count = lax.axis_size("row")
    swap = [(0, 1), (1, 0)]
    paired = col_count == 2 and blocks == 2

    def strip(low):
        return canvas[:, low : low + REACH].transpose(1, 0, 2)

    if col_count == 2:
        low = jnp.where(col_index == 0, cols - REACH, 0)
        mine = lax.dynamic_slice_in_dim(canvas, low, REACH, axis=1).transpose(1, 0, 2)
        left = right = lax.ppermute(mine, "col", swap)
    else:
        right_way, left_way = neighbours("col")
        left = lax.ppermute(strip(cols - REACH), "col", right_way)
        right = lax.ppermute(strip(0), "col", left_way)

    flags = jnp.stack(
        [
            (row_index > 0).astype(jnp.int32),
            (row_index < row_count - 1).astype(jnp.int32),
            (col_index > 0).astype(jnp.int32),
            (col_index < col_count - 1).astype(jnp.int32),
            col_index.astype(jnp.int32) if paired else jnp.int32(0),
        ]
    )

    def cell_scratch(count, copies):
        return [pltpu.VMEM((count, BLOCK), BF16)] * copies

    flat_buf = pltpu.VMEM((BLOCK // LANES, flat_rows, LANES), F32)
    part_shape = (2 * head + 16, BLOCK)

    def interior(blk, keep_in):
        first = blk == 0
        out_specs = [whole(part_shape)]
        out_shape = [jax.ShapeDtypeStruct(part_shape, F32)]
        if first:
            out_specs.append(whole((cells, LANES)))
            out_shape.append(jax.ShapeDtypeStruct((cells, LANES), BF16))
        k_at, v_at = blocks + blk, 2 * blocks + blk
        return pl.pallas_call(
            functools.partial(interior_kernel, tile, head, first),
            grid=(1,),
            in_specs=[
                smem,
                whole(main.shape),
                whole(keep_in.shape),
                whole((REACH * rows, channels)),
                whole((REACH * rows, channels)),
                pl.BlockSpec((channels, BLOCK), lambda j: (0, k_at)),
                pl.BlockSpec((channels, BLOCK), lambda j: (0, v_at)),
                pl.BlockSpec((5, 5, BLOCK), lambda j: (0, 0, k_at)),
                pl.BlockSpec((5, 5, BLOCK), lambda j: (0, 0, v_at)),
                pl.BlockSpec((per, head, head), lambda j: (k_at, 0, 0)),
                pl.BlockSpec((per, head, head), lambda j: (v_at, 0, 0)),
            ],
            out_specs=out_specs,
            out_shape=out_shape,
            scratch_shapes=[
                flat_buf,
                flat_buf,
                *cell_scratch(cells, 2),
                *cell_scratch(cells - 4 * cols, 4),
            ],
            compiler_params=params,
            cost_estimate=cost(5 * cells * channels * channels, 4 * cells * channels),
            name=f"interior_{blk}",
        )(
            flags,
            main,
            keep_in,
            left.reshape(REACH * rows, channels),
            right.reshape(REACH * rows, channels),
            w_qkv,
            w_qkv,
            w_spread,
            w_spread,
            w_group,
            w_group,
        )

    down, up = neighbours("row")
    with jax.named_scope("row_down"):
        above = lax.ppermute(wide(canvas, left, right, rows - REACH), "row", down)
    with jax.named_scope("inner_a"):
        part_a, keep = interior(0, keep_mask)
    edges, part_a = lax.optimization_barrier((wide(canvas, left, right, 0), part_a))
    with jax.named_scope("row_up"):
        below = lax.ppermute(edges, "row", up)
    with jax.named_scope("inner_b"):
        (part_b,) = interior(1, keep)
    above = above.reshape(REACH * stride, channels)
    below = below.reshape(REACH * stride, channels)
    left = left.reshape(REACH * rows, channels)
    right = right.reshape(REACH * rows, channels)
    proj_q = pl.pallas_call(
        query_project_kernel,
        grid=(blocks,),
        in_specs=[
            whole(main.shape),
            pl.BlockSpec((channels, BLOCK), lambda j: (0, j)),
        ],
        out_specs=pl.BlockSpec((1, cells, BLOCK), lambda j: (j, 0, 0)),
        out_shape=jax.ShapeDtypeStruct((blocks, cells, BLOCK), BF16),
        compiler_params=params,
        cost_estimate=cost(cells * channels * channels, 4 * cells * channels),
        name="query_project",
    )(main, w_qkv)

    halos = (above, below, left, right)
    halo_specs = [whole(h.shape) for h in halos]
    mine, sent = pl.pallas_call(
        functools.partial(border_kernel, tile, head),
        grid=(blocks,),
        in_specs=[
            smem,
            whole(main.shape),
            *halo_specs,
            whole(keep.shape),
            whole(part_shape),
            whole(part_shape),
            pl.BlockSpec((channels, BLOCK), lambda j: (0, blocks + j)),
            pl.BlockSpec((channels, BLOCK), lambda j: (0, 2 * blocks + j)),
            pl.BlockSpec((5, 5, BLOCK), lambda j: (0, 0, blocks + j)),
            pl.BlockSpec((5, 5, BLOCK), lambda j: (0, 0, 2 * blocks + j)),
            pl.BlockSpec((per, head, head), lambda j: (blocks + j, 0, 0)),
            pl.BlockSpec((per, head, head), lambda j: (2 * blocks + j, 0, 0)),
        ],
        out_specs=[whole(part_shape)] * 2,
        out_shape=[jax.ShapeDtypeStruct(part_shape, BF16)] * 2,
        scratch_shapes=[flat_buf, flat_buf, *cell_scratch(4 * cols, 4)],
        compiler_params=params,
        cost_estimate=cost(cells * channels * channels, 2 * cells * channels),
        name="border",
    )(
        flags,
        main,
        *halos,
        keep,
        part_a,
        part_b,
        w_qkv,
        w_qkv,
        w_spread,
        w_spread,
        w_group,
        w_group,
    )
    if paired:
        got = lax.ppermute(sent, "col", swap)
        mine = total_over((mine.astype(F32) + got.astype(F32)).astype(BF16), "row")
        other = lax.ppermute(mine, "col", swap)
    else:
        mine = total_over(total_over(mine, "col"), "row")
        other = total_over(total_over(sent, "col"), "row")

    count = cells + 2 * cols + 2 * tall
    far = []
    for blk in range(blocks):
        far.append(
            pl.pallas_call(
                functools.partial(query_kernel, tile),
                grid=(1,),
                in_specs=[
                    smem,
                    pl.BlockSpec((1, cells, BLOCK), lambda j, blk=blk: (blk, 0, 0)),
                    *halo_specs,
                    pl.BlockSpec((channels, BLOCK), lambda j, blk=blk: (0, blk)),
                    pl.BlockSpec((5, 5, BLOCK), lambda j, blk=blk: (0, 0, blk)),
                    pl.BlockSpec((per, head, head), lambda j, blk=blk: (blk, 0, 0)),
                ],
                out_specs=[whole((count - cells, BLOCK)), whole((count, BLOCK))],
                out_shape=[
                    jax.ShapeDtypeStruct((count - cells, BLOCK), BF16),
                    jax.ShapeDtypeStruct((count, BLOCK), BF16),
                ],
                scratch_shapes=[
                    pltpu.VMEM((BLOCK // LANES, flat_rows, LANES), F32),
                    pltpu.VMEM((count, BLOCK), BF16),
                ],
                compiler_params=params,
                cost_estimate=cost(3 * cells * channels * channels, 3 * cells * channels),
                name=f"query_{blk}",
            )(flags, proj_q, *halos, w_qkv, w_spread, w_group)
        )

    hbm = pl.BlockSpec(memory_space=pl.ANY)
    vmem = pl.BlockSpec(memory_space=pltpu.VMEM)
    buf = pltpu.VMEM((BLOCK // LANES, flat_rows_ff, LANES), F32)
    decoded = pl.pallas_call(
        functools.partial(feed_kernel, tile, head),
        in_specs=[
            smem,
            hbm,
            *[vmem] * 4,
            hbm,
            vmem,
            vmem,
            hbm,
            hbm,
            vmem,
            vmem,
            hbm,
            vmem,
            hbm,
            vmem,
            hbm,
            vmem,
        ],
        out_specs=hbm,
        out_shape=jax.ShapeDtypeStruct(main.shape, BF16),
        scratch_shapes=[
            pltpu.VMEM(main.shape, BF16),
            pltpu.VMEM(proj_q.shape, BF16),
            pltpu.VMEM((blocks, count, BLOCK), BF16),
            pltpu.VMEM(w_proj.shape, BF16),
            pltpu.VMEM(w_expand.shape, BF16),
            pltpu.VMEM(w_reduce.shape, BF16),
            pltpu.VMEM((count, channels), BF16),
            pltpu.VMEM((count, channels), BF16),
            pltpu.VMEM((count, 2 * channels), BF16),
            pltpu.VMEM((count - cells, channels), F32),
            buf,
            buf,
            buf,
            buf,
            pltpu.VMEM((cells, hidden), BF16),
            pltpu.VMEM(main.shape, BF16),
            pltpu.SemaphoreType.DMA((9,)),
        ],
        compiler_params=pltpu.CompilerParams(vmem_limit_bytes=FEED_VMEM),
        name="feed",
    )(
        flags,
        main,
        *halos,
        proj_q,
        far[0][0],
        far[1][0],
        far[0][1],
        far[1][1],
        mine,
        other,
        w_proj,
        gain_attn.reshape(1, channels),
        w_expand,
        w_spatial,
        w_reduce,
        gain_ff.reshape(1, channels),
    )
    return decoded.reshape(rows, cols, channels)


def solution(mesh):
    tile = P(("groups", "row"), "col", None)
    return jax.shard_map(
        body,
        mesh=mesh,
        in_specs=(tile, P(("groups", "row"), "col")) + (P(),) * 9,
        out_specs=tile,
        check_vma=False,
    )
```

```python
import functools

import jax
import jax.numpy as jnp
from jax import lax
from jax.experimental import pallas as pl
from jax.experimental.pallas import tpu as pltpu
from jax.sharding import PartitionSpec as P


LANES = 128
BLOCK = 256
PAD = 8
REACH = 3
PIECE = 16
END_ROWS = 128
FINE = 4
SMALL_VMEM = 24 * 1024 * 1024
FEED_VMEM = 40 * 1024 * 1024
BF16 = jnp.bfloat16
F32 = jnp.float32


def lane_chunks(width=BLOCK):
    return [slice(low, low + LANES) for low in range(0, width, LANES)]


def depthwise_rows(streams, span, out_rows, pieces, emit, between=None):
    sums = [{} for _ in streams]
    for row_in in range(out_rows + span - 1):
        for side, (load, taps) in enumerate(streams):
            for piece in range(pieces):
                views = [load(row_in, b, piece * PIECE) for b in range(span)]
                for a in range(span):
                    row_out = row_in - a
                    if not 0 <= row_out < out_rows:
                        continue
                    part = views[0] * taps[a * span]
                    for b in range(1, span):
                        part = part + views[b] * taps[a * span + b]
                    key = (row_out, piece)
                    sums[side][key] = part if a == 0 else sums[side][key] + part
        done = row_in - span + 1
        if done >= 0:
            for piece in range(pieces):
                emit(done, piece * PIECE, *[s.pop((done, piece)) for s in sums])
        if between is not None:
            between()


def aligned(value, size):
    return value if isinstance(value, int) else pl.multiple_of(value, size)


def paced(tasks, slots):
    queue = list(tasks)
    state = [0]

    def between():
        state[0] += 1
        while queue and (len(tasks) - len(queue)) * slots < state[0] * len(tasks):
            queue.pop(0)()

    def flush():
        while queue:
            queue.pop(0)()

    return between, flush


def tap_list(weight_ref, lanes, rows):
    span = weight_ref.shape[0]
    return [
        jnp.broadcast_to(weight_ref[a, b : b + 1, lanes].astype(F32), (rows, LANES)).astype(BF16)
        for a in range(span)
        for b in range(span)
    ]


def head_mask(size, head):
    return (
        lax.broadcasted_iota(jnp.int32, (size, size), 0) // head
        == lax.broadcasted_iota(jnp.int32, (size, size), 1) // head
    )


def spread_blocks(group_ref):
    count, head, _ = group_ref.shape
    size = count * head
    rows = group_ref[...].reshape(size, head)
    pick = (
        lax.broadcasted_iota(jnp.int32, (head, size), 1) % head
        == lax.broadcasted_iota(jnp.int32, (head, size), 0)
    ).astype(BF16)
    wide = jnp.dot(rows, pick, preferred_element_type=F32)
    return jnp.where(head_mask(size, head), wide, 0.0).astype(BF16)


def fill_keep(keep_ref, out):
    rows, cols = keep_ref.shape
    cell = lax.broadcasted_iota(jnp.int32, (rows * cols, rows), 0)
    own_row = cell // cols == lax.broadcasted_iota(jnp.int32, (rows * cols, rows), 1)
    lines = jnp.dot(
        own_row.astype(BF16), keep_ref[...].astype(F32).astype(BF16), preferred_element_type=F32
    )
    cell = lax.broadcasted_iota(jnp.int32, (rows * cols, cols), 0)
    own_col = cell % cols == lax.broadcasted_iota(jnp.int32, (rows * cols, cols), 1)
    picked = jnp.where(own_col, lines, 0.0).astype(BF16)
    out[...] = jnp.dot(picked, jnp.ones((cols, LANES), BF16), preferred_element_type=F32).astype(
        BF16
    )


def summarise(keys, values, head):
    kv = lax.dot_general(
        keys[...], values[...], (((0,), (0,)), ((), ())), preferred_element_type=F32
    )
    lane_head = lax.broadcasted_iota(jnp.int32, (head, BLOCK), 1) // head
    packed = jnp.zeros((head, BLOCK), F32)
    for h in range(BLOCK // head):
        packed = packed + jnp.where(lane_head == h, kv[h * head : (h + 1) * head], 0.0)
    total = jnp.sum(keys[...].astype(F32), axis=0, keepdims=True)
    return packed, jnp.broadcast_to(total, (8, BLOCK))


def put_row(buf, stride, row, col, values):
    for ch, lanes in enumerate(lane_chunks()):
        start = PAD + (row + REACH) * stride + col
        buf[ch, pl.ds(start, values.shape[0]), :] = values[:, lanes]


def stack_halos(flags_ref, even_ref, odd_ref, sides, out):
    low = 0
    for ref in sides:
        out[low : low + ref.shape[0]] = ref[...]
        low += ref.shape[0]
    count = even_ref.shape[0]

    def ends(above_ref, below_ref):
        out[low : low + count] = above_ref[...]
        out[low + END_ROWS : low + END_ROWS + count] = below_ref[...]

    @pl.when(flags_ref[5] == 0)
    def _():
        ends(odd_ref, even_ref)

    @pl.when(flags_ref[5] != 0)
    def _():
        ends(even_ref, odd_ref)

    return low + 2 * END_ROWS


def fill_sides(tile, flags, count, p, buf):
    rows, cols = tile
    stride = cols + PAD
    for side, (col0, flag) in enumerate(((-REACH, flags[0]), (cols, flags[1]))):
        base = (side % count) * REACH * rows
        q = jnp.where(flag, p[base : base + REACH * rows], 0.0)
        for k in range(REACH):
            for ch, lanes in enumerate(lane_chunks()):
                start = PAD + REACH * stride + col0 + k
                buf[ch, pl.ds(start, rows, stride=stride), :] = q[k * rows : (k + 1) * rows, lanes]


def fill_ends(tile, flags, p, buf):
    rows, cols = tile
    stride = cols + PAD
    for end, row0 in enumerate((-REACH, rows)):
        for k in range(REACH):
            low = end * END_ROWS + k * stride
            put_row(buf, stride, row0 + k, 0, p[low : low + cols])
            tail = p[low + cols : low + stride]
            put_row(buf, stride, row0 + k, -REACH, jnp.where(flags[0], tail, 0.0)[0:REACH])
            put_row(
                buf, stride, row0 + k, cols, jnp.where(flags[1], tail, 0.0)[REACH : 2 * REACH]
            )


def conv_rows(buf, s_ref, cols, row_first, row_count, out, out_row, tasks=()):
    stride = cols + PAD
    between, flush = paced(tasks, (row_count + 4) * (BLOCK // LANES))
    for ch, lanes in enumerate(lane_chunks()):
        taps = tap_list(s_ref, lanes, PIECE)

        def load(row_in, b, at, ch=ch):
            start = PAD + (row_first + row_in - 2 + REACH) * stride + b - 2 + at
            return buf[ch, pl.ds(start, PIECE), :].astype(BF16)

        def emit(row, at, value, lanes=lanes):
            low = (out_row + row) * cols + at
            out[low : low + PIECE, lanes] = value

        depthwise_rows([(load, taps)], 5, row_count, cols // PIECE, emit, between)
    flush()


def keep_keys(values, keep):
    values = jnp.maximum(values, 0)
    return jnp.concatenate([values[:, lanes] * keep for lanes in lane_chunks()], axis=1)


def interior_kernel(tile, head, first, side_count, *refs):
    flags_ref, main_ref, keep_in_ref, *refs = refs
    sides, refs = refs[:side_count], refs[side_count:]
    wk_ref, wv_ref, sk_ref, sv_ref, gk_ref, gv_ref, part_ref, *refs = refs
    keep_ref = keep_in_ref
    if first:
        keep_ref, *refs = refs
        fill_keep(keep_in_ref, keep_ref)
    buf_k, buf_v, mat_k, mat_v, sp_k, sp_v, agg_k, agg_v, stack = refs
    rows, cols = tile
    stride = cols + PAD
    flags = (flags_ref[2] != 0, flags_ref[3] != 0)
    step = main_ref.shape[0] // 2
    for n, ref in enumerate(sides):
        stack[n * REACH * rows : (n + 1) * REACH * rows] = ref[...]

    def project_task(w_ref, buf, mat, is_key, start):
        p = jnp.dot(main_ref[start : start + step], w_ref[...], preferred_element_type=F32)
        for low in range(0, step, cols):
            put_row(buf, stride, (start + low) // cols, 0, p[low : low + cols])
        p = p.astype(BF16)
        if is_key:
            p = keep_keys(p, keep_ref[start : start + step])
        mat[start : start + step] = p

    def side_task(w_ref, buf):
        p = jnp.dot(stack[...], w_ref[...], preferred_element_type=F32)
        fill_sides(tile, flags, side_count, p, buf)

    def group_task(g_ref, spread, out, is_key, start, stop):
        blocks = spread_blocks(g_ref)
        agg = jnp.dot(spread[start:stop], blocks, preferred_element_type=F32).astype(BF16)
        if is_key:
            agg = keep_keys(agg, keep_ref[2 * cols + start : 2 * cols + stop])
        out[start:stop] = agg

    def stats_task(keys, values, row, total_row):
        packed, total = summarise(keys, values, head)
        part_ref[row : row + head] = packed
        part_ref[total_row : total_row + 8] = total

    half = sp_k.shape[0] // 2
    task = functools.partial
    project_task(wk_ref, buf_k, mat_k, True, 0)
    project_task(wk_ref, buf_k, mat_k, True, step)
    side_task(wk_ref, buf_k)
    conv_rows(
        buf_k,
        sk_ref,
        cols,
        2,
        rows - 4,
        sp_k,
        0,
        [
            task(project_task, wv_ref, buf_v, mat_v, False, 0),
            task(project_task, wv_ref, buf_v, mat_v, False, step),
            task(side_task, wv_ref, buf_v),
        ],
    )
    conv_rows(
        buf_v,
        sv_ref,
        cols,
        2,
        rows - 4,
        sp_v,
        0,
        [
            task(stats_task, mat_k, mat_v, 0, 2 * head),
            task(group_task, gk_ref, sp_k, agg_k, True, 0, half),
            task(group_task, gk_ref, sp_k, agg_k, True, half, 2 * half),
        ],
    )
    group_task(gv_ref, sp_v, agg_v, False, 0, half)
    group_task(gv_ref, sp_v, agg_v, False, half, 2 * half)
    stats_task(agg_k, agg_v, head, 2 * head + 8)


def border_kernel(tile, head, side_count, flags_ref, top_ref, bottom_ref, *refs):
    even_ref, odd_ref, *refs = refs
    sides, refs = refs[:side_count], refs[side_count:]
    keep_ref, part_a_ref, part_b_ref, *refs = refs
    wk_ref, wv_ref, sk_ref, sv_ref, gk_ref, gv_ref, mine_ref, sent_ref, *refs = refs
    buf_k, buf_v, sp_k, sp_v, agg_k, agg_v, stack = refs
    rows, cols = tile
    stride = cols + PAD
    flags = (flags_ref[2] != 0, flags_ref[3] != 0)
    edge = 4 * cols

    @pl.when(pl.program_id(0) == 0)
    def _():
        stack[0:edge] = top_ref[...]
        stack[edge : 2 * edge] = bottom_ref[...]
        stack_halos(flags_ref, even_ref, odd_ref, sides, stack.at[2 * edge :])

    side_rows = side_count * REACH * rows
    for w_ref, buf in ((wk_ref, buf_k), (wv_ref, buf_v)):
        p = jnp.dot(stack[...], w_ref[...], preferred_element_type=F32)
        for end, row0 in enumerate((0, rows - 4)):
            for k in range(4):
                low = end * edge + k * cols
                put_row(buf, stride, row0 + k, 0, p[low : low + cols])
        fill_sides(tile, flags, side_count, p[2 * edge : 2 * edge + side_rows], buf)
        fill_ends(tile, flags, p[2 * edge + side_rows :], buf)
    for s_ref, g_ref, buf, spread, out, is_key in (
        (sk_ref, gk_ref, buf_k, sp_k, agg_k, True),
        (sv_ref, gv_ref, buf_v, sp_v, agg_v, False),
    ):
        conv_rows(buf, s_ref, cols, 0, 2, spread, 0)
        conv_rows(buf, s_ref, cols, rows - 2, 2, spread, 2)
        agg = jnp.dot(spread[...], spread_blocks(g_ref), preferred_element_type=F32).astype(BF16)
        if is_key:
            keep = jnp.concatenate(
                [keep_ref[0 : 2 * cols], keep_ref[(rows - 2) * cols : rows * cols]], axis=0
            )
            agg = keep_keys(agg, keep)
        out[...] = agg
    packed, total = summarise(agg_k, agg_v, head)
    step = pl.program_id(0)
    part = jnp.where(step == 0, part_a_ref[...], part_b_ref[...])
    own = step == flags_ref[4]

    def store(out_ref):
        out_ref[0:head] = part[0:head].astype(BF16)
        out_ref[head : 2 * head] = (part[head : 2 * head] + packed).astype(BF16)
        low = 2 * head
        out_ref[low : low + 16] = jnp.concatenate(
            [part[low : low + 8], part[low + 8 : low + 16] + total], axis=0
        ).astype(BF16)

    @pl.when(own)
    def _():
        store(mine_ref)

    @pl.when(jnp.logical_not(own))
    def _():
        store(sent_ref)


def query_project_kernel(main_ref, w_ref, proj_ref):
    cells = main_ref.shape[0]
    step = 256
    w = w_ref[...]
    for start in range(0, cells, step):
        proj_ref[0, start : start + step] = jnp.dot(
            main_ref[start : start + step], w, preferred_element_type=F32
        ).astype(BF16)


def query_kernel(tile, side_count, flags_ref, proj_ref, even_ref, odd_ref, *refs):
    sides, refs = refs[:side_count], refs[side_count:]
    w_ref, s_ref, g_ref, edge_ref, q_ref, buf, spread, stack = refs
    rows, cols = tile
    stride = cols + PAD
    cells = rows * cols
    tall = rows + PAD
    flags = (flags_ref[2] != 0, flags_ref[3] != 0)
    stack_halos(flags_ref, even_ref, odd_ref, sides, stack)
    for row in range(rows):
        values = proj_ref[0, row * cols : (row + 1) * cols].astype(F32)
        put_row(buf, stride, row, 0, values)
    p = jnp.dot(stack[...], w_ref[...], preferred_element_type=F32)
    side_rows = side_count * REACH * rows
    fill_sides(tile, flags, side_count, p[0:side_rows], buf)
    fill_ends(tile, flags, p[side_rows:], buf)
    side0 = cells + 2 * cols

    def slot(row):
        if row < 0:
            return cells
        if row >= rows:
            return cells + cols
        return row * cols

    for ch, lanes in enumerate(lane_chunks()):
        for row in (-1, rows):
            start = PAD + (row + REACH) * stride
            value = buf[ch, pl.ds(start, cols), :].astype(BF16)
            low = slot(row) - cells
            edge_ref[low : low + cols, lanes] = jnp.maximum(value, 0)
        for side, col in enumerate((-1, cols)):
            start = PAD + (REACH - 1) * stride + col
            value = buf[ch, pl.ds(start, tall, stride=stride), :].astype(BF16)
            low = 2 * cols + side * tall
            edge_ref[low : low + tall, lanes] = jnp.maximum(value, 0)

        taps = tap_list(s_ref, lanes, PIECE)

        def load(row_in, b, at, ch=ch):
            start = PAD + row_in * stride + b - 2 + at
            return buf[ch, pl.ds(start, PIECE), :].astype(BF16)

        def emit(row, at, value, lanes=lanes):
            low = slot(row - 1) + at
            spread[low : low + PIECE, lanes] = value

        depthwise_rows([(load, taps)], 5, rows + 2, cols // PIECE, emit)
        taps = tap_list(s_ref, lanes, tall)
        for side, col in enumerate((-1, cols)):
            total = None
            for a in range(5):
                part = None
                for b in range(5):
                    start = PAD + a * stride + col + b - 2
                    view = buf[ch, pl.ds(start, tall, stride=stride), :].astype(BF16)
                    term = view * taps[a * 5 + b]
                    part = term if part is None else part + term
                total = part if total is None else total + part
            low = side0 + side * tall
            spread[low : low + tall, lanes] = total

    blocks = spread_blocks(g_ref)
    count = spread.shape[0]
    for start in range(0, count, 256):
        stop = min(count, start + 256)
        agg = jnp.dot(spread[start:stop], blocks, preferred_element_type=F32)
        q_ref[start:stop] = jnp.maximum(agg.astype(BF16), 0)


def rms_add(residual, branch, gain):
    scale = lax.rsqrt(jnp.mean(branch * branch, axis=-1, keepdims=True) + 1e-05)
    return residual.astype(F32) + branch * scale * gain


def feed_kernel(tile, head, side_count, flags_ref, main_any, even_ref, odd_ref, *refs):
    sides, refs = refs[:side_count], refs[side_count:]
    (
        proj_any,
        q_edge_a_ref,
        q_edge_b_ref,
        q_far_a_any,
        q_far_b_any,
        mine_ref,
        other_ref,
        wp_any,
        gain_a_ref,
        we_any,
        sp_ref,
        wr_any,
        gain_f_ref,
        out_any,
        main_ref,
        proj_ref,
        q_far_ref,
        wp_ref,
        we_ref,
        wr_ref,
        mid,
        half,
        att,
        edge,
        buf_av,
        buf_ag,
        buf_bv,
        buf_bg,
        gated,
        folded,
        reduced,
        result,
        sems,
    ) = refs
    rows, cols = tile
    stride = cols + PAD
    cells = rows * cols
    tall = rows + PAD
    blocks = proj_ref.shape[0]
    channels = main_ref.shape[1]
    hidden = wr_ref.shape[0]
    steps = hidden // BLOCK
    count = mid.shape[0]
    big = cells // 2
    bounds = [(0, big), (big, cells), (cells, count)]

    loads = [
        pltpu.make_async_copy(src, dst, sems.at[i])
        for i, (src, dst) in enumerate(
            (
                (proj_any, proj_ref),
                (q_far_a_any, q_far_ref.at[0]),
                (q_far_b_any, q_far_ref.at[1]),
                (wp_any, wp_ref),
                (main_any, main_ref),
                (we_any, we_ref),
                (wr_any, wr_ref),
            )
        )
    ]
    for load in loads:
        load.start()
    q_edges = (q_edge_a_ref, q_edge_b_ref)

    def ends(above_ref, below_ref):
        edge[0:cols] = above_ref[(REACH - 1) * stride : (REACH - 1) * stride + cols].astype(F32)
        edge[cols : 2 * cols] = below_ref[0:cols].astype(F32)
        top_tail = above_ref[(REACH - 1) * stride + cols : REACH * stride].astype(F32)
        low_tail = below_ref[cols:stride].astype(F32)
        for side, near in enumerate((REACH - 1, 0)):
            base = 2 * cols + side * tall
            pick = side * REACH + near
            edge[base : base + 1] = top_tail[pick : pick + 1]
            edge[base + 1 + rows : base + 2 + rows] = low_tail[pick : pick + 1]

    @pl.when(flags_ref[5] == 0)
    def _():
        ends(odd_ref, even_ref)

    @pl.when(flags_ref[5] != 0)
    def _():
        ends(even_ref, odd_ref)

    for side, near in enumerate((REACH - 1, 0)):
        ref = sides[side % len(sides)]
        base = 2 * cols + side * tall
        edge[base + 1 : base + 1 + rows] = ref[near * rows : (near + 1) * rows].astype(F32)
        edge[base + 2 + rows : base + tall] = jnp.zeros((tall - rows - 2, channels), F32)

    same = head_mask(BLOCK, head)
    eye = lax.broadcasted_iota(jnp.int32, (BLOCK, BLOCK), 0) == lax.broadcasted_iota(
        jnp.int32, (BLOCK, BLOCK), 1
    )
    loads[3].wait()
    sums_of = {}
    for scale in range(2):
        for blk in range(blocks):
            mine = flags_ref[4] == blk
            low = scale * head
            packed = jnp.where(
                mine,
                mine_ref[low : low + head].astype(F32),
                other_ref[low : low + head].astype(F32),
            )
            kv = jnp.where(same, jnp.concatenate([packed] * (BLOCK // head), axis=0), 0.0)
            both = jnp.where(
                mine,
                mine_ref[2 * head : 2 * head + 16].astype(F32),
                other_ref[2 * head : 2 * head + 16].astype(F32),
            )
            sums = both[8 * scale : 8 * scale + 1]
            diag = jnp.where(eye, jnp.broadcast_to(sums, (BLOCK, BLOCK)), 0.0)
            sums_of[scale, blk] = jnp.dot(
                diag.astype(BF16), same.astype(BF16), preferred_element_type=F32
            ).astype(BF16)
            low = scale * channels + blk * BLOCK
            folded[low : low + BLOCK] = jnp.dot(
                kv.astype(BF16), wp_ref[low : low + BLOCK], preferred_element_type=F32
            ).astype(BF16)

    def expand_task(j, part, buf, start, stop):
        w = we_ref[:, pl.ds(aligned(part * hidden + j * BLOCK, BLOCK), BLOCK)]
        p = jnp.dot(half[start:stop], w, preferred_element_type=F32)
        p = p * jnp.tanh(p) + p
        for ch, lanes in enumerate(lane_chunks()):

            def put(row, low):
                at = PAD + (row + 1) * stride
                buf[ch, pl.ds(at, cols), :] = p[low : low + cols, lanes]

            if start < cells:
                for low in range(0, stop - start, cols):
                    put((start + low) // cols, low)
            else:
                put(-1, 0)
                put(rows, cols)
                for side, col in enumerate((-1, cols)):
                    low = 2 * cols + side * tall
                    buf[ch, pl.ds(PAD + col, tall, stride=stride), :] = p[low : low + tall, lanes]

    def reduce_task(k, start, stop):
        width = 2 * BLOCK
        part = jnp.dot(
            gated[start:stop, k * width : (k + 1) * width],
            wr_ref[k * width : (k + 1) * width],
            preferred_element_type=F32,
        )
        reduced[start:stop] = part if k == 0 else reduced[start:stop] + part

    def mix(j, bufs, tasks):
        between, flush = paced(tasks, (rows + 2) * (BLOCK // LANES))
        for ch in range(BLOCK // LANES):
            col0 = aligned(j * BLOCK + ch * LANES, LANES)
            streams = []
            for part, buf in enumerate(bufs):

                def load(row_in, b, at, buf=buf, ch=ch):
                    start = PAD + row_in * stride + b - 1 + at
                    return buf[ch, pl.ds(start, PIECE), :].astype(BF16)

                at = aligned(part * hidden + col0, LANES)
                taps = tap_list(sp_ref, pl.ds(at, LANES), PIECE)
                if part:
                    taps = [t * jnp.asarray(0.5, BF16) for t in taps]
                streams.append((load, taps))

            def emit(row, at, value, gate, col0=col0):
                low = row * cols + at
                gated[low : low + PIECE, pl.ds(col0, LANES)] = value * (
                    gate * jnp.tanh(gate) + gate
                )

            depthwise_rows(streams, 3, rows, cols // PIECE, emit, between)
        flush()

    bufs = ((buf_av, buf_ag), (buf_bv, buf_bg))
    gain = gain_a_ref[...]
    for n, (start, stop) in enumerate(bounds):
        if n == 0:
            for load in loads[:3]:
                load.wait()
        for scale in range(2):
            for blk in range(blocks):
                if scale:
                    q = q_far_ref[blk, start:stop]
                elif start < cells:
                    q = jnp.maximum(proj_ref[blk, start:stop], 0)
                else:
                    q = q_edges[blk][...]
                den = jnp.dot(q, sums_of[scale, blk], preferred_element_type=F32)
                low = scale * channels + blk * BLOCK
                att[start:stop, low : low + BLOCK] = (q.astype(F32) / (den + 1.0)).astype(BF16)
        branch = jnp.dot(att[start:stop], folded[...], preferred_element_type=F32)
        if n == 0:
            loads[4].wait()
        if start < cells:
            value = rms_add(main_ref[start:stop], branch, gain)
        else:
            value = rms_add(edge[...], branch, gain)
            index = lax.broadcasted_iota(jnp.int32, (stop - start, 1), 0)
            side = index - 2 * cols
            place = lax.rem(side + tall, tall)
            in_rows = index < 2 * cols
            is_top = (index < cols) | (~in_rows & (place == 0))
            is_bottom = (in_rows & (index >= cols)) | (~in_rows & (place == rows + 1))
            is_left = ~in_rows & (side < tall)
            is_right = ~in_rows & (side >= tall)
            dead = (
                (is_top & (flags_ref[0] == 0))
                | (is_bottom & (flags_ref[1] == 0))
                | (is_left & (flags_ref[2] == 0))
                | (is_right & (flags_ref[3] == 0))
            )
            value = jnp.where(dead, 0.0, value)
        value = value.astype(BF16)
        mid[start:stop] = value
        half[start:stop] = value * jnp.asarray(0.5, BF16)
        if n == 0:
            loads[5].wait()
        for part, buf in enumerate(bufs[0]):
            expand_task(0, part, buf, start, stop)

    loads[6].wait()
    fine = cells // FINE
    fine_bounds = [(s, s + fine) for s in range(0, cells, fine)] + [(cells, count)]

    def expansions(j, buf_pair):
        return [
            functools.partial(expand_task, j, part, buf, start, stop)
            for part, buf in enumerate(buf_pair)
            for start, stop in fine_bounds
        ]

    def pair(i, carry):
        mix(2 * i, bufs[0], expansions(2 * i + 1, bufs[1]))
        mix(2 * i + 1, bufs[1], expansions(2 * i + 2, bufs[0]))
        return carry

    last = steps // 2 - 1
    lax.fori_loop(0, last, pair, 0)
    mix(2 * last, bufs[0], expansions(2 * last + 1, bufs[1]))
    mix(
        2 * last + 1,
        bufs[1],
        [functools.partial(reduce_task, k, *at) for k in range(last) for at in bounds[:2]],
    )

    gain = gain_f_ref[...]
    stores = []
    for n, (start, stop) in enumerate(bounds[:2]):
        reduce_task(steps // 2 - 1, start, stop)
        result[start:stop] = rms_add(mid[start:stop], reduced[start:stop], gain).astype(BF16)
        store = pltpu.make_async_copy(
            result.at[start:stop], out_any.at[start:stop], sems.at[len(loads) + n]
        )
        store.start()
        stores.append(store)
    for store in stores:
        store.wait()


def wide(canvas, left, right, low):
    channels = canvas.shape[2]

    def take(x, axis):
        return lax.dynamic_slice_in_dim(x, low, REACH, axis=axis)

    return jnp.concatenate(
        [
            take(canvas, 0),
            take(left, 1).transpose(1, 0, 2),
            take(right, 1).transpose(1, 0, 2),
            jnp.zeros((REACH, PAD - 2 * REACH, channels), canvas.dtype),
        ],
        axis=1,
    )


def swaps(axis, first):
    count = lax.axis_size(axis)
    pairs = []
    for i in range(first, count - 1, 2):
        pairs += [(i, i + 1), (i + 1, i)]
    return pairs


def neighbours(axis):
    count = lax.axis_size(axis)
    forward = [(i, i + 1) for i in range(count - 1)]
    return forward, [(b, a) for a, b in forward]


def total_over(x, axis):
    count = lax.axis_size(axis)
    if count & (count - 1):
        return lax.psum(x.astype(F32), axis).astype(BF16)
    step = 1
    while step < count:
        radix = 2
        total = x.astype(F32)
        for k in range(1, radix):
            pairs = [(i, i ^ (k * step)) for i in range(count)]
            total = total + lax.ppermute(x, axis, pairs).astype(F32)
        x = total.astype(BF16)
        step *= radix
    return x


def body(
    canvas,
    keep_mask,
    w_qkv,
    w_spread,
    w_group,
    w_proj,
    gain_attn,
    w_expand,
    w_spatial,
    w_reduce,
    gain_ff,
):
    rows, cols, channels = canvas.shape
    cells = rows * cols
    head = w_group.shape[1]
    hidden = w_reduce.shape[0]
    blocks = channels // BLOCK
    per = BLOCK // head
    tall = rows + PAD
    stride = cols + PAD
    tile = (rows, cols)
    flat_rows = PAD + (tall + 4) * stride
    flat_rows_ff = PAD + tall * stride

    main = canvas.reshape(cells, channels)

    def whole(shape):
        return pl.BlockSpec(shape, lambda *_: (0,) * len(shape))

    smem = pl.BlockSpec(memory_space=pltpu.SMEM)
    params = pltpu.CompilerParams(
        dimension_semantics=("arbitrary",), vmem_limit_bytes=SMALL_VMEM
    )

    def cost(macs, moved):
        return pl.CostEstimate(flops=2 * macs, bytes_accessed=moved, transcendentals=0)

    col_index = lax.axis_index("col")
    col_count = lax.axis_size("col")
    row_index = lax.axis_index("row")
    row_count = lax.axis_size("row")
    swap = [(0, 1), (1, 0)]
    paired = col_count == 2 and blocks == 2

    def strip(low):
        return canvas[:, low : low + REACH].transpose(1, 0, 2)

    if col_count == 2:
        low = jnp.where(col_index == 0, cols - REACH, 0)
        mine = lax.dynamic_slice_in_dim(canvas, low, REACH, axis=1).transpose(1, 0, 2)
        left = right = lax.ppermute(mine, "col", swap)
    else:
        right_way, left_way = neighbours("col")
        left = lax.ppermute(strip(cols - REACH), "col", right_way)
        right = lax.ppermute(strip(0), "col", left_way)

    flags = jnp.stack(
        [
            (row_index > 0).astype(jnp.int32),
            (row_index < row_count - 1).astype(jnp.int32),
            (col_index > 0).astype(jnp.int32),
            (col_index < col_count - 1).astype(jnp.int32),
            col_index.astype(jnp.int32) if paired else jnp.int32(0),
            (row_index % 2).astype(jnp.int32),
        ]
    )

    sides = [left.reshape(REACH * rows, channels)]
    if col_count != 2:
        sides.append(right.reshape(REACH * rows, channels))
    side_count = len(sides)
    side_rows = side_count * REACH * rows

    def cell_scratch(count, copies):
        return [pltpu.VMEM((count, BLOCK), BF16)] * copies

    flat_buf = pltpu.VMEM((BLOCK // LANES, flat_rows, LANES), F32)
    part_shape = (2 * head + 16, BLOCK)

    def interior(blk, keep_in):
        first = blk == 0
        out_specs = [whole(part_shape)]
        out_shape = [jax.ShapeDtypeStruct(part_shape, F32)]
        if first:
            out_specs.append(whole((cells, LANES)))
            out_shape.append(jax.ShapeDtypeStruct((cells, LANES), BF16))
        k_at, v_at = blocks + blk, 2 * blocks + blk
        return pl.pallas_call(
            functools.partial(interior_kernel, tile, head, first, side_count),
            grid=(1,),
            in_specs=[
                smem,
                whole(main.shape),
                whole(keep_in.shape),
                *[whole(side.shape) for side in sides],
                pl.BlockSpec((channels, BLOCK), lambda j: (0, k_at)),
                pl.BlockSpec((channels, BLOCK), lambda j: (0, v_at)),
                pl.BlockSpec((5, 5, BLOCK), lambda j: (0, 0, k_at)),
                pl.BlockSpec((5, 5, BLOCK), lambda j: (0, 0, v_at)),
                pl.BlockSpec((per, head, head), lambda j: (k_at, 0, 0)),
                pl.BlockSpec((per, head, head), lambda j: (v_at, 0, 0)),
            ],
            out_specs=out_specs,
            out_shape=out_shape,
            scratch_shapes=[
                flat_buf,
                flat_buf,
                *cell_scratch(cells, 2),
                *cell_scratch(cells - 4 * cols, 4),
                pltpu.VMEM((side_rows, channels), BF16),
            ],
            compiler_params=params,
            cost_estimate=cost(5 * cells * channels * channels, 4 * cells * channels),
        )(
            flags,
            main,
            keep_in,
            *sides,
            w_qkv,
            w_qkv,
            w_spread,
            w_spread,
            w_group,
            w_group,
        )

    parity = row_index % 2
    low_even = jnp.where(parity == 0, rows - REACH, 0)
    low_odd = jnp.where(parity == 0, 0, rows - REACH)
    even = lax.ppermute(wide(canvas, left, right, low_even), "row", swaps("row", 0))
    part_a, keep = interior(0, keep_mask)
    edges, part_a = lax.optimization_barrier((wide(canvas, left, right, low_odd), part_a))
    odd = lax.ppermute(edges, "row", swaps("row", 1))
    (part_b,) = interior(1, keep)
    even = even.reshape(REACH * stride, channels)
    odd = odd.reshape(REACH * stride, channels)
    project_queries = pl.pallas_call(
        query_project_kernel,
        grid=(blocks,),
        in_specs=[
            whole(main.shape),
            pl.BlockSpec((channels, BLOCK), lambda j: (0, j)),
        ],
        out_specs=pl.BlockSpec((1, cells, BLOCK), lambda j: (j, 0, 0)),
        out_shape=jax.ShapeDtypeStruct((blocks, cells, BLOCK), BF16),
        compiler_params=params,
        cost_estimate=cost(cells * channels * channels, 4 * cells * channels),
        name="query_project",
    )
    proj_q = project_queries(main, w_qkv)

    halos = (even, odd, *sides)
    halo_specs = [whole(h.shape) for h in halos]
    mine, sent = pl.pallas_call(
        functools.partial(border_kernel, tile, head, side_count),
        grid=(blocks,),
        in_specs=[
            smem,
            pl.BlockSpec((4 * cols, channels), lambda j: (0, 0)),
            pl.BlockSpec((4 * cols, channels), lambda j: (rows // 4 - 1, 0)),
            *halo_specs,
            whole(keep.shape),
            whole(part_shape),
            whole(part_shape),
            pl.BlockSpec((channels, BLOCK), lambda j: (0, blocks + j)),
            pl.BlockSpec((channels, BLOCK), lambda j: (0, 2 * blocks + j)),
            pl.BlockSpec((5, 5, BLOCK), lambda j: (0, 0, blocks + j)),
            pl.BlockSpec((5, 5, BLOCK), lambda j: (0, 0, 2 * blocks + j)),
            pl.BlockSpec((per, head, head), lambda j: (blocks + j, 0, 0)),
            pl.BlockSpec((per, head, head), lambda j: (2 * blocks + j, 0, 0)),
        ],
        out_specs=[whole(part_shape)] * 2,
        out_shape=[jax.ShapeDtypeStruct(part_shape, BF16)] * 2,
        scratch_shapes=[
            flat_buf,
            flat_buf,
            *cell_scratch(4 * cols, 4),
            pltpu.VMEM((8 * cols + side_rows + 2 * END_ROWS, channels), BF16),
        ],
        compiler_params=params,
        cost_estimate=cost(cells * channels * channels, 2 * cells * channels),
        name="border",
    )(
        flags,
        main,
        main,
        *halos,
        keep,
        part_a,
        part_b,
        w_qkv,
        w_qkv,
        w_spread,
        w_spread,
        w_group,
        w_group,
    )
    if paired:
        got = lax.ppermute(sent, "col", swap)
        mine = total_over((mine.astype(F32) + got.astype(F32)).astype(BF16), "row")
        other = lax.ppermute(mine, "col", swap)
    else:
        mine = total_over(total_over(mine, "col"), "row")
        other = total_over(total_over(sent, "col"), "row")

    count = cells + 2 * cols + 2 * tall
    far = []
    for blk in range(blocks):
        query = pl.pallas_call(
            functools.partial(query_kernel, tile, side_count),
            grid=(1,),
            in_specs=[
                smem,
                pl.BlockSpec((1, cells, BLOCK), lambda j, blk=blk: (blk, 0, 0)),
                *halo_specs,
                pl.BlockSpec((channels, BLOCK), lambda j, blk=blk: (0, blk)),
                pl.BlockSpec((5, 5, BLOCK), lambda j, blk=blk: (0, 0, blk)),
                pl.BlockSpec((per, head, head), lambda j, blk=blk: (blk, 0, 0)),
            ],
            out_specs=[whole((count - cells, BLOCK)), whole((count, BLOCK))],
            out_shape=[
                jax.ShapeDtypeStruct((count - cells, BLOCK), BF16),
                jax.ShapeDtypeStruct((count, BLOCK), BF16),
            ],
            scratch_shapes=[
                flat_buf,
                pltpu.VMEM((count, BLOCK), BF16),
                pltpu.VMEM((side_rows + 2 * END_ROWS, channels), BF16),
            ],
            compiler_params=params,
            cost_estimate=cost(3 * cells * channels * channels, 3 * cells * channels),
        )
        far.append(query(flags, proj_q, *halos, w_qkv, w_spread, w_group))

    hbm = pl.BlockSpec(memory_space=pl.ANY)
    vmem = pl.BlockSpec(memory_space=pltpu.VMEM)
    buf = pltpu.VMEM((BLOCK // LANES, flat_rows_ff, LANES), F32)
    decoded = pl.pallas_call(
        functools.partial(feed_kernel, tile, head, side_count),
        in_specs=[
            smem,
            hbm,
            *[vmem] * len(halos),
            hbm,
            vmem,
            vmem,
            hbm,
            hbm,
            vmem,
            vmem,
            hbm,
            vmem,
            hbm,
            vmem,
            hbm,
            vmem,
        ],
        out_specs=hbm,
        out_shape=jax.ShapeDtypeStruct(main.shape, BF16),
        scratch_shapes=[
            pltpu.VMEM(main.shape, BF16),
            pltpu.VMEM(proj_q.shape, BF16),
            pltpu.VMEM((blocks, count, BLOCK), BF16),
            pltpu.VMEM(w_proj.shape, BF16),
            pltpu.VMEM(w_expand.shape, BF16),
            pltpu.VMEM(w_reduce.shape, BF16),
            pltpu.VMEM((count, channels), BF16),
            pltpu.VMEM((count, channels), BF16),
            pltpu.VMEM((count, 2 * channels), BF16),
            pltpu.VMEM((count - cells, channels), F32),
            buf,
            buf,
            buf,
            buf,
            pltpu.VMEM((cells, hidden), BF16),
            pltpu.VMEM(w_proj.shape, BF16),
            pltpu.VMEM(main.shape, F32),
            pltpu.VMEM(main.shape, BF16),
            pltpu.SemaphoreType.DMA((9,)),
        ],
        compiler_params=pltpu.CompilerParams(vmem_limit_bytes=FEED_VMEM),
        name="feed",
    )(
        flags,
        main,
        *halos,
        proj_q,
        far[0][0],
        far[1][0],
        far[0][1],
        far[1][1],
        mine,
        other,
        w_proj,
        gain_attn.reshape(1, channels),
        w_expand,
        w_spatial,
        w_reduce,
        gain_ff.reshape(1, channels),
    )
    return decoded.reshape(rows, cols, channels)


def solution(mesh):
    tile = P(("groups", "row"), "col", None)
    return jax.shard_map(
        body,
        mesh=mesh,
        in_specs=(tile, P(("groups", "row"), "col")) + (P(),) * 9,
        out_specs=tile,
        check_vma=False,
    )
```

```python
import functools

import jax
import jax.numpy as jnp
from jax import lax
from jax.experimental import pallas as pl
from jax.experimental.pallas import tpu as pltpu
from jax.sharding import PartitionSpec as P


LANES = 128
BLOCK = 256
PAD = 8
REACH = 3
PIECE = 16
END_ROWS = 128
FINE = 4
SPLIT = 8
SMALL_VMEM = 24 * 1024 * 1024
FEED_VMEM = 40 * 1024 * 1024
BF16 = jnp.bfloat16
F32 = jnp.float32


def lane_chunks(width=BLOCK):
    return [slice(low, low + LANES) for low in range(0, width, LANES)]


def depthwise_rows(streams, span, out_rows, pieces, emit, between=None):
    sums = [{} for _ in streams]
    for row_in in range(out_rows + span - 1):
        for side, (load, taps) in enumerate(streams):
            for piece in range(pieces):
                views = [load(row_in, b, piece * PIECE) for b in range(span)]
                for a in range(span):
                    row_out = row_in - a
                    if not 0 <= row_out < out_rows:
                        continue
                    part = views[0] * taps[a * span]
                    for b in range(1, span):
                        part = part + views[b] * taps[a * span + b]
                    key = (row_out, piece)
                    sums[side][key] = part if a == 0 else sums[side][key] + part
        done = row_in - span + 1
        if done >= 0:
            for piece in range(pieces):
                emit(done, piece * PIECE, *[s.pop((done, piece)) for s in sums])
        if between is not None:
            between()


def aligned(value, size):
    return value if isinstance(value, int) else pl.multiple_of(value, size)


def paced(tasks, slots):
    queue = list(tasks)
    state = [0]

    def between():
        state[0] += 1
        while queue and (len(tasks) - len(queue)) * slots < state[0] * len(tasks):
            queue.pop(0)()

    def flush():
        while queue:
            queue.pop(0)()

    return between, flush


def tap_list(weight_ref, lanes, rows):
    span = weight_ref.shape[0]
    return [
        jnp.broadcast_to(weight_ref[a, b : b + 1, lanes].astype(F32), (rows, LANES)).astype(BF16)
        for a in range(span)
        for b in range(span)
    ]


def head_mask(size, head):
    return (
        lax.broadcasted_iota(jnp.int32, (size, size), 0) // head
        == lax.broadcasted_iota(jnp.int32, (size, size), 1) // head
    )


def spread_blocks(group_ref):
    count, head, _ = group_ref.shape
    size = count * head
    rows = group_ref[...].reshape(size, head)
    pick = (
        lax.broadcasted_iota(jnp.int32, (head, size), 1) % head
        == lax.broadcasted_iota(jnp.int32, (head, size), 0)
    ).astype(BF16)
    wide = jnp.dot(rows, pick, preferred_element_type=F32)
    return jnp.where(head_mask(size, head), wide, 0.0).astype(BF16)


def fill_keep(keep_ref, out):
    rows, cols = keep_ref.shape
    cell = lax.broadcasted_iota(jnp.int32, (rows * cols, rows), 0)
    own_row = cell // cols == lax.broadcasted_iota(jnp.int32, (rows * cols, rows), 1)
    lines = jnp.dot(
        own_row.astype(BF16), keep_ref[...].astype(F32).astype(BF16), preferred_element_type=F32
    )
    cell = lax.broadcasted_iota(jnp.int32, (rows * cols, cols), 0)
    own_col = cell % cols == lax.broadcasted_iota(jnp.int32, (rows * cols, cols), 1)
    picked = jnp.where(own_col, lines, 0.0).astype(BF16)
    out[...] = jnp.dot(picked, jnp.ones((cols, LANES), BF16), preferred_element_type=F32).astype(
        BF16
    )


def summarise(keys, values, head):
    kv = lax.dot_general(
        keys[...], values[...], (((0,), (0,)), ((), ())), preferred_element_type=F32
    )
    lane_head = lax.broadcasted_iota(jnp.int32, (head, BLOCK), 1) // head
    packed = jnp.zeros((head, BLOCK), F32)
    for h in range(BLOCK // head):
        packed = packed + jnp.where(lane_head == h, kv[h * head : (h + 1) * head], 0.0)
    total = jnp.sum(keys[...].astype(F32), axis=0, keepdims=True)
    return packed, jnp.broadcast_to(total, (8, BLOCK))


def put_row(buf, stride, row, col, values):
    for ch, lanes in enumerate(lane_chunks()):
        start = PAD + (row + REACH) * stride + col
        buf[ch, pl.ds(start, values.shape[0]), :] = values[:, lanes]


def stack_halos(flags_ref, even_ref, odd_ref, sides, out):
    low = 0
    for ref in sides:
        out[low : low + ref.shape[0]] = ref[...]
        low += ref.shape[0]
    count = even_ref.shape[0]

    def ends(above_ref, below_ref):
        out[low : low + count] = above_ref[...]
        out[low + END_ROWS : low + END_ROWS + count] = below_ref[...]

    @pl.when(flags_ref[4] == 0)
    def _():
        ends(odd_ref, even_ref)

    @pl.when(flags_ref[4] != 0)
    def _():
        ends(even_ref, odd_ref)

    return low + 2 * END_ROWS


def fill_sides(tile, flags, count, p, buf):
    rows, cols = tile
    stride = cols + PAD
    for side, (col0, flag) in enumerate(((-REACH, flags[0]), (cols, flags[1]))):
        base = (side % count) * REACH * rows
        q = jnp.where(flag, p[base : base + REACH * rows], 0.0)
        for k in range(REACH):
            for ch, lanes in enumerate(lane_chunks()):
                start = PAD + REACH * stride + col0 + k
                buf[ch, pl.ds(start, rows, stride=stride), :] = q[k * rows : (k + 1) * rows, lanes]


def fill_ends(tile, flags, p, buf):
    rows, cols = tile
    stride = cols + PAD
    for end, row0 in enumerate((-REACH, rows)):
        for k in range(REACH):
            low = end * END_ROWS + k * stride
            put_row(buf, stride, row0 + k, 0, p[low : low + cols])
            tail = p[low + cols : low + stride]
            put_row(buf, stride, row0 + k, -REACH, jnp.where(flags[0], tail, 0.0)[0:REACH])
            put_row(
                buf, stride, row0 + k, cols, jnp.where(flags[1], tail, 0.0)[REACH : 2 * REACH]
            )


def conv_rows(buf, s_ref, cols, row_first, row_count, out, out_row, tasks=()):
    stride = cols + PAD
    between, flush = paced(tasks, (row_count + 4) * (BLOCK // LANES))
    for ch, lanes in enumerate(lane_chunks()):
        taps = tap_list(s_ref, lanes, PIECE)

        def load(row_in, b, at, ch=ch):
            start = PAD + (row_first + row_in - 2 + REACH) * stride + b - 2 + at
            return buf[ch, pl.ds(start, PIECE), :].astype(BF16)

        def emit(row, at, value, lanes=lanes):
            low = (out_row + row) * cols + at
            out[low : low + PIECE, lanes] = value

        depthwise_rows([(load, taps)], 5, row_count, cols // PIECE, emit, between)
    flush()


def keep_keys(values, keep):
    values = jnp.maximum(values, 0)
    return jnp.concatenate([values[:, lanes] * keep for lanes in lane_chunks()], axis=1)


def interior_kernel(tile, head, first, side_count, *refs):
    flags_ref, main_ref, keep_in_ref, *refs = refs
    sides, refs = refs[:side_count], refs[side_count:]
    wk_ref, wv_ref, sk_ref, sv_ref, gk_ref, gv_ref, part_ref, *refs = refs
    keep_ref = keep_in_ref
    if first:
        keep_ref, *refs = refs
        fill_keep(keep_in_ref, keep_ref)
    buf_k, buf_v, mat_k, mat_v, sp_k, sp_v, agg_k, agg_v, stack = refs
    rows, cols = tile
    stride = cols + PAD
    flags = (flags_ref[2] != 0, flags_ref[3] != 0)
    step = main_ref.shape[0] // SPLIT
    for n, ref in enumerate(sides):
        stack[n * REACH * rows : (n + 1) * REACH * rows] = ref[...]

    def project_task(w_ref, buf, mat, is_key, start):
        p = jnp.dot(main_ref[start : start + step], w_ref[...], preferred_element_type=F32)
        for low in range(0, step, cols):
            put_row(buf, stride, (start + low) // cols, 0, p[low : low + cols])
        p = p.astype(BF16)
        if is_key:
            p = keep_keys(p, keep_ref[start : start + step])
        mat[start : start + step] = p

    def side_task(w_ref, buf):
        p = jnp.dot(stack[...], w_ref[...], preferred_element_type=F32)
        fill_sides(tile, flags, side_count, p, buf)

    def group_task(g_ref, spread, out, is_key, start, stop):
        blocks = spread_blocks(g_ref)
        agg = jnp.dot(spread[start:stop], blocks, preferred_element_type=F32).astype(BF16)
        if is_key:
            agg = keep_keys(agg, keep_ref[2 * cols + start : 2 * cols + stop])
        out[start:stop] = agg

    def stats_task(keys, values, row, total_row):
        packed, total = summarise(keys, values, head)
        part_ref[row : row + head] = packed
        part_ref[total_row : total_row + 8] = total

    half = sp_k.shape[0] // 2
    task = functools.partial
    starts = range(0, main_ref.shape[0], step)
    for start in starts:
        project_task(wk_ref, buf_k, mat_k, True, start)
    side_task(wk_ref, buf_k)
    conv_rows(
        buf_k,
        sk_ref,
        cols,
        2,
        rows - 4,
        sp_k,
        0,
        [
            *[task(project_task, wv_ref, buf_v, mat_v, False, start) for start in starts],
            task(side_task, wv_ref, buf_v),
        ],
    )
    conv_rows(
        buf_v,
        sv_ref,
        cols,
        2,
        rows - 4,
        sp_v,
        0,
        [
            task(stats_task, mat_k, mat_v, 0, 2 * head),
            task(group_task, gk_ref, sp_k, agg_k, True, 0, half),
            task(group_task, gk_ref, sp_k, agg_k, True, half, 2 * half),
        ],
    )
    group_task(gv_ref, sp_v, agg_v, False, 0, half)
    group_task(gv_ref, sp_v, agg_v, False, half, 2 * half)
    stats_task(agg_k, agg_v, head, 2 * head + 8)


def border_kernel(tile, head, side_count, flags_ref, top_ref, bottom_ref, *refs):
    even_ref, odd_ref, *refs = refs
    sides, refs = refs[:side_count], refs[side_count:]
    keep_ref, part_a_ref, part_b_ref, *refs = refs
    wk_ref, wv_ref, sk_ref, sv_ref, gk_ref, gv_ref, out_ref, *refs = refs
    buf_k, buf_v, sp_k, sp_v, agg_k, agg_v, stack = refs
    rows, cols = tile
    stride = cols + PAD
    flags = (flags_ref[2] != 0, flags_ref[3] != 0)
    edge = 4 * cols

    @pl.when(pl.program_id(0) == 0)
    def _():
        stack[0:edge] = top_ref[...]
        stack[edge : 2 * edge] = bottom_ref[...]
        stack_halos(flags_ref, even_ref, odd_ref, sides, stack.at[2 * edge :])

    side_rows = side_count * REACH * rows
    for w_ref, buf in ((wk_ref, buf_k), (wv_ref, buf_v)):
        p = jnp.dot(stack[...], w_ref[...], preferred_element_type=F32)
        for end, row0 in enumerate((0, rows - 4)):
            for k in range(4):
                low = end * edge + k * cols
                put_row(buf, stride, row0 + k, 0, p[low : low + cols])
        fill_sides(tile, flags, side_count, p[2 * edge : 2 * edge + side_rows], buf)
        fill_ends(tile, flags, p[2 * edge + side_rows :], buf)
    for s_ref, g_ref, buf, spread, out, is_key in (
        (sk_ref, gk_ref, buf_k, sp_k, agg_k, True),
        (sv_ref, gv_ref, buf_v, sp_v, agg_v, False),
    ):
        conv_rows(buf, s_ref, cols, 0, 2, spread, 0)
        conv_rows(buf, s_ref, cols, rows - 2, 2, spread, 2)
        agg = jnp.dot(spread[...], spread_blocks(g_ref), preferred_element_type=F32).astype(BF16)
        if is_key:
            keep = jnp.concatenate(
                [keep_ref[0 : 2 * cols], keep_ref[(rows - 2) * cols : rows * cols]], axis=0
            )
            agg = keep_keys(agg, keep)
        out[...] = agg
    packed, total = summarise(agg_k, agg_v, head)
    step = pl.program_id(0)
    part = jnp.where(step == 0, part_a_ref[...], part_b_ref[...])
    out_ref[0:head] = part[0:head].astype(BF16)
    out_ref[head : 2 * head] = (part[head : 2 * head] + packed).astype(BF16)
    low = 2 * head
    out_ref[low : low + 16] = jnp.concatenate(
        [part[low : low + 8], part[low + 8 : low + 16] + total], axis=0
    ).astype(BF16)


def query_project_kernel(main_ref, w_ref, proj_ref):
    cells = main_ref.shape[0]
    step = 256
    w = w_ref[...]
    for start in range(0, cells, step):
        proj_ref[0, start : start + step] = jnp.dot(
            main_ref[start : start + step], w, preferred_element_type=F32
        ).astype(BF16)


def query_kernel(tile, side_count, flags_ref, proj_ref, even_ref, odd_ref, *refs):
    sides, refs = refs[:side_count], refs[side_count:]
    w_ref, s_ref, g_ref, edge_ref, q_ref, buf, spread, stack = refs
    rows, cols = tile
    stride = cols + PAD
    cells = rows * cols
    tall = rows + PAD
    flags = (flags_ref[2] != 0, flags_ref[3] != 0)
    stack_halos(flags_ref, even_ref, odd_ref, sides, stack)
    for row in range(rows):
        values = proj_ref[0, row * cols : (row + 1) * cols].astype(F32)
        put_row(buf, stride, row, 0, values)
    p = jnp.dot(stack[...], w_ref[...], preferred_element_type=F32)
    side_rows = side_count * REACH * rows
    fill_sides(tile, flags, side_count, p[0:side_rows], buf)
    fill_ends(tile, flags, p[side_rows:], buf)
    side0 = cells + 2 * cols

    def slot(row):
        if row < 0:
            return cells
        if row >= rows:
            return cells + cols
        return row * cols

    for ch, lanes in enumerate(lane_chunks()):
        for row in (-1, rows):
            start = PAD + (row + REACH) * stride
            value = buf[ch, pl.ds(start, cols), :].astype(BF16)
            low = slot(row) - cells
            edge_ref[low : low + cols, lanes] = jnp.maximum(value, 0)
        for side, col in enumerate((-1, cols)):
            start = PAD + (REACH - 1) * stride + col
            value = buf[ch, pl.ds(start, tall, stride=stride), :].astype(BF16)
            low = 2 * cols + side * tall
            edge_ref[low : low + tall, lanes] = jnp.maximum(value, 0)

        taps = tap_list(s_ref, lanes, PIECE)

        def load(row_in, b, at, ch=ch):
            start = PAD + row_in * stride + b - 2 + at
            return buf[ch, pl.ds(start, PIECE), :].astype(BF16)

        def emit(row, at, value, lanes=lanes):
            low = slot(row - 1) + at
            spread[low : low + PIECE, lanes] = value

        depthwise_rows([(load, taps)], 5, rows + 2, cols // PIECE, emit)
        taps = tap_list(s_ref, lanes, tall)
        for side, col in enumerate((-1, cols)):
            total = None
            for a in range(5):
                part = None
                for b in range(5):
                    start = PAD + a * stride + col + b - 2
                    view = buf[ch, pl.ds(start, tall, stride=stride), :].astype(BF16)
                    term = view * taps[a * 5 + b]
                    part = term if part is None else part + term
                total = part if total is None else total + part
            low = side0 + side * tall
            spread[low : low + tall, lanes] = total

    blocks = spread_blocks(g_ref)
    count = spread.shape[0]
    for start in range(0, count, 256):
        stop = min(count, start + 256)
        agg = jnp.dot(spread[start:stop], blocks, preferred_element_type=F32)
        q_ref[start:stop] = jnp.maximum(agg.astype(BF16), 0)


def rms_add(residual, branch, gain):
    scale = lax.rsqrt(jnp.mean(branch * branch, axis=-1, keepdims=True) + 1e-05)
    return residual.astype(F32) + branch * scale * gain


def feed_kernel(tile, head, side_count, flags_ref, main_any, even_ref, odd_ref, *refs):
    sides, refs = refs[:side_count], refs[side_count:]
    (
        proj_any,
        q_edge_a_ref,
        q_edge_b_ref,
        q_far_a_any,
        q_far_b_any,
        stats_ref,
        wp_any,
        gain_a_ref,
        we_any,
        sp_ref,
        wr_any,
        gain_f_ref,
        out_any,
        main_ref,
        proj_ref,
        q_far_ref,
        wp_ref,
        we_ref,
        wr_ref,
        mid,
        half,
        att,
        edge,
        buf_av,
        buf_ag,
        buf_bv,
        buf_bg,
        gated,
        folded,
        reduced,
        result,
        sems,
    ) = refs
    rows, cols = tile
    stride = cols + PAD
    cells = rows * cols
    tall = rows + PAD
    blocks = proj_ref.shape[0]
    channels = main_ref.shape[1]
    hidden = wr_ref.shape[0]
    steps = hidden // BLOCK
    count = mid.shape[0]
    big = cells // 2
    bounds = [(0, big), (big, cells), (cells, count)]

    loads = [
        pltpu.make_async_copy(src, dst, sems.at[i])
        for i, (src, dst) in enumerate(
            (
                (proj_any, proj_ref),
                (q_far_a_any, q_far_ref.at[0]),
                (q_far_b_any, q_far_ref.at[1]),
                (wp_any, wp_ref),
                (main_any, main_ref),
                (we_any, we_ref),
                (wr_any, wr_ref),
            )
        )
    ]
    for load in loads:
        load.start()
    q_edges = (q_edge_a_ref, q_edge_b_ref)

    def ends(above_ref, below_ref):
        edge[0:cols] = above_ref[(REACH - 1) * stride : (REACH - 1) * stride + cols].astype(F32)
        edge[cols : 2 * cols] = below_ref[0:cols].astype(F32)
        top_tail = above_ref[(REACH - 1) * stride + cols : REACH * stride].astype(F32)
        low_tail = below_ref[cols:stride].astype(F32)
        for side, near in enumerate((REACH - 1, 0)):
            base = 2 * cols + side * tall
            pick = side * REACH + near
            edge[base : base + 1] = top_tail[pick : pick + 1]
            edge[base + 1 + rows : base + 2 + rows] = low_tail[pick : pick + 1]

    @pl.when(flags_ref[4] == 0)
    def _():
        ends(odd_ref, even_ref)

    @pl.when(flags_ref[4] != 0)
    def _():
        ends(even_ref, odd_ref)

    for side, near in enumerate((REACH - 1, 0)):
        ref = sides[side % len(sides)]
        base = 2 * cols + side * tall
        edge[base + 1 : base + 1 + rows] = ref[near * rows : (near + 1) * rows].astype(F32)
        edge[base + 2 + rows : base + tall] = jnp.zeros((tall - rows - 2, channels), F32)

    same = head_mask(BLOCK, head)
    eye = lax.broadcasted_iota(jnp.int32, (BLOCK, BLOCK), 0) == lax.broadcasted_iota(
        jnp.int32, (BLOCK, BLOCK), 1
    )
    loads[3].wait()
    sums_of = {}
    for scale in range(2):
        for blk in range(blocks):
            base = blk * (2 * head + 16)
            low = base + scale * head
            packed = stats_ref[low : low + head].astype(F32)
            kv = jnp.where(same, jnp.concatenate([packed] * (BLOCK // head), axis=0), 0.0)
            low = base + 2 * head
            both = stats_ref[low : low + 16].astype(F32)
            sums = both[8 * scale : 8 * scale + 1]
            diag = jnp.where(eye, jnp.broadcast_to(sums, (BLOCK, BLOCK)), 0.0)
            sums_of[scale, blk] = jnp.dot(
                diag.astype(BF16), same.astype(BF16), preferred_element_type=F32
            ).astype(BF16)
            low = scale * channels + blk * BLOCK
            folded[low : low + BLOCK] = jnp.dot(
                kv.astype(BF16), wp_ref[low : low + BLOCK], preferred_element_type=F32
            ).astype(BF16)

    def expand_task(j, part, buf, start, stop):
        w = we_ref[:, pl.ds(aligned(part * hidden + j * BLOCK, BLOCK), BLOCK)]
        p = jnp.dot(half[start:stop], w, preferred_element_type=F32)
        p = p * jnp.tanh(p) + p
        for ch, lanes in enumerate(lane_chunks()):

            def put(row, low):
                at = PAD + (row + 1) * stride
                buf[ch, pl.ds(at, cols), :] = p[low : low + cols, lanes]

            if start < cells:
                for low in range(0, stop - start, cols):
                    put((start + low) // cols, low)
            else:
                put(-1, 0)
                put(rows, cols)
                for side, col in enumerate((-1, cols)):
                    low = 2 * cols + side * tall
                    buf[ch, pl.ds(PAD + col, tall, stride=stride), :] = p[low : low + tall, lanes]

    def reduce_task(k, start, stop):
        width = 2 * BLOCK
        part = jnp.dot(
            gated[start:stop, k * width : (k + 1) * width],
            wr_ref[k * width : (k + 1) * width],
            preferred_element_type=F32,
        )
        reduced[start:stop] = part if k == 0 else reduced[start:stop] + part

    def mix(j, bufs, tasks):
        between, flush = paced(tasks, (rows + 2) * (BLOCK // LANES))
        for ch in range(BLOCK // LANES):
            col0 = aligned(j * BLOCK + ch * LANES, LANES)
            streams = []
            for part, buf in enumerate(bufs):

                def load(row_in, b, at, buf=buf, ch=ch):
                    start = PAD + row_in * stride + b - 1 + at
                    return buf[ch, pl.ds(start, PIECE), :].astype(BF16)

                at = aligned(part * hidden + col0, LANES)
                taps = tap_list(sp_ref, pl.ds(at, LANES), PIECE)
                if part:
                    taps = [t * jnp.asarray(0.5, BF16) for t in taps]
                streams.append((load, taps))

            def emit(row, at, value, gate, col0=col0):
                low = row * cols + at
                gated[low : low + PIECE, pl.ds(col0, LANES)] = value * (
                    gate * jnp.tanh(gate) + gate
                )

            depthwise_rows(streams, 3, rows, cols // PIECE, emit, between)
        flush()

    bufs = ((buf_av, buf_ag), (buf_bv, buf_bg))
    gain = gain_a_ref[...]
    for n, (start, stop) in enumerate(bounds):
        if n == 0:
            for load in loads[:3]:
                load.wait()
        for scale in range(2):
            for blk in range(blocks):
                if scale:
                    q = q_far_ref[blk, start:stop]
                elif start < cells:
                    q = jnp.maximum(proj_ref[blk, start:stop], 0)
                else:
                    q = q_edges[blk][...]
                den = jnp.dot(q, sums_of[scale, blk], preferred_element_type=F32)
                low = scale * channels + blk * BLOCK
                att[start:stop, low : low + BLOCK] = (q.astype(F32) / (den + 1.0)).astype(BF16)
        branch = jnp.dot(att[start:stop], folded[...], preferred_element_type=F32)
        if n == 0:
            loads[4].wait()
        if start < cells:
            value = rms_add(main_ref[start:stop], branch, gain)
        else:
            value = rms_add(edge[...], branch, gain)
            index = lax.broadcasted_iota(jnp.int32, (stop - start, 1), 0)
            side = index - 2 * cols
            place = lax.rem(side + tall, tall)
            in_rows = index < 2 * cols
            is_top = (index < cols) | (~in_rows & (place == 0))
            is_bottom = (in_rows & (index >= cols)) | (~in_rows & (place == rows + 1))
            is_left = ~in_rows & (side < tall)
            is_right = ~in_rows & (side >= tall)
            dead = (
                (is_top & (flags_ref[0] == 0))
                | (is_bottom & (flags_ref[1] == 0))
                | (is_left & (flags_ref[2] == 0))
                | (is_right & (flags_ref[3] == 0))
            )
            value = jnp.where(dead, 0.0, value)
        value = value.astype(BF16)
        mid[start:stop] = value
        half[start:stop] = value * jnp.asarray(0.5, BF16)
        if n == 0:
            loads[5].wait()
        for part, buf in enumerate(bufs[0]):
            expand_task(0, part, buf, start, stop)

    loads[6].wait()
    fine = cells // FINE
    fine_bounds = [(s, s + fine) for s in range(0, cells, fine)] + [(cells, count)]

    def expansions(j, buf_pair):
        return [
            functools.partial(expand_task, j, part, buf, start, stop)
            for part, buf in enumerate(buf_pair)
            for start, stop in fine_bounds
        ]

    def pair(i, carry):
        mix(2 * i, bufs[0], expansions(2 * i + 1, bufs[1]))
        mix(2 * i + 1, bufs[1], expansions(2 * i + 2, bufs[0]))
        return carry

    last = steps // 2 - 1
    lax.fori_loop(0, last, pair, 0)
    mix(2 * last, bufs[0], expansions(2 * last + 1, bufs[1]))
    mix(
        2 * last + 1,
        bufs[1],
        [functools.partial(reduce_task, k, *at) for k in range(last) for at in bounds[:2]],
    )

    gain = gain_f_ref[...]
    stores = []
    for n, (start, stop) in enumerate(bounds[:2]):
        reduce_task(steps // 2 - 1, start, stop)
        result[start:stop] = rms_add(mid[start:stop], reduced[start:stop], gain).astype(BF16)
        store = pltpu.make_async_copy(
            result.at[start:stop], out_any.at[start:stop], sems.at[len(loads) + n]
        )
        store.start()
        stores.append(store)
    for store in stores:
        store.wait()


def wide(canvas, left, right, low):
    channels = canvas.shape[2]

    def take(x, axis):
        return lax.dynamic_slice_in_dim(x, low, REACH, axis=axis)

    return jnp.concatenate(
        [
            take(canvas, 0),
            take(left, 1).transpose(1, 0, 2),
            take(right, 1).transpose(1, 0, 2),
            jnp.zeros((REACH, PAD - 2 * REACH, channels), canvas.dtype),
        ],
        axis=1,
    )


def swaps(axis, first):
    count = lax.axis_size(axis)
    pairs = []
    for i in range(first, count - 1, 2):
        pairs += [(i, i + 1), (i + 1, i)]
    return pairs


def neighbours(axis):
    count = lax.axis_size(axis)
    forward = [(i, i + 1) for i in range(count - 1)]
    return forward, [(b, a) for a, b in forward]


def total_over(x, axis):
    count = lax.axis_size(axis)
    if count & (count - 1):
        return lax.psum(x.astype(F32), axis).astype(BF16)
    step = 1
    while step < count:
        radix = 2
        total = x.astype(F32)
        for k in range(1, radix):
            pairs = [(i, i ^ (k * step)) for i in range(count)]
            total = total + lax.ppermute(x, axis, pairs).astype(F32)
        x = total.astype(BF16)
        step *= radix
    return x


def body(
    canvas,
    keep_mask,
    w_qkv,
    w_spread,
    w_group,
    w_proj,
    gain_attn,
    w_expand,
    w_spatial,
    w_reduce,
    gain_ff,
):
    rows, cols, channels = canvas.shape
    cells = rows * cols
    head = w_group.shape[1]
    hidden = w_reduce.shape[0]
    blocks = channels // BLOCK
    per = BLOCK // head
    tall = rows + PAD
    stride = cols + PAD
    tile = (rows, cols)
    flat_rows = PAD + (tall + 4) * stride
    flat_rows_ff = PAD + tall * stride

    main = canvas.reshape(cells, channels)

    def whole(shape):
        return pl.BlockSpec(shape, lambda *_: (0,) * len(shape))

    smem = pl.BlockSpec(memory_space=pltpu.SMEM)
    params = pltpu.CompilerParams(
        dimension_semantics=("arbitrary",), vmem_limit_bytes=SMALL_VMEM
    )

    def cost(macs, moved):
        return pl.CostEstimate(flops=2 * macs, bytes_accessed=moved, transcendentals=0)

    col_index = lax.axis_index("col")
    col_count = lax.axis_size("col")
    row_index = lax.axis_index("row")
    row_count = lax.axis_size("row")
    swap = [(0, 1), (1, 0)]

    def strip(low):
        return canvas[:, low : low + REACH].transpose(1, 0, 2)

    if col_count == 2:
        low = jnp.where(col_index == 0, cols - REACH, 0)
        mine = lax.dynamic_slice_in_dim(canvas, low, REACH, axis=1).transpose(1, 0, 2)
        left = right = lax.ppermute(mine, "col", swap)
    else:
        right_way, left_way = neighbours("col")
        left = lax.ppermute(strip(cols - REACH), "col", right_way)
        right = lax.ppermute(strip(0), "col", left_way)

    flags = jnp.stack(
        [
            (row_index > 0).astype(jnp.int32),
            (row_index < row_count - 1).astype(jnp.int32),
            (col_index > 0).astype(jnp.int32),
            (col_index < col_count - 1).astype(jnp.int32),
            (row_index % 2).astype(jnp.int32),
        ]
    )

    sides = [left.reshape(REACH * rows, channels)]
    if col_count != 2:
        sides.append(right.reshape(REACH * rows, channels))
    side_count = len(sides)
    side_rows = side_count * REACH * rows

    def cell_scratch(count, copies):
        return [pltpu.VMEM((count, BLOCK), BF16)] * copies

    flat_buf = pltpu.VMEM((BLOCK // LANES, flat_rows, LANES), F32)
    part_shape = (2 * head + 16, BLOCK)

    def interior(blk, keep_in):
        first = blk == 0
        out_specs = [whole(part_shape)]
        out_shape = [jax.ShapeDtypeStruct(part_shape, F32)]
        if first:
            out_specs.append(whole((cells, LANES)))
            out_shape.append(jax.ShapeDtypeStruct((cells, LANES), BF16))
        k_at, v_at = blocks + blk, 2 * blocks + blk
        return pl.pallas_call(
            functools.partial(interior_kernel, tile, head, first, side_count),
            grid=(1,),
            in_specs=[
                smem,
                whole(main.shape),
                whole(keep_in.shape),
                *[whole(side.shape) for side in sides],
                pl.BlockSpec((channels, BLOCK), lambda j: (0, k_at)),
                pl.BlockSpec((channels, BLOCK), lambda j: (0, v_at)),
                pl.BlockSpec((5, 5, BLOCK), lambda j: (0, 0, k_at)),
                pl.BlockSpec((5, 5, BLOCK), lambda j: (0, 0, v_at)),
                pl.BlockSpec((per, head, head), lambda j: (k_at, 0, 0)),
                pl.BlockSpec((per, head, head), lambda j: (v_at, 0, 0)),
            ],
            out_specs=out_specs,
            out_shape=out_shape,
            scratch_shapes=[
                flat_buf,
                flat_buf,
                *cell_scratch(cells, 2),
                *cell_scratch(cells - 4 * cols, 4),
                pltpu.VMEM((side_rows, channels), BF16),
            ],
            compiler_params=params,
            cost_estimate=cost(5 * cells * channels * channels, 4 * cells * channels),
        )(
            flags,
            main,
            keep_in,
            *sides,
            w_qkv,
            w_qkv,
            w_spread,
            w_spread,
            w_group,
            w_group,
        )

    parity = row_index % 2
    low_even = jnp.where(parity == 0, rows - REACH, 0)
    low_odd = jnp.where(parity == 0, 0, rows - REACH)
    even = lax.ppermute(wide(canvas, left, right, low_even), "row", swaps("row", 0))
    part_a, keep = interior(0, keep_mask)
    edges, part_a = lax.optimization_barrier((wide(canvas, left, right, low_odd), part_a))
    odd = lax.ppermute(edges, "row", swaps("row", 1))
    (part_b,) = interior(1, keep)
    even = even.reshape(REACH * stride, channels)
    odd = odd.reshape(REACH * stride, channels)
    project_queries = pl.pallas_call(
        query_project_kernel,
        grid=(blocks,),
        in_specs=[
            whole(main.shape),
            pl.BlockSpec((channels, BLOCK), lambda j: (0, j)),
        ],
        out_specs=pl.BlockSpec((1, cells, BLOCK), lambda j: (j, 0, 0)),
        out_shape=jax.ShapeDtypeStruct((blocks, cells, BLOCK), BF16),
        compiler_params=params,
        cost_estimate=cost(cells * channels * channels, 4 * cells * channels),
        name="query_project",
    )
    proj_q = project_queries(main, w_qkv)

    halos = (even, odd, *sides)
    halo_specs = [whole(h.shape) for h in halos]
    stats = pl.pallas_call(
        functools.partial(border_kernel, tile, head, side_count),
        grid=(blocks,),
        in_specs=[
            smem,
            pl.BlockSpec((4 * cols, channels), lambda j: (0, 0)),
            pl.BlockSpec((4 * cols, channels), lambda j: (rows // 4 - 1, 0)),
            *halo_specs,
            whole(keep.shape),
            whole(part_shape),
            whole(part_shape),
            pl.BlockSpec((channels, BLOCK), lambda j: (0, blocks + j)),
            pl.BlockSpec((channels, BLOCK), lambda j: (0, 2 * blocks + j)),
            pl.BlockSpec((5, 5, BLOCK), lambda j: (0, 0, blocks + j)),
            pl.BlockSpec((5, 5, BLOCK), lambda j: (0, 0, 2 * blocks + j)),
            pl.BlockSpec((per, head, head), lambda j: (blocks + j, 0, 0)),
            pl.BlockSpec((per, head, head), lambda j: (2 * blocks + j, 0, 0)),
        ],
        out_specs=pl.BlockSpec(part_shape, lambda j: (j, 0)),
        out_shape=jax.ShapeDtypeStruct((blocks * part_shape[0], BLOCK), BF16),
        scratch_shapes=[
            flat_buf,
            flat_buf,
            *cell_scratch(4 * cols, 4),
            pltpu.VMEM((8 * cols + side_rows + 2 * END_ROWS, channels), BF16),
        ],
        compiler_params=params,
        cost_estimate=cost(cells * channels * channels, 2 * cells * channels),
        name="border",
    )(
        flags,
        main,
        main,
        *halos,
        keep,
        part_a,
        part_b,
        w_qkv,
        w_qkv,
        w_spread,
        w_spread,
        w_group,
        w_group,
    )
    stats = total_over(total_over(stats, "col"), "row")

    count = cells + 2 * cols + 2 * tall
    far = []
    for blk in range(blocks):
        query = pl.pallas_call(
            functools.partial(query_kernel, tile, side_count),
            grid=(1,),
            in_specs=[
                smem,
                pl.BlockSpec((1, cells, BLOCK), lambda j, blk=blk: (blk, 0, 0)),
                *halo_specs,
                pl.BlockSpec((channels, BLOCK), lambda j, blk=blk: (0, blk)),
                pl.BlockSpec((5, 5, BLOCK), lambda j, blk=blk: (0, 0, blk)),
                pl.BlockSpec((per, head, head), lambda j, blk=blk: (blk, 0, 0)),
            ],
            out_specs=[whole((count - cells, BLOCK)), whole((count, BLOCK))],
            out_shape=[
                jax.ShapeDtypeStruct((count - cells, BLOCK), BF16),
                jax.ShapeDtypeStruct((count, BLOCK), BF16),
            ],
            scratch_shapes=[
                flat_buf,
                pltpu.VMEM((count, BLOCK), BF16),
                pltpu.VMEM((side_rows + 2 * END_ROWS, channels), BF16),
            ],
            compiler_params=params,
            cost_estimate=cost(3 * cells * channels * channels, 3 * cells * channels),
        )
        far.append(query(flags, proj_q, *halos, w_qkv, w_spread, w_group))

    hbm = pl.BlockSpec(memory_space=pl.ANY)
    vmem = pl.BlockSpec(memory_space=pltpu.VMEM)
    buf = pltpu.VMEM((BLOCK // LANES, flat_rows_ff, LANES), F32)
    decoded = pl.pallas_call(
        functools.partial(feed_kernel, tile, head, side_count),
        in_specs=[
            smem,
            hbm,
            *[vmem] * len(halos),
            hbm,
            vmem,
            vmem,
            hbm,
            hbm,
            vmem,
            hbm,
            vmem,
            hbm,
            vmem,
            hbm,
            vmem,
        ],
        out_specs=hbm,
        out_shape=jax.ShapeDtypeStruct(main.shape, BF16),
        scratch_shapes=[
            pltpu.VMEM(main.shape, BF16),
            pltpu.VMEM(proj_q.shape, BF16),
            pltpu.VMEM((blocks, count, BLOCK), BF16),
            pltpu.VMEM(w_proj.shape, BF16),
            pltpu.VMEM(w_expand.shape, BF16),
            pltpu.VMEM(w_reduce.shape, BF16),
            pltpu.VMEM((count, channels), BF16),
            pltpu.VMEM((count, channels), BF16),
            pltpu.VMEM((count, 2 * channels), BF16),
            pltpu.VMEM((count - cells, channels), F32),
            buf,
            buf,
            buf,
            buf,
            pltpu.VMEM((cells, hidden), BF16),
            pltpu.VMEM(w_proj.shape, BF16),
            pltpu.VMEM(main.shape, F32),
            pltpu.VMEM(main.shape, BF16),
            pltpu.SemaphoreType.DMA((9,)),
        ],
        compiler_params=pltpu.CompilerParams(vmem_limit_bytes=FEED_VMEM),
        name="feed",
    )(
        flags,
        main,
        *halos,
        proj_q,
        far[0][0],
        far[1][0],
        far[0][1],
        far[1][1],
        stats,
        w_proj,
        gain_attn.reshape(1, channels),
        w_expand,
        w_spatial,
        w_reduce,
        gain_ff.reshape(1, channels),
    )
    return decoded.reshape(rows, cols, channels)


def solution(mesh):
    tile = P(("groups", "row"), "col", None)
    return jax.shard_map(
        body,
        mesh=mesh,
        in_specs=(tile, P(("groups", "row"), "col")) + (P(),) * 9,
        out_specs=tile,
        check_vma=False,
    )
```
